128 devices in a mesh: slab: 32 (over z, x, core), sector: 4 (over y).
Axes of the slice: x: 4, y: 4, z: 4, core: 2. Of those that a mesh axis runs over, the one named last changes fastest.
Arguments:
- fields: float32 [9, 256, 128, 256], P(None, 'slab', 'sector'), may hold values from -6 to 6
- volume: float32 [256, 128, 256], P('slab', 'sector'), may hold values from 2 to 4
- swept_axial: float32 [256, 128, 256], P('slab', 'sector'), may hold values from -0.15 to 0.15
- swept_angular: float32 [256, 128, 256], P('slab', 'sector'), may hold values from -0.15 to 0.15
- swept_radial: float32 [256, 128, 256], P('slab', 'sector'), may hold values from -0.15 to 0.15
- conductivity: float32 [256, 128, 256], P('slab', 'sector'), may hold values from 0.1 to 1
- corner_areas: bfloat16 [3, 8, 256, 128, 256], P(None, None, 'slab', 'sector'), may hold values from -6 to 6
- parcel_loads: float32 [9, 524288], P(None, ('slab', 'sector')), may hold values from -6 to 6
- dest_device: int32 [524288, 1], P(('slab', 'sector')), may hold values from 0 to 127; in each aligned block of 4096 rows (0 to 4095, 4096 to 8191, ...) at most 64 rows name the same one
- dest_cell: int32 [524288], P(('slab', 'sector')), may hold values from 0 to 65535
Outputs:
- volume_new: float32 [256, 128, 256], P('slab', 'sector')
- diffused: float32 [9, 256, 128, 256], P(None, 'slab', 'sector')
- gradients: float32 [27, 256, 128, 256], P(None, 'slab', 'sector')
The draws below stay inside these ranges and needn't reach their ends.
Inputs may be any that keep to these rules, and one draw needn't show every extreme that they name: `dest_device`: for the parcels of one device, at most 64 name the same destination device, and some destination gets exactly 64. `dest_cell`: A local cell index a 8192 + t * 256 + j in the destination device's block.
All inputs are finite; a program needn't handle non-finite values.
Results may differ from the reference program's by a relative error of at most 0.0003.
Values sent between devices are 32-bit elements; how exact they have to be, the bound alone decides.
A program may use at most 256 MiB of HBM per device.

```python
import math
import jax
import jax.numpy as jnp
import numpy as np

FIELDS = 9
CZ = 8
CT = 32
NR = 256
PAR_DEV = 4096
CAP = 64
NZ = 256
NT = 128
CELLS_DEV = 65536
PARCELS = 524288
N_SECTOR = 4
DEVICES = 128


def set_ends(drawn, rng, least, top_value):
    shape = drawn.shape
    spot = [jax.random.randint(jax.random.fold_in(rng, axis), (), 0, shape[axis]) for axis in range(len(shape))]
    drawn = drawn.at[tuple(spot)].set(least)
    longest = shape.index(max(shape))
    spot[longest] = (spot[longest] + 1) % shape[longest]
    return drawn.at[tuple(spot)].set(top_value)


def levels(stream_key, dims, pieces, smallest, top_value):
    gain, own = 1.0, jax.random.fold_in(stream_key, 6)
    for position, blocks in pieces:
        heights = jnp.exp(jax.random.uniform(jax.random.fold_in(own, position), (blocks,), jnp.float32, smallest / len(pieces), top_value / len(pieces)))
        gain = gain * jnp.repeat(heights, dims[position] // blocks).reshape([-1 if axis == position else 1 for axis in range(len(dims))])
    return gain


def shared_out(key, own, number, rows, number_of, top, most, slope):
    sequence = jax.random.permutation(key, number_of)
    crowded, usual = portions_of(number_of, rows * top, most, slope, True), portions_of(number_of, rows * top, most, slope, False)
    places = jnp.arange(number_of)

    def named(sizes, turn):
        used = int((sizes > 0).sum())
        fixed = max(1, used // 4)
        shifted = fixed + (places - fixed + turn * (used - fixed)) % max(1, number_of - fixed)
        return jnp.zeros((number_of,), jnp.int32).at[sequence[jnp.where(places < fixed, places, shifted)]].set(jnp.asarray(sizes, jnp.int32))

    sizes = jnp.where(number % 4 == 0, named(crowded, number // 4), named(usual, number - number // 4 - 1))
    mixed = jax.random.permutation(jax.random.fold_in(own, 3), number_of)
    source_of, sink = mixed[0:number_of // 2 * 2:2], mixed[1:number_of // 2 * 2:2]
    margin = jnp.minimum(sizes[source_of] - 1, most - sizes[sink]) // 2
    margin = jnp.where((source_of == sequence[0]) | (sink == sequence[0]) | (sizes[sink] == 0), 0, jnp.maximum(margin, 0))
    shifted = jax.random.randint(jax.random.fold_in(own, 4), (number_of // 2,), 0, 1 << 20) % (margin + 1)
    sizes = sizes.at[source_of].add(-shifted).at[sink].add(shifted)
    items = jnp.searchsorted(jnp.cumsum(sizes), jnp.arange(rows * top), side="right").astype(jnp.int32)
    table = items.reshape(top, rows).T
    table = table[jax.random.permutation(jax.random.fold_in(own, 1), rows)]
    turn = jax.random.randint(jax.random.fold_in(own, 2), (rows, 1), 0, top)
    return jnp.take_along_axis(table, (jnp.arange(top)[None, :] + turn) % top, axis=1)


def portions_of(number_of, total, bound, lean, full):
    loads = [(1 << 20) // math.isqrt(rank ** lean) + 1 for rank in range(1, number_of + 1)]
    largest = bound if full else min(bound, max(-(-total // number_of), total * loads[0] // sum(loads)))
    least = 1 if total - largest >= number_of - 1 else 0
    counts, rest = [largest] + [least] * (number_of - 1), total - largest - least * (number_of - 1)
    while rest > 0:
        movable = [i for i in range(1, number_of) if counts[i] < largest] or [i for i in range(1, number_of) if counts[i] < bound]
        pool, budget = sum([loads[i] for i in movable]), rest
        for i in movable:
            extra = min(bound - counts[i], max(1, budget * loads[i] // pool), rest)
            counts[i] = counts[i] + extra
            rest = rest - extra
    return np.array(counts)


def centred(rng, extent, spread, limit, pieces=(), kind=jnp.bfloat16):
    drawn = jax.random.normal(rng, extent, jnp.float32) * spread
    if len(pieces) > 0:
        drawn = levels(rng, extent, pieces, -0.22, 0.18) * drawn
    return jnp.clip(drawn, min=-limit, max=limit).astype(kind)


def setup_inputs(seed: int = 0) -> dict:
    key_of = jax.random.split(jax.random.key(seed), 11)
    fields = centred(key_of[0], (FIELDS, NZ, NT, NR), 1.0, 6.0, ((1, 32), (2, 4)), jnp.float32)
    volume = jnp.clip(2.0 + 2.0 * jax.random.uniform(key_of[1], (NZ, NT, NR), jnp.float32) ** levels(key_of[1], (NZ, NT, NR), ((0, 32), (1, 4)), -0.2, 0.2), 2.0, 4.0)
    swept_axial = jnp.clip(jax.random.uniform(key_of[2], (NZ, NT, NR), jnp.float32, -0.15, 0.15) * levels(key_of[2], (NZ, NT, NR), ((0, 32), (1, 4)), -0.4, 0.0), -0.15, 0.15)
    swept_angular = jnp.clip(jax.random.uniform(key_of[3], (NZ, NT, NR), jnp.float32, -0.15, 0.15) * levels(key_of[3], (NZ, NT, NR), ((0, 32), (1, 4)), -0.4, 0.0), -0.15, 0.15)
    swept_radial = jnp.clip(jax.random.uniform(key_of[4], (NZ, NT, NR), jnp.float32, -0.15, 0.15) * levels(key_of[4], (NZ, NT, NR), ((0, 32), (1, 4)), -0.4, 0.0), -0.15, 0.15)
    conductivity = jnp.clip(jnp.exp(math.log(1.0) - 2.3025851 * jax.random.uniform(key_of[5], (NZ, NT, NR), jnp.float32) ** levels(key_of[5], (NZ, NT, NR), ((0, 32), (1, 4)), -0.2, 0.2)), 0.1, 1.0)
    corner_areas = centred(key_of[6], (3, 8, NZ, NT, NR), 1.0, 6.0, ((2, 32), (3, 4)))
    parcel_loads = centred(key_of[7], (FIELDS, PARCELS), 1.0, 6.0, ((1, 128),), jnp.float32)
    dest_device_keys = jax.random.split(jax.random.fold_in(key_of[8], 1), PARCELS // PAR_DEV)
    dest_device_turns = jax.random.permutation(jax.random.fold_in(key_of[8], 3), PARCELS // PAR_DEV)
    dest_device = jax.vmap(lambda own, number: shared_out(jax.random.fold_in(key_of[8], 2), own, number, PAR_DEV, DEVICES, 1, CAP, 2))(dest_device_keys, dest_device_turns).reshape((PARCELS, 1))
    dest_cell = set_ends(jax.random.randint(key_of[9], (PARCELS,), 0, CELLS_DEV), jax.random.fold_in(key_of[9], 1), 0, CELLS_DEV - 1).astype(jnp.int32)
    return {"fields": fields, "volume": volume, "swept_axial": swept_axial, "swept_angular": swept_angular, "swept_radial": swept_radial, "conductivity": conductivity, "corner_areas": corner_areas, "parcel_loads": parcel_loads, "dest_device": dest_device, "dest_cell": dest_cell}


def beside_all(array):
    lead = [(0, 0)] * (array.ndim - 3)
    padded_z = jnp.pad(array, lead + [(1, 1), (0, 0), (0, 0)])
    padded_r = jnp.pad(array, lead + [(0, 0), (0, 0), (1, 1)])
    return [padded_z[..., :-2, :, :], padded_z[..., 2:, :, :], jnp.roll(array, 1, -2), jnp.roll(array, -1, -2), padded_r[..., :-2], padded_r[..., 2:]]


def reference(fields, volume, swept_axial, swept_angular, swept_radial, conductivity, corner_areas, parcel_loads, dest_device, dest_cell):
    lower_z = jnp.pad(swept_axial, ((1, 0), (0, 0), (0, 0)))[:-1]
    lower_t = jnp.roll(swept_angular, 1, 1)
    lower_r = jnp.pad(swept_radial, ((0, 0), (0, 0), (1, 0)))[..., :-1]
    volume_new = volume + swept_axial - lower_z + swept_angular - lower_t + swept_radial - lower_r
    dest_dev = dest_device[:, 0]
    slab_of = dest_dev // N_SECTOR
    sector_of = dest_dev % N_SECTOR
    axial_i = dest_cell // (CT * NR)
    angle_i = (dest_cell // NR) % CT
    radial_i = dest_cell % NR
    flat_at = (((slab_of * CZ + axial_i) * NT + sector_of * CT + angle_i) * NR + radial_i).astype(jnp.int32)
    deposit = jnp.zeros((FIELDS, NZ * NT * NR), jnp.float32).at[:, flat_at].add(parcel_loads)
    deposit = deposit.reshape(FIELDS, NZ, NT, NR)
    source_fields = fields + deposit / volume_new
    flux_sum = jnp.zeros_like(source_fields)
    for near_field, near_kappa in zip(beside_all(source_fields), beside_all(conductivity)):
        conduct = 2.0 * conductivity * near_kappa / (conductivity + near_kappa)
        flux_sum = flux_sum + conduct * (near_field - source_fields)
    diffused = source_fields + 0.1 * flux_sum / volume_new
    node_sums = jnp.zeros((3 * FIELDS + 1, NZ + 1, NT, NR), jnp.float32)
    for corner in range(8):
        step_z = corner // 4
        step_t = (corner // 2) % 2
        step_r = corner % 2
        areas = corner_areas[:, corner].astype(jnp.float32)
        terms = (areas[:, None] * fields[None]).reshape(3 * FIELDS, NZ, NT, NR)
        terms = jnp.concatenate([terms, (volume * 0.125)[None]], 0)
        if step_r == 0:
            terms = jnp.pad(terms[..., 1:], ((0, 0), (0, 0), (0, 0), (0, 1)))
        if step_t == 1:
            terms = jnp.roll(terms, 1, 2)
        terms = jnp.pad(terms, ((0, 0), (step_z, 1 - step_z), (0, 0), (0, 0)))
        node_sums = node_sums + terms
    gradients = node_sums[:-1, :NZ] / node_sums[-1:, :NZ]
    return volume_new, diffused, gradients
```

```python
import jax
import jax.numpy as jnp
from jax import lax
from jax.experimental import pallas as pl
from jax.experimental.pallas import tpu as pltpu

F32, BF16, I32 = jnp.float32, jnp.bfloat16, jnp.int32
VM = pl.BlockSpec(memory_space=pltpu.VMEM)


def nt(a, b):
    return lax.dot_general(a, b, (((1,), (1,)), ((), ())), preferred_element_type=F32)


def iota(shape, dim):
    return lax.broadcasted_iota(I32, shape, dim)


def one_hot(row, count):
    n = row.shape[1]
    return jnp.where(iota((count, n), 0) == row, 1.0, 0.0).astype(BF16)


def split(x):
    hi = x.astype(BF16)
    return hi, (x - hi.astype(F32)).astype(BF16)


def before(n):
    return jnp.where(iota((n, n), 0) < iota((n, n), 1), 1.0, 0.0).astype(BF16)


def bucket_kernel(loads_ref, dest_ref, cell_ref, out_ref, acc_ref):
    blk = 256
    devices = 128
    earlier = before(blk)
    carry = jnp.zeros((devices, 1), F32)
    acc_ref[...] = jnp.zeros_like(acc_ref)
    for b in range(4096 // blk):
        sl = pl.ds(b * blk, blk)
        d = one_hot(dest_ref[:, sl], devices)
        df = d.astype(F32)
        count = jnp.dot(d, earlier, preferred_element_type=F32)
        rank = jnp.sum(df * (count + carry), axis=0, keepdims=True).astype(I32)
        carry = carry + jnp.sum(df, axis=1, keepdims=True)
        o = one_hot(rank, 64)
        hi, lo = split(loads_ref[:, sl])
        cell = cell_ref[:, sl]
        row = (lax.shift_right_logical(cell, 8) * 256).astype(F32).astype(BF16)
        col = ((cell & 255) + 1).astype(F32).astype(BF16)
        his = [hi[c : c + 1] * o for c in range(9)] + [row * o]
        los = [lo[c : c + 1] * o for c in range(9)] + [col * o]
        rhs = jnp.concatenate([jnp.concatenate(his, 0), jnp.concatenate(los, 0)], 1)
        acc_ref[...] += nt(jnp.concatenate([d, d], 1), rhs)
    for s in range(5):
        out_ref[:, s, :] = acc_ref[:, s * 128 : (s + 1) * 128]


def bucket(loads, dest, cell):
    return pl.pallas_call(
        bucket_kernel,
        out_shape=jax.ShapeDtypeStruct((128, 5, 128), F32),
        in_specs=[VM] * 3,
        out_specs=VM,
        scratch_shapes=[pltpu.VMEM((128, 640), F32)],
        name="bucket",
    )(loads, dest.reshape(1, 4096), cell.reshape(1, 4096))


GROUPS, ROWS, SLOTS, CHUNK = 16, 16, 256, 2048


def deposit_kernel(
    recv_ref, fields_ref, vol_ref, sa_ref, st_ref, sr_ref, saz_ref, stt_ref,
    vn_ref, src_ref, zlo_ref, zhi_ref, tlo_ref, thi_ref,
    chan_ref, sort_ref, acc_ref, rank_ref,
):
    sa, st, sr = sa_ref[...], st_ref[...], sr_ref[...]
    for a in range(8):
        below = saz_ref[...] if a == 0 else sa_ref[a - 1]
        stp = st_ref[a]
        row = iota((32, 256), 0)
        side = jnp.where(row == 0, stt_ref[a : a + 1], pltpu.roll(stp, 1, 0))
        srp = sr_ref[a]
        lane = iota((32, 256), 1)
        inner = jnp.where(lane == 0, 0.0, pltpu.roll(srp, 1, 1))
        vn_ref[a] = vol_ref[a] + sa_ref[a] - below + stp - side + srp - inner
    lane = iota((64, 128), 1) < 64
    for s in range(5):
        first, second = recv_ref[0:64, s, :], recv_ref[64:128, s, :]
        chan_ref[2 * s] = jnp.where(lane, first, pltpu.roll(second, 64, 1))
        chan_ref[2 * s + 1] = jnp.where(lane, pltpu.roll(first, 64, 1), second)
    acc_ref[...] = jnp.zeros_like(acc_ref)
    earlier = before(256)

    def rows_of(c, start, count):
        part = chan_ref[c, start : start + count, :]
        return jnp.concatenate([part[i : i + 1] for i in range(count)], 1)

    for ch in range(8192 // CHUNK):
        nrow = CHUNK // 128
        carry = jnp.zeros((GROUPS, 1), F32)
        cell = rows_of(9, ch * nrow, nrow).astype(I32) - 1
        group = lax.shift_right_arithmetic(cell, 12)
        g = one_hot(group, GROUPS)
        gf = g.astype(F32)
        ranks = []
        for b in range(CHUNK // 256):
            gb = gf[:, b * 256 : (b + 1) * 256]
            count = jnp.dot(g[:, b * 256 : (b + 1) * 256], earlier, preferred_element_type=F32)
            ranks.append(jnp.sum(gb * (count + carry) , axis=0, keepdims=True))
            carry = carry + jnp.sum(gb, axis=1, keepdims=True)
        rank_ref[...] = jnp.concatenate(ranks, 1).astype(I32)
        most = jnp.max(carry).astype(I32)
        his, los = [], []
        for c in range(9):
            hi, lo = split(rows_of(c, ch * nrow, nrow))
            his.append(hi * g)
            los.append(lo * g)
        rowin = (lax.shift_right_logical(cell, 8) & 15).astype(F32).astype(BF16)
        colin = (cell & 255).astype(F32).astype(BF16)
        lhs = jnp.concatenate(his + los + [(rowin + 1.0) * g, colin * g], 0)

        def one_round(r, carry_unused):
            o = one_hot(rank_ref[...] - r * SLOTS, SLOTS)
            sort_ref[...] = nt(lhs, o)
            for gi in range(GROUPS):
                pick = lambda c: sort_ref[c * GROUPS + gi : c * GROUPS + gi + 1, :]
                rm = one_hot(pick(18).astype(I32) - 1, ROWS)
                j = one_hot(pick(19).astype(I32), 256)
                left = jnp.concatenate([pick(c).astype(BF16) * rm for c in range(18)], 0)
                out = nt(left, j)
                for f in range(9):
                    acc_ref[f, gi // 2, (gi % 2) * 16 : (gi % 2) * 16 + 16, :] += (
                        out[f * 16 : f * 16 + 16] + out[(9 + f) * 16 : (9 + f) * 16 + 16]
                    )
            return carry_unused

        lax.fori_loop(0, (most + SLOTS - 1) // SLOTS, one_round, 0)
    for a in range(8):
        inv = 1.0 / vn_ref[a]
        for f in range(9):
            v = fields_ref[f, a] + acc_ref[f, a] * inv
            src_ref[f, a] = v
            if a == 0:
                zlo_ref[f] = v
            if a == 7:
                zhi_ref[f] = v
            tlo_ref[f, a : a + 1, :] = v[0:1]
            thi_ref[f, a : a + 1, :] = v[31:32]


def deposit(recv, fields, volume, sa, st, sr, saz, stt):
    sd = jax.ShapeDtypeStruct
    return pl.pallas_call(
        deposit_kernel,
        out_shape=(
            sd((8, 32, 256), F32), sd((9, 8, 32, 256), F32),
            sd((9, 32, 256), F32), sd((9, 32, 256), F32), sd((9, 8, 256), F32), sd((9, 8, 256), F32),
        ),
        in_specs=[VM] * 8,
        out_specs=[VM] * 6,
        scratch_shapes=[
            pltpu.VMEM((10, 64, 128), F32),
            pltpu.VMEM((320, 256), F32),
            pltpu.VMEM((9, 8, 32, 256), F32),
            pltpu.VMEM((1, CHUNK), I32),
        ],
        name="deposit",
    )(recv, fields, volume, sa, st, sr, saz, stt)


def t_shift(x, edge):
    return jnp.where(iota(x.shape, 0) == 0, edge, pltpu.roll(x, 1, 0))


def r_shift(x):
    n = x.shape[1]
    return jnp.where(iota(x.shape, 1) == n - 1, 0.0, pltpu.roll(x, n - 1, 1))


def gradient_kernel(fields_ref, areas_ref, vol_ref, zh_ref, th_ref, out_ref, fv_ref, a1_ref, a0_ref, w_ref):
    a = pl.program_id(0)
    now = lax.rem(a, 2)
    prev = 1 - now

    def prepare(slot, field, area1, vol, edge):
        for f in range(9):
            x = field(f)
            xt = t_shift(x, edge(f))
            fv_ref[slot, 0, f] = r_shift(x)
            fv_ref[slot, 1, f] = x
            fv_ref[slot, 2, f] = r_shift(xt)
            fv_ref[slot, 3, f] = xt
        for i in range(3):
            for q in range(4):
                x = area1(i, q)
                if q // 2 == 1:
                    x = t_shift(x, edge(9 + 4 * i + 2 + q % 2))
                a1_ref[slot, i, q] = x if q % 2 == 1 else pltpu.roll(x, 255, 1)
        v = vol * 0.125
        v = v + t_shift(v, edge(21) * 0.125)
        w_ref[slot] = v + r_shift(v)

    @pl.when(a == 0)
    def _():
        prepare(1, lambda f: zh_ref[f], lambda i, q: zh_ref[9 + 4 * i + q], zh_ref[21],
                lambda c: th_ref[c, 8:9, :])

    here = lambda c: th_ref[c, pl.ds(a, 1), :]
    prepare(now, lambda f: fields_ref[f, 0], lambda i, q: areas_ref[i, 4 + q, 0].astype(F32), vol_ref[0], here)
    for i in range(3):
        for q in range(4):
            x = areas_ref[i, q, 0].astype(F32)
            if q // 2 == 1:
                x = t_shift(x, here(9 + 4 * i + q % 2))
            a0_ref[i, q] = x if q % 2 == 1 else pltpu.roll(x, 255, 1)
    for t in range(4):
        for h in range(2):
            at = (pl.ds(8 * t, 8), pl.ds(128 * h, 128))
            acc = [[None] * 9 for _ in range(3)]
            for dz in range(2):
                slot = prev if dz else now
                for q in range(4):
                    area = [(a1_ref[(slot, i, q) + at] if dz else a0_ref[(i, q) + at]) for i in range(3)]
                    for f in range(9):
                        x = fv_ref[(slot, q, f) + at]
                        for i in range(3):
                            term = area[i] * x
                            acc[i][f] = term if acc[i][f] is None else acc[i][f] + term
            inv = 1.0 / (w_ref[(now,) + at] + w_ref[(prev,) + at])
            for i in range(3):
                for f in range(9):
                    out_ref[(9 * i + f, 0) + at] = acc[i][f] * inv


def gradients(fields, areas, volume, zh, th):
    whole = lambda shape: pl.BlockSpec(shape, lambda a: (0,) * len(shape))
    return pl.pallas_call(
        gradient_kernel,
        grid=(8,),
        out_shape=jax.ShapeDtypeStruct((27, 8, 32, 256), F32),
        in_specs=[
            pl.BlockSpec((9, 1, 32, 256), lambda a: (0, a, 0, 0)),
            pl.BlockSpec((3, 8, 1, 32, 256), lambda a: (0, 0, a, 0, 0)),
            pl.BlockSpec((1, 32, 256), lambda a: (a, 0, 0)),
            whole((24, 32, 256)),
            whole((24, 9, 256)),
        ],
        out_specs=pl.BlockSpec((27, 1, 32, 256), lambda a: (0, a, 0, 0)),
        scratch_shapes=[
            pltpu.VMEM((2, 4, 9, 32, 256), F32),
            pltpu.VMEM((2, 3, 4, 32, 256), F32),
            pltpu.VMEM((3, 4, 32, 256), F32),
            pltpu.VMEM((2, 32, 256), F32),
        ],
        cost_estimate=pl.CostEstimate(flops=30_000_000, bytes_accessed=14_000_000, transcendentals=0),
        name="gradients",
    )(fields, areas, volume, zh, th)


def diffuse_kernel(src_ref, zlo_ref, zhi_ref, tlo_ref, thi_ref, k_ref, vn_ref, kzl_ref, kzh_ref, ktl_ref, kth_ref, out_ref, w_ref):
    row = iota((32, 256), 0)
    lane = iota((32, 256), 1)

    @pl.when(pl.program_id(0) == 0)
    def _():
        for a in range(8):
            k = k_ref[a]
            near = [
                kzl_ref[...] if a == 0 else k_ref[a - 1],
                kzh_ref[...] if a == 7 else k_ref[a + 1],
                jnp.where(row == 0, ktl_ref[a : a + 1], pltpu.roll(k, 1, 0)),
                jnp.where(row == 31, kth_ref[a : a + 1], pltpu.roll(k, 31, 0)),
                jnp.where(lane == 0, 0.0, pltpu.roll(k, 1, 1)),
                jnp.where(lane == 255, 0.0, pltpu.roll(k, 255, 1)),
            ]
            scale = (0.2 * k) / vn_ref[a]
            total = None
            for n, kn in enumerate(near):
                w = scale * kn / (k + kn)
                w_ref[n, a] = w
                total = w if total is None else total + w
            w_ref[6, a] = 1.0 - total

    for a in range(8):
        s = src_ref[0, a]
        near = [
            zlo_ref[0] if a == 0 else src_ref[0, a - 1],
            zhi_ref[0] if a == 7 else src_ref[0, a + 1],
            jnp.where(row == 0, tlo_ref[0, a : a + 1], pltpu.roll(s, 1, 0)),
            jnp.where(row == 31, thi_ref[0, a : a + 1], pltpu.roll(s, 31, 0)),
            pltpu.roll(s, 1, 1),
            pltpu.roll(s, 255, 1),
        ]
        out = w_ref[6, a] * s
        for n in range(6):
            out = out + w_ref[n, a] * near[n]
        out_ref[0, a] = out


def diffuse(src, zlo, zhi, tlo, thi, k, vn, kzl, kzh, ktl, kth):
    whole = lambda shape: pl.BlockSpec(shape, lambda f: (0,) * len(shape))
    each = lambda shape: pl.BlockSpec((1,) + shape, lambda f: (f,) + (0,) * len(shape))
    return pl.pallas_call(
        diffuse_kernel,
        grid=(9,),
        out_shape=jax.ShapeDtypeStruct((9, 8, 32, 256), F32),
        in_specs=[
            each((8, 32, 256)), each((32, 256)), each((32, 256)), each((8, 256)), each((8, 256)),
            whole((8, 32, 256)), whole((8, 32, 256)), whole((32, 256)), whole((32, 256)), whole((8, 256)), whole((8, 256)),
        ],
        out_specs=each((8, 32, 256)),
        scratch_shapes=[pltpu.VMEM((7, 8, 32, 256), F32)],
        name="diffuse",
    )(src, zlo, zhi, tlo, thi, k, vn, kzl, kzh, ktl, kth)


def exchange_kernel(src_ref, out_ref, send_sem, recv_sem, own_sem):
    slab, sector = lax.axis_index("slab"), lax.axis_index("sector")
    me = slab * 4 + sector
    own = pltpu.make_async_copy(src_ref.at[me], out_ref.at[me], own_sem)
    own.start()

    def send(k, unused):
        to = lax.rem(me + k, 128)
        pltpu.make_async_remote_copy(
            src_ref=src_ref.at[to],
            dst_ref=out_ref.at[me],
            send_sem=send_sem,
            recv_sem=recv_sem,
            device_id=(to // 4, lax.rem(to, 4)),
            device_id_type=pl.DeviceIdType.MESH,
        ).start()
        return unused

    lax.fori_loop(1, 128, send, 0)
    own.wait()
    most = pl.ds(0, 127)
    pltpu.make_async_copy(src_ref.at[most], out_ref.at[most], send_sem).wait()
    pltpu.make_async_copy(src_ref.at[most], out_ref.at[most], recv_sem).wait()


def exchange(outgoing):
    hbm = pl.BlockSpec(memory_space=pl.ANY)
    return pl.pallas_call(
        exchange_kernel,
        out_shape=jax.ShapeDtypeStruct((128, 5, 128), F32),
        in_specs=[hbm],
        out_specs=hbm,
        scratch_shapes=[pltpu.SemaphoreType.DMA, pltpu.SemaphoreType.DMA, pltpu.SemaphoreType.DMA],
        compiler_params=pltpu.CompilerParams(has_side_effects=True),
        name="exchange",
    )(outgoing)


def up(x):
    return lax.ppermute(x, "slab", [(i, i + 1) for i in range(31)])


def down(x):
    return lax.ppermute(x, "slab", [(i + 1, i) for i in range(31)])


def onward(x):
    return lax.ppermute(x, "sector", [(i, (i + 1) % 4) for i in range(4)])


def backward(x):
    return lax.ppermute(x, "sector", [((i + 1) % 4, i) for i in range(4)])


def local(fields, volume, swept_axial, swept_angular, swept_radial, conductivity, corner_areas, parcel_loads, dest_device, dest_cell):
    zh = up(jnp.concatenate(
        [fields[:, 7], corner_areas[:, 4:8, 7].astype(F32).reshape(12, 32, 256), volume[7:8], swept_axial[7:8], conductivity[7:8]], 0
    ))
    k_above = down(conductivity[0])
    k_next = backward(conductivity[:, 0])
    own = jnp.concatenate(
        [fields[:, :, 31], jnp.stack([corner_areas[:, k, :, 31] for k in (2, 3, 6, 7)], 1).astype(F32).reshape(12, 8, 256),
         volume[:, 31][None], swept_angular[:, 31][None], conductivity[:, 31][None]], 0
    )
    th = onward(jnp.concatenate([own, zh[:, 31:32]], 1))
    outgoing = bucket(parcel_loads, dest_device, dest_cell)
    recv = exchange(outgoing)
    vn, src, zlo, zhi, tlo, thi = deposit(
        recv, fields, volume, swept_axial, swept_angular, swept_radial, zh[22], th[22, :8]
    )
    below, above = up(zhi), down(zlo)
    before_, after = onward(thi), backward(tlo)
    grads = gradients(fields, corner_areas, volume, zh, th)
    diffused = diffuse(src, below, above, before_, after, conductivity, vn, zh[23], k_above, th[23, :8], k_next)
    return vn, diffused, grads


def solution(mesh):
    P = jax.sharding.PartitionSpec
    cells = P("slab", "sector", None)
    in_specs = (
        P(None, "slab", "sector", None), cells, cells, cells, cells, cells,
        P(None, None, "slab", "sector", None), P(None, ("slab", "sector")), P(("slab", "sector"), None), P(("slab", "sector")),
    )
    out_specs = (cells, P(None, "slab", "sector", None), P(None, "slab", "sector", None))
    return jax.shard_map(local, mesh=mesh, in_specs=in_specs, out_specs=out_specs, check_vma=False)
```

```python
import jax
import jax.numpy as jnp
from jax import lax
from jax.experimental import pallas as pl
from jax.experimental.pallas import tpu as pltpu

F32, BF16, I32 = jnp.float32, jnp.bfloat16, jnp.int32
VM = pl.BlockSpec(memory_space=pltpu.VMEM)


def nt(a, b):
    return lax.dot_general(a, b, (((1,), (1,)), ((), ())), preferred_element_type=F32)


def iota(shape, dim):
    return lax.broadcasted_iota(I32, shape, dim)


def one_hot(row, count):
    n = row.shape[1]
    return jnp.where(iota((count, n), 0) == row, 1.0, 0.0).astype(BF16)


def split(x):
    hi = x.astype(BF16)
    return hi, (x - hi.astype(F32)).astype(BF16)


def before(n):
    return jnp.where(iota((n, n), 0) < iota((n, n), 1), 1.0, 0.0).astype(BF16)


GROUPS, ROWS, SLOTS, CHUNK = 16, 16, 256, 2048


def deposit_kernel(
    chan_ref, fields_ref, vol_ref, sa_ref, st_ref, sr_ref, saz_ref, stt_ref,
    vn_ref, src_ref, zlo_ref, zhi_ref, tlo_ref, thi_ref,
    sort_ref, acc_ref, rank_ref,
):
    sa, st, sr = sa_ref[...], st_ref[...], sr_ref[...]
    for a in range(8):
        below = saz_ref[...] if a == 0 else sa_ref[a - 1]
        stp = st_ref[a]
        row = iota((32, 256), 0)
        side = jnp.where(row == 0, stt_ref[a : a + 1], pltpu.roll(stp, 1, 0))
        srp = sr_ref[a]
        lane = iota((32, 256), 1)
        inner = jnp.where(lane == 0, 0.0, pltpu.roll(srp, 1, 1))
        vn_ref[a] = vol_ref[a] + sa_ref[a] - below + stp - side + srp - inner
    acc_ref[...] = jnp.zeros_like(acc_ref)
    earlier = before(256)

    def rows_of(c, start, count):
        part = chan_ref[c, start : start + count, :]
        return jnp.concatenate([part[i : i + 1] for i in range(count)], 1)

    for ch in range(8192 // CHUNK):
        nrow = CHUNK // 128
        carry = jnp.zeros((GROUPS, 1), F32)
        cell = rows_of(9, ch * nrow, nrow).astype(I32) - 1
        group = lax.shift_right_arithmetic(cell, 12)
        g = one_hot(group, GROUPS)
        gf = g.astype(F32)
        ranks = []
        for b in range(CHUNK // 256):
            gb = gf[:, b * 256 : (b + 1) * 256]
            count = jnp.dot(g[:, b * 256 : (b + 1) * 256], earlier, preferred_element_type=F32)
            ranks.append(jnp.sum(gb * (count + carry) , axis=0, keepdims=True))
            carry = carry + jnp.sum(gb, axis=1, keepdims=True)
        rank_ref[...] = jnp.concatenate(ranks, 1).astype(I32)
        most = jnp.max(carry).astype(I32)
        his, los = [], []
        for c in range(9):
            hi, lo = split(rows_of(c, ch * nrow, nrow))
            his.append(hi * g)
            los.append(lo * g)
        rowin = (lax.shift_right_logical(cell, 8) & 15).astype(F32).astype(BF16)
        colin = (cell & 255).astype(F32).astype(BF16)
        lhs = jnp.concatenate(his + los + [(rowin + 1.0) * g, colin * g], 0)

        def one_round(r, carry_unused):
            o = one_hot(rank_ref[...] - r * SLOTS, SLOTS)
            sort_ref[...] = nt(lhs, o)
            for gi in range(GROUPS):
                pick = lambda c: sort_ref[c * GROUPS + gi : c * GROUPS + gi + 1, :]
                rm = one_hot(pick(18).astype(I32) - 1, ROWS)
                j = one_hot(pick(19).astype(I32), 256)
                left = jnp.concatenate([pick(c).astype(BF16) * rm for c in range(18)], 0)
                out = nt(left, j)
                for f in range(9):
                    acc_ref[f, gi // 2, (gi % 2) * 16 : (gi % 2) * 16 + 16, :] += (
                        out[f * 16 : f * 16 + 16] + out[(9 + f) * 16 : (9 + f) * 16 + 16]
                    )
            return carry_unused

        lax.fori_loop(0, (most + SLOTS - 1) // SLOTS, one_round, 0)
    for a in range(8):
        inv = 1.0 / vn_ref[a]
        for f in range(9):
            v = fields_ref[f, a] + acc_ref[f, a] * inv
            src_ref[f, a] = v
            if a == 0:
                zlo_ref[f] = v
            if a == 7:
                zhi_ref[f] = v
            tlo_ref[f, a : a + 1, :] = v[0:1]
            thi_ref[f, a : a + 1, :] = v[31:32]


def deposit(chan, fields, volume, sa, st, sr, saz, stt):
    sd = jax.ShapeDtypeStruct
    return pl.pallas_call(
        deposit_kernel,
        out_shape=(
            sd((8, 32, 256), F32), sd((9, 8, 32, 256), F32),
            sd((9, 32, 256), F32), sd((9, 32, 256), F32), sd((9, 8, 256), F32), sd((9, 8, 256), F32),
        ),
        in_specs=[VM] * 8,
        out_specs=[VM] * 6,
        scratch_shapes=[
            pltpu.VMEM((320, 256), F32),
            pltpu.VMEM((9, 8, 32, 256), F32),
            pltpu.VMEM((1, CHUNK), I32),
        ],
        name="deposit",
    )(chan, fields, volume, sa, st, sr, saz, stt)


def t_shift(x, edge):
    return jnp.where(iota(x.shape, 0) == 0, edge, pltpu.roll(x, 1, 0))


def r_shift(x):
    n = x.shape[1]
    return jnp.where(iota(x.shape, 1) == n - 1, 0.0, pltpu.roll(x, n - 1, 1))


def gradient_kernel(fields_ref, areas_ref, vol_ref, zh_ref, th_ref, out_ref, fv_ref, a1_ref, a0_ref, w_ref):
    a = pl.program_id(0)
    now = lax.rem(a, 2)
    prev = 1 - now

    def prepare(slot, field, area1, vol, edge):
        for f in range(9):
            x = field(f)
            xt = t_shift(x, edge(f))
            fv_ref[slot, 0, f] = r_shift(x)
            fv_ref[slot, 1, f] = x
            fv_ref[slot, 2, f] = r_shift(xt)
            fv_ref[slot, 3, f] = xt
        for i in range(3):
            for q in range(4):
                x = area1(i, q)
                if q // 2 == 1:
                    x = t_shift(x, edge(9 + 4 * i + 2 + q % 2))
                a1_ref[slot, i, q] = x if q % 2 == 1 else pltpu.roll(x, 255, 1)
        v = vol * 0.125
        v = v + t_shift(v, edge(21) * 0.125)
        w_ref[slot] = v + r_shift(v)

    @pl.when(a == 0)
    def _():
        prepare(1, lambda f: zh_ref[f], lambda i, q: zh_ref[9 + 4 * i + q], zh_ref[21],
                lambda c: th_ref[c, 8:9, :])

    here = lambda c: th_ref[c, pl.ds(a, 1), :]
    prepare(now, lambda f: fields_ref[f, 0], lambda i, q: areas_ref[i, 4 + q, 0].astype(F32), vol_ref[0], here)
    for i in range(3):
        for q in range(4):
            x = areas_ref[i, q, 0].astype(F32)
            if q // 2 == 1:
                x = t_shift(x, here(9 + 4 * i + q % 2))
            a0_ref[i, q] = x if q % 2 == 1 else pltpu.roll(x, 255, 1)
    for t in range(4):
        for h in range(2):
            at = (pl.ds(8 * t, 8), pl.ds(128 * h, 128))
            acc = [[None] * 9 for _ in range(3)]
            for dz in range(2):
                slot = prev if dz else now
                for q in range(4):
                    area = [(a1_ref[(slot, i, q) + at] if dz else a0_ref[(i, q) + at]) for i in range(3)]
                    for f in range(9):
                        x = fv_ref[(slot, q, f) + at]
                        for i in range(3):
                            term = area[i] * x
                            acc[i][f] = term if acc[i][f] is None else acc[i][f] + term
            inv = 1.0 / (w_ref[(now,) + at] + w_ref[(prev,) + at])
            for i in range(3):
                for f in range(9):
                    out_ref[(9 * i + f, 0) + at] = acc[i][f] * inv


def gradients(fields, areas, volume, zh, th):
    whole = lambda shape: pl.BlockSpec(shape, lambda a: (0,) * len(shape))
    return pl.pallas_call(
        gradient_kernel,
        grid=(8,),
        out_shape=jax.ShapeDtypeStruct((27, 8, 32, 256), F32),
        in_specs=[
            pl.BlockSpec((9, 1, 32, 256), lambda a: (0, a, 0, 0)),
            pl.BlockSpec((3, 8, 1, 32, 256), lambda a: (0, 0, a, 0, 0)),
            pl.BlockSpec((1, 32, 256), lambda a: (a, 0, 0)),
            whole((24, 32, 256)),
            whole((24, 9, 256)),
        ],
        out_specs=pl.BlockSpec((27, 1, 32, 256), lambda a: (0, a, 0, 0)),
        scratch_shapes=[
            pltpu.VMEM((2, 4, 9, 32, 256), F32),
            pltpu.VMEM((2, 3, 4, 32, 256), F32),
            pltpu.VMEM((3, 4, 32, 256), F32),
            pltpu.VMEM((2, 32, 256), F32),
        ],
        cost_estimate=pl.CostEstimate(flops=30_000_000, bytes_accessed=14_000_000, transcendentals=0),
        name="gradients",
    )(fields, areas, volume, zh, th)


def diffuse_kernel(src_ref, zlo_ref, zhi_ref, tlo_ref, thi_ref, k_ref, vn_ref, kzl_ref, kzh_ref, ktl_ref, kth_ref, out_ref, w_ref):
    row = iota((32, 256), 0)
    lane = iota((32, 256), 1)

    @pl.when(pl.program_id(0) == 0)
    def _():
        for a in range(8):
            k = k_ref[a]
            near = [
                kzl_ref[...] if a == 0 else k_ref[a - 1],
                kzh_ref[...] if a == 7 else k_ref[a + 1],
                jnp.where(row == 0, ktl_ref[a : a + 1], pltpu.roll(k, 1, 0)),
                jnp.where(row == 31, kth_ref[a : a + 1], pltpu.roll(k, 31, 0)),
                jnp.where(lane == 0, 0.0, pltpu.roll(k, 1, 1)),
                jnp.where(lane == 255, 0.0, pltpu.roll(k, 255, 1)),
            ]
            scale = (0.2 * k) / vn_ref[a]
            total = None
            for n, kn in enumerate(near):
                w = scale * kn / (k + kn)
                w_ref[n, a] = w
                total = w if total is None else total + w
            w_ref[6, a] = 1.0 - total

    for a in range(8):
        s = src_ref[0, a]
        near = [
            zlo_ref[0] if a == 0 else src_ref[0, a - 1],
            zhi_ref[0] if a == 7 else src_ref[0, a + 1],
            jnp.where(row == 0, tlo_ref[0, a : a + 1], pltpu.roll(s, 1, 0)),
            jnp.where(row == 31, thi_ref[0, a : a + 1], pltpu.roll(s, 31, 0)),
            pltpu.roll(s, 1, 1),
            pltpu.roll(s, 255, 1),
        ]
        out = w_ref[6, a] * s
        for n in range(6):
            out = out + w_ref[n, a] * near[n]
        out_ref[0, a] = out


def diffuse(src, zlo, zhi, tlo, thi, k, vn, kzl, kzh, ktl, kth):
    whole = lambda shape: pl.BlockSpec(shape, lambda f: (0,) * len(shape))
    each = lambda shape: pl.BlockSpec((1,) + shape, lambda f: (f,) + (0,) * len(shape))
    return pl.pallas_call(
        diffuse_kernel,
        grid=(9,),
        out_shape=jax.ShapeDtypeStruct((9, 8, 32, 256), F32),
        in_specs=[
            each((8, 32, 256)), each((32, 256)), each((32, 256)), each((8, 256)), each((8, 256)),
            whole((8, 32, 256)), whole((8, 32, 256)), whole((32, 256)), whole((32, 256)), whole((8, 256)), whole((8, 256)),
        ],
        out_specs=each((8, 32, 256)),
        scratch_shapes=[pltpu.VMEM((7, 8, 32, 256), F32)],
        name="diffuse",
    )(src, zlo, zhi, tlo, thi, k, vn, kzl, kzh, ktl, kth)


def exchange_kernel(
    loads_ref, dest_ref, cell_ref, fz_ref, az_ref, vz_ref, sz_ref, kz_ref, kz0_ref,
    ft_ref, at_ref, vt_ref, st_ref, kt_ref, kt0_ref,
    chan_ref, zh_ref, th_ref, kza_ref, kn_ref,
    acc_ref, d_ref, rank_ref, out_buf, in_buf, azs, ts, cs, kbs, zr, tr, cr, kar, knr,
    send_sems, recv_sems, psend_sem, precv_sem, own_sem,
):
    slab, sector = lax.axis_index("slab"), lax.axis_index("sector")
    me = slab * 4 + sector
    barrier = pltpu.get_barrier_semaphore()

    def greet(k, unused):
        to = lax.rem(me + k, 128)
        pl.semaphore_signal(barrier, inc=1, device_id=(to // 4, lax.rem(to, 4)), device_id_type=pl.DeviceIdType.MESH)
        return unused

    lax.fori_loop(1, 128, greet, 0)

    for n in range(12):
        azs[n] = az_ref[n // 4, n % 4, 0].astype(F32)
    areas_t = [at_ref[i, k, :, 7, :].astype(F32) for i in range(3) for k in (2, 3, 6, 7)]
    for f in range(9):
        ts[f] = ft_ref[f, :, 7, :]
        cs[f : f + 1] = fz_ref[f, 0, 31:32]
    for n in range(12):
        ts[9 + n] = areas_t[n]
        cs[9 + n : 10 + n] = az_ref[n // 4, n % 4, 0].astype(F32)[31:32]
    for n, (t_ref, z_ref) in enumerate(((vt_ref, vz_ref), (st_ref, sz_ref), (kt_ref, kz_ref))):
        ts[21 + n] = t_ref[:, 7, :]
        cs[21 + n : 22 + n] = z_ref[0, 31:32]
    kbs[...] = kt0_ref[:, 0, :]

    blk, devices = 256, 128
    earlier = before(blk)
    carry = jnp.zeros((devices, 1), F32)
    count = 4096 // blk
    for b in range(count):
        d_ref[b * 128 : (b + 1) * 128, :] = one_hot(dest_ref[:, b * blk : (b + 1) * blk], devices)
    counts = jnp.dot(d_ref[...], earlier, preferred_element_type=F32)
    for b in range(count):
        df = d_ref[b * 128 : (b + 1) * 128, :].astype(F32)
        rank_ref[:, b * blk : (b + 1) * blk] = jnp.sum(
            df * (counts[b * 128 : (b + 1) * 128] + carry), axis=0, keepdims=True
        ).astype(I32)
        carry = carry + jnp.sum(df, axis=1, keepdims=True)

    above = (lax.rem(slab + 1, 32), sector)
    below = (lax.rem(slab + 31, 32), sector)
    ahead = (slab, lax.rem(sector + 1, 4))
    behind = (slab, lax.rem(sector + 3, 4))
    across = (lax.rem(slab + 1, 32), lax.rem(sector + 1, 4))
    halo = [
        (sz_ref.at[0], zr.at[22], above),
        (kz_ref.at[0], zr.at[23], above),
        (kz0_ref.at[0], kar, below),
        (kbs, knr, behind),
        (ts, tr, ahead),
        (cs, cr, across),
        (vz_ref.at[0], zr.at[21], above),
        (fz_ref.at[:, 0], zr.at[0:9], above),
        (azs, zr.at[9:21], above),
    ]
    copies = [
        pltpu.make_async_remote_copy(
            src_ref=s, dst_ref=t, send_sem=send_sems.at[n], recv_sem=recv_sems.at[n],
            device_id=to, device_id_type=pl.DeviceIdType.MESH,
        )
        for n, (s, t, to) in enumerate(halo)
    ]
    pl.semaphore_wait(barrier, 127)
    for copy in copies:
        copy.start()

    acc_ref[...] = jnp.zeros_like(acc_ref)
    part = 512
    for b in range(4096 // part):
        sl = pl.ds(b * part, part)
        o = one_hot(rank_ref[:, sl], 64)
        hi, lo = split(loads_ref[:, sl])
        cell = cell_ref[:, sl]
        row = (lax.shift_right_logical(cell, 8) * 256).astype(F32).astype(BF16)
        col = ((cell & 255) + 1).astype(F32).astype(BF16)
        his = jnp.concatenate([hi[c : c + 1] * o for c in range(9)] + [row * o], 0)
        los = jnp.concatenate([lo[c : c + 1] * o for c in range(9)] + [col * o], 0)
        d = jnp.concatenate([d_ref[(2 * b + i) * 128 : (2 * b + i + 1) * 128, :] for i in range(2)], 1)
        acc_ref[...] += nt(jnp.concatenate([his, los], 1), jnp.concatenate([d, d], 1))
    for s in range(5):
        out_buf[:, s, :] = acc_ref[s * 128 : (s + 1) * 128, :].T

    own = pltpu.make_async_copy(out_buf.at[me], in_buf.at[me], own_sem)
    own.start()

    def send(k, unused):
        to = lax.rem(me + k, 128)
        pltpu.make_async_remote_copy(
            src_ref=out_buf.at[to], dst_ref=in_buf.at[me], send_sem=psend_sem, recv_sem=precv_sem,
            device_id=(to // 4, lax.rem(to, 4)), device_id_type=pl.DeviceIdType.MESH,
        ).start()
        return unused

    lax.fori_loop(1, 128, send, 0)
    own.wait()
    for copy in copies:
        copy.wait()
    inside = slab > 0
    zh_ref[...] = jnp.where(inside, zr[...], 0.0)
    th_ref[:, 0:8, :] = tr[...]
    th_ref[:, 8, :] = jnp.where(inside, cr[...], 0.0)
    kza_ref[...] = jnp.where(slab < 31, kar[...], 0.0)
    kn_ref[...] = knr[...]
    most = pl.ds(0, 127)
    pltpu.make_async_copy(out_buf.at[most], in_buf.at[most], psend_sem).wait()
    pltpu.make_async_copy(out_buf.at[most], in_buf.at[most], precv_sem).wait()
    lane = iota((64, 128), 1) < 64
    for s in range(5):
        first, second = in_buf[0:64, s, :], in_buf[64:128, s, :]
        chan_ref[2 * s] = jnp.where(lane, first, pltpu.roll(second, 64, 1))
        chan_ref[2 * s + 1] = jnp.where(lane, pltpu.roll(first, 64, 1), second)


def exchange(loads, dest, cell, fields, areas, volume, sa, st, k):
    at = lambda shape, *index: pl.BlockSpec(shape, lambda i: index)
    whole = lambda *shape: at(shape, *(0,) * len(shape))
    shapes = [(10, 64, 128), (24, 32, 256), (24, 9, 256), (32, 256), (8, 256)]
    dma = pltpu.SemaphoreType.DMA
    vm = lambda *shape, t=F32: pltpu.VMEM(shape, t)
    plane, column = (1, 32, 256), (8, 8, 256)
    return pl.pallas_call(
        exchange_kernel,
        grid=(1,),
        out_shape=[jax.ShapeDtypeStruct(s, F32) for s in shapes],
        in_specs=[
            whole(9, 4096), whole(1, 4096), whole(1, 4096),
            at((9, 1, 32, 256), 0, 7, 0, 0), at((3, 4, 1, 32, 256), 0, 1, 7, 0, 0),
            at(plane, 7, 0, 0), at(plane, 7, 0, 0), at(plane, 7, 0, 0), at(plane, 0, 0, 0),
            at((9, 8, 8, 256), 0, 0, 3, 0), at((3, 8, 8, 8, 256), 0, 0, 0, 3, 0),
            at(column, 0, 3, 0), at(column, 0, 3, 0), at(column, 0, 3, 0), at(column, 0, 0, 0),
        ],
        out_specs=[whole(*s) for s in shapes],
        scratch_shapes=[
            vm(640, 128), vm(2048, 256, t=BF16), vm(1, 4096, t=I32), vm(128, 5, 128), vm(128, 5, 128),
            vm(12, 32, 256), vm(24, 8, 256), vm(24, 256), vm(8, 256),
            vm(24, 32, 256), vm(24, 8, 256), vm(24, 256), vm(32, 256), vm(8, 256),
            dma((9,)), dma((9,)), dma, dma, dma,
        ],
        compiler_params=pltpu.CompilerParams(has_side_effects=True, collective_id=0),
        name="exchange",
    )(loads, dest.reshape(1, 4096), cell.reshape(1, 4096), fields, areas, volume, sa, k, k,
      fields, areas, volume, st, k, k)


def up(x):
    return lax.ppermute(x, "slab", [(i, i + 1) for i in range(31)])


def down(x):
    return lax.ppermute(x, "slab", [(i + 1, i) for i in range(31)])


def onward(x):
    return lax.ppermute(x, "sector", [(i, (i + 1) % 4) for i in range(4)])


def backward(x):
    return lax.ppermute(x, "sector", [((i + 1) % 4, i) for i in range(4)])


def local(fields, volume, swept_axial, swept_angular, swept_radial, conductivity, corner_areas, parcel_loads, dest_device, dest_cell):
    chan, zh, th, k_above, k_next = exchange(
        parcel_loads, dest_device, dest_cell, fields, corner_areas, volume, swept_axial, swept_angular, conductivity
    )
    vn, src, zlo, zhi, tlo, thi = deposit(
        chan, fields, volume, swept_axial, swept_angular, swept_radial, zh[22], th[22, :8]
    )
    below, above = up(zhi), down(zlo)
    before_, after = onward(thi), backward(tlo)
    grads = gradients(fields, corner_areas, volume, zh, th)
    diffused = diffuse(src, below, above, before_, after, conductivity, vn, zh[23], k_above, th[23, :8], k_next)
    return vn, diffused, grads


def solution(mesh):
    P = jax.sharding.PartitionSpec
    cells = P("slab", "sector", None)
    in_specs = (
        P(None, "slab", "sector", None), cells, cells, cells, cells, cells,
        P(None, None, "slab", "sector", None), P(None, ("slab", "sector")), P(("slab", "sector"), None), P(("slab", "sector")),
    )
    out_specs = (cells, P(None, "slab", "sector", None), P(None, "slab", "sector", None))
    return jax.shard_map(local, mesh=mesh, in_specs=in_specs, out_specs=out_specs, check_vma=False)
```

```python
import jax
import jax.numpy as jnp
from jax import lax
from jax.experimental import pallas as pl
from jax.experimental.pallas import tpu as pltpu

F32, BF16, I32 = jnp.float32, jnp.bfloat16, jnp.int32
VM = pl.BlockSpec(memory_space=pltpu.VMEM)


def nt(a, b):
    return lax.dot_general(a, b, (((1,), (1,)), ((), ())), preferred_element_type=F32)


def iota(shape, dim):
    return lax.broadcasted_iota(I32, shape, dim)


def one_hot(row, count):
    n = row.shape[1]
    return jnp.where(iota((count, n), 0) == row, 1.0, 0.0).astype(BF16)


def split(x):
    hi = x.astype(BF16)
    return hi, (x - hi.astype(F32)).astype(BF16)


def before(n):
    return jnp.where(iota((n, n), 0) < iota((n, n), 1), 1.0, 0.0).astype(BF16)


GROUPS, ROWS, SLOTS, CHUNK = 16, 16, 256, 2048


def deposit_kernel(
    chan_ref, fields_ref, vol_ref, sa_ref, st_ref, sr_ref, saz_ref, stt_ref, grads_ref,
    vn_ref, src_ref, zlo_ref, zhi_ref, tlo_ref, thi_ref, grads_out_ref,
    sort_ref, acc_ref, rank_ref, gbuf, sems,
):
    arriving = pltpu.make_async_copy(grads_ref, gbuf, sems.at[0])
    leaving = pltpu.make_async_copy(gbuf, grads_out_ref, sems.at[1])
    arriving.start()
    sa, st, sr = sa_ref[...], st_ref[...], sr_ref[...]
    for a in range(8):
        below = saz_ref[...] if a == 0 else sa_ref[a - 1]
        stp = st_ref[a]
        row = iota((32, 256), 0)
        side = jnp.where(row == 0, stt_ref[a : a + 1], pltpu.roll(stp, 1, 0))
        srp = sr_ref[a]
        lane = iota((32, 256), 1)
        inner = jnp.where(lane == 0, 0.0, pltpu.roll(srp, 1, 1))
        vn_ref[a] = vol_ref[a] + sa_ref[a] - below + stp - side + srp - inner
    acc_ref[...] = jnp.zeros_like(acc_ref)
    earlier = before(256)

    def rows_of(c, start, count):
        part = chan_ref[c, start : start + count, :]
        return jnp.concatenate([part[i : i + 1] for i in range(count)], 1)

    for ch in range(8192 // CHUNK):
        nrow = CHUNK // 128
        carry = jnp.zeros((GROUPS, 1), F32)
        cell = rows_of(9, ch * nrow, nrow).astype(I32) - 1
        group = lax.shift_right_arithmetic(cell, 12)
        g = one_hot(group, GROUPS)
        gf = g.astype(F32)
        ranks = []
        for b in range(CHUNK // 256):
            gb = gf[:, b * 256 : (b + 1) * 256]
            count = jnp.dot(g[:, b * 256 : (b + 1) * 256], earlier, preferred_element_type=F32)
            ranks.append(jnp.sum(gb * (count + carry) , axis=0, keepdims=True))
            carry = carry + jnp.sum(gb, axis=1, keepdims=True)
        if ch == 1:
            arriving.wait()
            leaving.start()
        rank_ref[...] = jnp.concatenate(ranks, 1).astype(I32)
        most = jnp.max(carry).astype(I32)
        his, los = [], []
        for c in range(9):
            hi, lo = split(rows_of(c, ch * nrow, nrow))
            his.append(hi * g)
            los.append(lo * g)
        rowin = (lax.shift_right_logical(cell, 8) & 15).astype(F32).astype(BF16)
        colin = (cell & 255).astype(F32).astype(BF16)
        lhs = jnp.concatenate(his + los + [(rowin + 1.0) * g, colin * g], 0)

        def one_round(r, carry_unused):
            o = one_hot(rank_ref[...] - r * SLOTS, SLOTS)
            sort_ref[...] = nt(lhs, o)
            for gi in range(GROUPS):
                pick = lambda c: sort_ref[c * GROUPS + gi : c * GROUPS + gi + 1, :]
                rm = one_hot(pick(18).astype(I32) - 1, ROWS)
                j = one_hot(pick(19).astype(I32), 256)
                left = jnp.concatenate([pick(c).astype(BF16) * rm for c in range(18)], 0)
                out = nt(left, j)
                for f in range(9):
                    acc_ref[f, gi // 2, (gi % 2) * 16 : (gi % 2) * 16 + 16, :] += (
                        out[f * 16 : f * 16 + 16] + out[(9 + f) * 16 : (9 + f) * 16 + 16]
                    )
            return carry_unused

        lax.fori_loop(0, (most + SLOTS - 1) // SLOTS, one_round, 0)
    leaving.wait()
    for a in range(8):
        inv = 1.0 / vn_ref[a]
        for f in range(9):
            v = fields_ref[f, a] + acc_ref[f, a] * inv
            src_ref[f, a] = v
            if a == 0:
                zlo_ref[f] = v
            if a == 7:
                zhi_ref[f] = v
            tlo_ref[f, a : a + 1, :] = v[0:1]
            thi_ref[f, a : a + 1, :] = v[31:32]


def deposit(chan, fields, volume, sa, st, sr, saz, stt, grads):
    sd = jax.ShapeDtypeStruct
    return pl.pallas_call(
        deposit_kernel,
        out_shape=(
            sd((8, 32, 256), F32), sd((9, 8, 32, 256), F32),
            sd((9, 32, 256), F32), sd((9, 32, 256), F32), sd((9, 8, 256), F32), sd((9, 8, 256), F32),
            sd((27, 8, 32, 256), F32),
        ),
        in_specs=[VM] * 8 + [pl.BlockSpec(memory_space=pl.ANY)],
        out_specs=[VM] * 6 + [pl.BlockSpec(memory_space=pl.ANY)],
        scratch_shapes=[
            pltpu.VMEM((320, 256), F32),
            pltpu.VMEM((9, 8, 32, 256), F32),
            pltpu.VMEM((1, CHUNK), I32),
            pltpu.VMEM((27, 8, 32, 256), F32),
            pltpu.SemaphoreType.DMA((2,)),
        ],
        name="deposit",
    )(chan, fields, volume, sa, st, sr, saz, stt, grads)


def t_shift(x, edge):
    return jnp.where(iota(x.shape, 0) == 0, edge, pltpu.roll(x, 1, 0))


def r_shift(x):
    n = x.shape[1]
    return jnp.where(iota(x.shape, 1) == n - 1, 0.0, pltpu.roll(x, n - 1, 1))


def prepare(f_ref, w_ref, slot, field, vol, edge):
    for f in range(9):
        x = field(f)
        xt = t_shift(x, edge(f))
        f_ref[slot, 0, f] = r_shift(x)
        f_ref[slot, 1, f] = x
        f_ref[slot, 2, f] = r_shift(xt)
        f_ref[slot, 3, f] = xt
    v = vol * 0.125
    v = v + t_shift(v, edge(21) * 0.125)
    w_ref[slot] = v + r_shift(v)


def prepare_areas(a_ref, area, edge):
    for i in range(3):
        for q in range(4):
            x = area(i, q)
            if q // 2 == 1:
                x = t_shift(x, edge(i, q))
            a_ref[i, q] = x if q % 2 == 1 else pltpu.roll(x, 255, 1)


def gradient_plane(f_ref, w_ref, a0_ref, a1_ref, now, prev, out_ref, a):
    for t in range(4):
        for h in range(2):
            at = (pl.ds(8 * t, 8), pl.ds(128 * h, 128))
            inv = 1.0 / (w_ref[(now,) + at] + w_ref[(prev,) + at])
            for i in range(3):
                acc = [None] * 9
                for dz in range(2):
                    for q in range(4):
                        area = (a1_ref if dz else a0_ref)[(i, q) + at]
                        for f in range(9):
                            term = area * f_ref[(prev if dz else now, q, f) + at]
                            acc[f] = term if dz + q == 0 else acc[f] + term
                for f in range(9):
                    out_ref[(9 * i + f, a) + at] = acc[f] * inv


def diffuse_kernel(src_ref, zlo_ref, zhi_ref, tlo_ref, thi_ref, k_ref, vn_ref, kzl_ref, kzh_ref, ktl_ref, kth_ref, out_ref, w_ref):
    row = iota((32, 256), 0)
    lane = iota((32, 256), 1)

    @pl.when(pl.program_id(0) == 0)
    def _():
        for a in range(8):
            k = k_ref[a]
            near = [
                kzl_ref[...] if a == 0 else k_ref[a - 1],
                kzh_ref[...] if a == 7 else k_ref[a + 1],
                jnp.where(row == 0, ktl_ref[a : a + 1], pltpu.roll(k, 1, 0)),
                jnp.where(row == 31, kth_ref[a : a + 1], pltpu.roll(k, 31, 0)),
                jnp.where(lane == 0, 0.0, pltpu.roll(k, 1, 1)),
                jnp.where(lane == 255, 0.0, pltpu.roll(k, 255, 1)),
            ]
            scale = (0.2 * k) / vn_ref[a]
            total = None
            for n, kn in enumerate(near):
                w = scale * kn / (k + kn)
                w_ref[n, a] = w
                total = w if total is None else total + w
            w_ref[6, a] = 1.0 - total

    for a in range(8):
        s = src_ref[0, a]
        near = [
            zlo_ref[0] if a == 0 else src_ref[0, a - 1],
            zhi_ref[0] if a == 7 else src_ref[0, a + 1],
            jnp.where(row == 0, tlo_ref[0, a : a + 1], pltpu.roll(s, 1, 0)),
            jnp.where(row == 31, thi_ref[0, a : a + 1], pltpu.roll(s, 31, 0)),
            pltpu.roll(s, 1, 1),
            pltpu.roll(s, 255, 1),
        ]
        out = w_ref[6, a] * s
        for n in range(6):
            out = out + w_ref[n, a] * near[n]
        out_ref[0, a] = out


def diffuse(src, zlo, zhi, tlo, thi, k, vn, kzl, kzh, ktl, kth):
    whole = lambda shape: pl.BlockSpec(shape, lambda f: (0,) * len(shape))
    each = lambda shape: pl.BlockSpec((1,) + shape, lambda f: (f,) + (0,) * len(shape))
    return pl.pallas_call(
        diffuse_kernel,
        grid=(9,),
        out_shape=jax.ShapeDtypeStruct((9, 8, 32, 256), F32),
        in_specs=[
            each((8, 32, 256)), each((32, 256)), each((32, 256)), each((8, 256)), each((8, 256)),
            whole((8, 32, 256)), whole((8, 32, 256)), whole((32, 256)), whole((32, 256)), whole((8, 256)), whole((8, 256)),
        ],
        out_specs=each((8, 32, 256)),
        scratch_shapes=[pltpu.VMEM((7, 8, 32, 256), F32)],
        name="diffuse",
    )(src, zlo, zhi, tlo, thi, k, vn, kzl, kzh, ktl, kth)


def exchange_kernel(
    loads_ref, dest_ref, cell_ref, sz_ref, kz_ref, kz0_ref, st_ref, kt_ref, kt0_ref,
    fields_ref, areas_ref, vol_ref,
    chan_ref, saz_ref, stt_ref, kzl_ref, kzh_ref, ktl_ref, kth_ref, grads_ref,
    acc_ref, d_ref, rank_ref, out_buf, in_buf, azs, ts, cs, kbs, zr, tr, cr, kar, knr,
    fbuf, abuf, vbuf, gbuf, f_ref, w_ref, a0_ref, a1_ref,
    send_sems, recv_sems, psend_sem, precv_sem, own_sem, load_sems, store_sems,
):
    slab, sector = lax.axis_index("slab"), lax.axis_index("sector")
    me = slab * 4 + sector
    barrier = pltpu.get_barrier_semaphore()
    loading = [
        pltpu.make_async_copy(s, t, load_sems.at[n])
        for n, (s, t) in enumerate(((fields_ref, fbuf), (areas_ref, abuf), (vol_ref, vbuf)))
    ]
    for copy in loading:
        copy.start()

    def greet(k, unused):
        to = lax.rem(me + k, 128)
        pl.semaphore_signal(barrier, inc=1, device_id=(to // 4, lax.rem(to, 4)), device_id_type=pl.DeviceIdType.MESH)
        return unused

    lax.fori_loop(1, 128, greet, 0)

    blk, devices = 256, 128
    earlier = before(blk)
    carry = jnp.zeros((devices, 1), F32)
    count = 4096 // blk
    for b in range(count):
        d_ref[b * 128 : (b + 1) * 128, :] = one_hot(dest_ref[:, b * blk : (b + 1) * blk], devices)
    counts = jnp.dot(d_ref[...], earlier, preferred_element_type=F32)
    for b in range(count):
        df = d_ref[b * 128 : (b + 1) * 128, :].astype(F32)
        rank_ref[:, b * blk : (b + 1) * blk] = jnp.sum(
            df * (counts[b * 128 : (b + 1) * 128] + carry), axis=0, keepdims=True
        ).astype(I32)
        carry = carry + jnp.sum(df, axis=1, keepdims=True)

    for copy in loading:
        copy.wait()
    for n in range(12):
        x = abuf[n // 4, 4 + n % 4, 7].astype(F32)
        azs[n] = x
        cs[9 + n : 10 + n] = x[31:32]
        for a in range(8):
            ts[9 + n, a : a + 1, :] = abuf[n // 4, (2, 3, 6, 7)[n % 4], a].astype(F32)[31:32]
    for f in range(9):
        ts[f] = fbuf[f, :, 31, :]
        cs[f : f + 1] = fbuf[f, 7, 31:32]
    ts[21] = vbuf[:, 31, :]
    cs[21:22] = vbuf[7, 31:32]
    for n, (t_ref, z_ref) in enumerate(((st_ref, sz_ref), (kt_ref, kz_ref))):
        ts[22 + n] = t_ref[:, 7, :]
        cs[22 + n : 23 + n] = z_ref[0, 31:32]
    kbs[...] = kt0_ref[:, 0, :]

    above = (lax.rem(slab + 1, 32), sector)
    below = (lax.rem(slab + 31, 32), sector)
    ahead = (slab, lax.rem(sector + 1, 4))
    behind = (slab, lax.rem(sector + 3, 4))
    across = (lax.rem(slab + 1, 32), lax.rem(sector + 1, 4))
    halo = [
        (sz_ref.at[0], zr.at[22], above),
        (kz_ref.at[0], zr.at[23], above),
        (kz0_ref.at[0], kar, below),
        (kbs, knr, behind),
        (ts, tr, ahead),
        (cs, cr, across),
        (vbuf.at[7], zr.at[21], above),
        (fbuf.at[:, 7], zr.at[0:9], above),
        (azs, zr.at[9:21], above),
    ]
    copies = [
        pltpu.make_async_remote_copy(
            src_ref=s, dst_ref=t, send_sem=send_sems.at[n], recv_sem=recv_sems.at[n],
            device_id=to, device_id_type=pl.DeviceIdType.MESH,
        )
        for n, (s, t, to) in enumerate(halo)
    ]
    pl.semaphore_wait(barrier, 127)
    for copy in copies:
        copy.start()

    acc_ref[...] = jnp.zeros_like(acc_ref)
    part = 512
    for b in range(4096 // part):
        sl = pl.ds(b * part, part)
        o = one_hot(rank_ref[:, sl], 64)
        hi, lo = split(loads_ref[:, sl])
        cell = cell_ref[:, sl]
        row = (lax.shift_right_logical(cell, 8) * 256).astype(F32).astype(BF16)
        col = ((cell & 255) + 1).astype(F32).astype(BF16)
        his = jnp.concatenate([hi[c : c + 1] * o for c in range(9)] + [row * o], 0)
        los = jnp.concatenate([lo[c : c + 1] * o for c in range(9)] + [col * o], 0)
        d = jnp.concatenate([d_ref[(2 * b + i) * 128 : (2 * b + i + 1) * 128, :] for i in range(2)], 1)
        acc_ref[...] += nt(jnp.concatenate([his, los], 1), jnp.concatenate([d, d], 1))
    for s in range(5):
        out_buf[:, s, :] = acc_ref[s * 128 : (s + 1) * 128, :].T

    own = pltpu.make_async_copy(out_buf.at[me], in_buf.at[me], own_sem)
    own.start()

    def send(k, unused):
        to = lax.rem(me + k, 128)
        pltpu.make_async_remote_copy(
            src_ref=out_buf.at[to], dst_ref=in_buf.at[me], send_sem=psend_sem, recv_sem=precv_sem,
            device_id=(to // 4, lax.rem(to, 4)), device_id_type=pl.DeviceIdType.MESH,
        ).start()
        return unused

    lax.fori_loop(1, 128, send, 0)
    copies[4].wait()

    def beside(plane):
        return lambda c: tr[c, pl.ds(plane, 1), :]

    def prepare_own(slot, plane):
        prepare(f_ref, w_ref, slot, lambda f: fbuf[f, plane], vbuf[plane], beside(plane))

    def own_areas(ref, plane, dz):
        prepare_areas(
            ref, lambda i, q: abuf[i, 4 * dz + q, plane].astype(F32),
            lambda i, q: beside(plane)(9 + 4 * i + 2 * dz + q % 2),
        )

    def store(a):
        return pltpu.make_async_copy(gbuf.at[:, a], grads_ref.at[:, a], store_sems.at[a])

    prepare_own(1, 7)

    def plane(n, unused):
        a = 7 - n
        now = lax.rem(a, 2)
        prepare_own(1 - now, a - 1)
        own_areas(a0_ref, a, 0)
        own_areas(a1_ref, a - 1, 1)
        gradient_plane(f_ref, w_ref, a0_ref, a1_ref, now, 1 - now, gbuf, a)
        store(a).start()
        return unused

    lax.fori_loop(0, 7, plane, 0)
    own.wait()
    for n, copy in enumerate(copies):
        if n != 4:
            copy.wait()
    inside = slab > 0

    def under(x):
        return jnp.where(inside, x, 0.0)

    prepare(f_ref, w_ref, 1, lambda f: under(zr[f]), under(zr[21]), lambda c: under(cr[c : c + 1, :]))
    own_areas(a0_ref, 0, 0)
    prepare_areas(a1_ref, lambda i, q: zr[9 + 4 * i + q], lambda i, q: cr[9 + 4 * i + q : 10 + 4 * i + q, :])
    gradient_plane(f_ref, w_ref, a0_ref, a1_ref, 0, 1, gbuf, 0)
    store(0).start()
    saz_ref[...] = under(zr[22])
    kzl_ref[...] = under(zr[23])
    kzh_ref[...] = jnp.where(slab < 31, kar[...], 0.0)
    stt_ref[...] = tr[22]
    ktl_ref[...] = tr[23]
    kth_ref[...] = knr[...]
    most = pl.ds(0, 127)
    pltpu.make_async_copy(out_buf.at[most], in_buf.at[most], psend_sem).wait()
    pltpu.make_async_copy(out_buf.at[most], in_buf.at[most], precv_sem).wait()
    lane = iota((64, 128), 1) < 64
    for s in range(5):
        first, second = in_buf[0:64, s, :], in_buf[64:128, s, :]
        chan_ref[2 * s] = jnp.where(lane, first, pltpu.roll(second, 64, 1))
        chan_ref[2 * s + 1] = jnp.where(lane, pltpu.roll(first, 64, 1), second)
    for a in range(8):
        store(a).wait()


def exchange(loads, dest, cell, fields, areas, volume, sa, st, k):
    at = lambda shape, *index: pl.BlockSpec(shape, lambda i: index)
    whole = lambda *shape: at(shape, *(0,) * len(shape))
    any_ = pl.BlockSpec(memory_space=pl.ANY)
    shapes = [(10, 64, 128), (32, 256), (8, 256), (32, 256), (32, 256), (8, 256), (8, 256)]
    dma = pltpu.SemaphoreType.DMA
    vm = lambda *shape, t=F32: pltpu.VMEM(shape, t)
    plane, column = (1, 32, 256), (8, 8, 256)
    return pl.pallas_call(
        exchange_kernel,
        grid=(1,),
        out_shape=[jax.ShapeDtypeStruct(s, F32) for s in shapes + [(27, 8, 32, 256)]],
        in_specs=[
            whole(9, 4096), whole(1, 4096), whole(1, 4096),
            at(plane, 7, 0, 0), at(plane, 7, 0, 0), at(plane, 0, 0, 0),
            at(column, 0, 3, 0), at(column, 0, 3, 0), at(column, 0, 0, 0),
            any_, any_, any_,
        ],
        out_specs=[whole(*s) for s in shapes] + [any_],
        scratch_shapes=[
            vm(640, 128), vm(2048, 256, t=BF16), vm(1, 4096, t=I32), vm(128, 5, 128), vm(128, 5, 128),
            vm(12, 32, 256), vm(24, 8, 256), vm(24, 256), vm(8, 256),
            vm(24, 32, 256), vm(24, 8, 256), vm(24, 256), vm(32, 256), vm(8, 256),
            vm(9, 8, 32, 256), vm(3, 8, 8, 32, 256, t=BF16), vm(8, 32, 256), vm(27, 8, 32, 256),
            vm(2, 4, 9, 32, 256), vm(2, 32, 256), vm(3, 4, 32, 256), vm(3, 4, 32, 256),
            dma((9,)), dma((9,)), dma, dma, dma, dma((3,)), dma((8,)),
        ],
        compiler_params=pltpu.CompilerParams(has_side_effects=True, collective_id=0),
        name="exchange",
    )(loads, dest.reshape(1, 4096), cell.reshape(1, 4096), sa, k, k, st, k, k, fields, areas, volume)


def up(x):
    return lax.ppermute(x, "slab", [(i, i + 1) for i in range(31)])


def down(x):
    return lax.ppermute(x, "slab", [(i + 1, i) for i in range(31)])


def onward(x):
    return lax.ppermute(x, "sector", [(i, (i + 1) % 4) for i in range(4)])


def backward(x):
    return lax.ppermute(x, "sector", [((i + 1) % 4, i) for i in range(4)])


def local(fields, volume, swept_axial, swept_angular, swept_radial, conductivity, corner_areas, parcel_loads, dest_device, dest_cell):
    chan, saz, stt, kzl, kzh, ktl, kth, grads = exchange(
        parcel_loads, dest_device, dest_cell, fields, corner_areas, volume, swept_axial, swept_angular, conductivity
    )
    vn, src, zlo, zhi, tlo, thi, grads = deposit(
        chan, fields, volume, swept_axial, swept_angular, swept_radial, saz, stt, grads
    )
    below, above = up(zhi), down(zlo)
    before_, after = onward(thi), backward(tlo)
    diffused = diffuse(src, below, above, before_, after, conductivity, vn, kzl, kzh, ktl, kth)
    return vn, diffused, grads


def solution(mesh):
    P = jax.sharding.PartitionSpec
    cells = P("slab", "sector", None)
    in_specs = (
        P(None, "slab", "sector", None), cells, cells, cells, cells, cells,
        P(None, None, "slab", "sector", None), P(None, ("slab", "sector")), P(("slab", "sector"), None), P(("slab", "sector")),
    )
    out_specs = (cells, P(None, "slab", "sector", None), P(None, "slab", "sector", None))
    return jax.shard_map(local, mesh=mesh, in_specs=in_specs, out_specs=out_specs, check_vma=False)
```

```python
import jax
import jax.numpy as jnp
from jax import lax
from jax.experimental import pallas as pl
from jax.experimental.pallas import tpu as pltpu

F32, BF16, I32 = jnp.float32, jnp.bfloat16, jnp.int32
VM = pl.BlockSpec(memory_space=pltpu.VMEM)


def nt(a, b):
    return lax.dot_general(a, b, (((1,), (1,)), ((), ())), preferred_element_type=F32)


def iota(shape, dim):
    return lax.broadcasted_iota(I32, shape, dim)


def one_hot(row, count):
    n = row.shape[1]
    return jnp.where(iota((count, n), 0) == row, 1.0, 0.0).astype(BF16)


def split(x):
    hi = x.astype(BF16)
    return hi, (x - hi.astype(F32)).astype(BF16)


def before(n):
    return jnp.where(iota((n, n), 0) < iota((n, n), 1), 1.0, 0.0).astype(BF16)


GROUPS, ROWS, SLOTS, CHUNK = 16, 16, 256, 2048


def deposit_kernel(
    chan_ref, fields_ref, vol_ref, sa_ref, st_ref, sr_ref, saz_ref, stt_ref, grads_ref,
    vn_ref, src_ref, tlo_ref, thi_ref, grads_out_ref,
    sort_ref, acc_ref, rank_ref, gbuf, sems,
):
    arriving = pltpu.make_async_copy(grads_ref, gbuf, sems.at[0])
    leaving = pltpu.make_async_copy(gbuf, grads_out_ref, sems.at[1])
    arriving.start()
    sa, st, sr = sa_ref[...], st_ref[...], sr_ref[...]
    for a in range(8):
        below = saz_ref[...] if a == 0 else sa_ref[a - 1]
        stp = st_ref[a]
        row = iota((32, 256), 0)
        side = jnp.where(row == 0, stt_ref[a : a + 1], pltpu.roll(stp, 1, 0))
        srp = sr_ref[a]
        lane = iota((32, 256), 1)
        inner = jnp.where(lane == 0, 0.0, pltpu.roll(srp, 1, 1))
        vn_ref[a] = vol_ref[a] + sa_ref[a] - below + stp - side + srp - inner
    acc_ref[...] = jnp.zeros_like(acc_ref)
    earlier = before(256)

    def rows_of(c, start, count):
        part = chan_ref[c, start : start + count, :]
        return jnp.concatenate([part[i : i + 1] for i in range(count)], 1)

    for ch in range(8192 // CHUNK):
        nrow = CHUNK // 128
        carry = jnp.zeros((GROUPS, 1), F32)
        cell = rows_of(9, ch * nrow, nrow).astype(I32) - 1
        group = lax.shift_right_arithmetic(cell, 12)
        g = one_hot(group, GROUPS)
        gf = g.astype(F32)
        ranks = []
        for b in range(CHUNK // 256):
            gb = gf[:, b * 256 : (b + 1) * 256]
            count = jnp.dot(g[:, b * 256 : (b + 1) * 256], earlier, preferred_element_type=F32)
            ranks.append(jnp.sum(gb * (count + carry) , axis=0, keepdims=True))
            carry = carry + jnp.sum(gb, axis=1, keepdims=True)
        if ch == 1:
            arriving.wait()
            leaving.start()
        rank_ref[...] = jnp.concatenate(ranks, 1).astype(I32)
        most = jnp.max(carry).astype(I32)
        his, los = [], []
        for c in range(9):
            hi, lo = split(rows_of(c, ch * nrow, nrow))
            his.append(hi * g)
            los.append(lo * g)
        rowin = (lax.shift_right_logical(cell, 8) & 15).astype(F32).astype(BF16)
        colin = (cell & 255).astype(F32).astype(BF16)
        lhs = jnp.concatenate(his + los + [(rowin + 1.0) * g, colin * g], 0)

        def one_round(r, carry_unused):
            o = one_hot(rank_ref[...] - r * SLOTS, SLOTS)
            sort_ref[...] = nt(lhs, o)
            for gi in range(GROUPS):
                pick = lambda c: sort_ref[c * GROUPS + gi : c * GROUPS + gi + 1, :]
                rm = one_hot(pick(18).astype(I32) - 1, ROWS)
                j = one_hot(pick(19).astype(I32), 256)
                left = jnp.concatenate([pick(c).astype(BF16) * rm for c in range(18)], 0)
                out = nt(left, j)
                for f in range(9):
                    acc_ref[f, gi // 2, (gi % 2) * 16 : (gi % 2) * 16 + 16, :] += (
                        out[f * 16 : f * 16 + 16] + out[(9 + f) * 16 : (9 + f) * 16 + 16]
                    )
            return carry_unused

        lax.fori_loop(0, (most + SLOTS - 1) // SLOTS, one_round, 0)
    leaving.wait()
    for a in range(8):
        inv = 1.0 / vn_ref[a]
        for f in range(9):
            v = fields_ref[f, a] + acc_ref[f, a] * inv
            src_ref[f, a] = v
            tlo_ref[f, a : a + 1, :] = v[0:1]
            thi_ref[f, a : a + 1, :] = v[31:32]


def deposit(chan, fields, volume, sa, st, sr, saz, stt, grads):
    sd = jax.ShapeDtypeStruct
    return pl.pallas_call(
        deposit_kernel,
        out_shape=(
            sd((8, 32, 256), F32), sd((9, 8, 32, 256), F32),
            sd((9, 8, 256), F32), sd((9, 8, 256), F32),
            sd((27, 8, 32, 256), F32),
        ),
        in_specs=[VM] * 8 + [pl.BlockSpec(memory_space=pl.ANY)],
        out_specs=[VM] * 4 + [pl.BlockSpec(memory_space=pl.ANY)],
        scratch_shapes=[
            pltpu.VMEM((320, 256), F32),
            pltpu.VMEM((9, 8, 32, 256), F32),
            pltpu.VMEM((1, CHUNK), I32),
            pltpu.VMEM((27, 8, 32, 256), F32),
            pltpu.SemaphoreType.DMA((2,)),
        ],
        name="deposit",
    )(chan, fields, volume, sa, st, sr, saz, stt, grads)


def t_shift(x, edge):
    return jnp.where(iota(x.shape, 0) == 0, edge, pltpu.roll(x, 1, 0))


def r_shift(x):
    n = x.shape[1]
    return jnp.where(iota(x.shape, 1) == n - 1, 0.0, pltpu.roll(x, n - 1, 1))


def prepare(f_ref, w_ref, slot, field, vol, edge):
    for f in range(9):
        x = field(f)
        xt = t_shift(x, edge(f))
        f_ref[slot, 0, f] = r_shift(x)
        f_ref[slot, 1, f] = x
        f_ref[slot, 2, f] = r_shift(xt)
        f_ref[slot, 3, f] = xt
    v = vol * 0.125
    v = v + t_shift(v, edge(21) * 0.125)
    w_ref[slot] = v + r_shift(v)


def prepare_areas(a_ref, area, edge):
    for i in range(3):
        for q in range(4):
            x = area(i, q)
            if q // 2 == 1:
                x = t_shift(x, edge(i, q))
            a_ref[i, q] = x if q % 2 == 1 else pltpu.roll(x, 255, 1)


def gradient_plane(f_ref, w_ref, a0_ref, a1_ref, now, prev, out_ref, a):
    def part(n, unused):
        i = lax.rem(n, 3)
        rows = pl.ds(pl.multiple_of(n // 3 * 8, 8), 8)
        inv = 1.0 / (w_ref[now, rows] + w_ref[prev, rows])
        acc = [None] * 9
        for dz in range(2):
            for q in range(4):
                area = (a1_ref if dz else a0_ref)[i, q, rows]
                for f in range(9):
                    term = area * f_ref[prev if dz else now, q, f, rows]
                    acc[f] = term if dz + q == 0 else acc[f] + term
        for f in range(9):
            out_ref[9 * i + f, a, rows] = acc[f] * inv
        return unused

    lax.fori_loop(0, 12, part, 0)


def diffuse_kernel(
    src_ref, tlo_ref, thi_ref, k_ref, vn_ref, kzl_ref, kzh_ref, ktl_ref, kth_ref, out_ref,
    sbuf, obuf, zlo, zhi, tlo, thi, w_ref, send_sems, recv_sems, load_sem, store_sems,
):
    slab, sector = lax.axis_index("slab"), lax.axis_index("sector")
    above = (lax.rem(slab + 1, 32), sector)
    below = (lax.rem(slab + 31, 32), sector)
    ahead = (slab, lax.rem(sector + 1, 4))
    behind = (slab, lax.rem(sector + 3, 4))
    barrier = pltpu.get_barrier_semaphore()
    for to in (above, below, ahead, behind):
        pl.semaphore_signal(barrier, inc=1, device_id=to, device_id_type=pl.DeviceIdType.MESH)
    loading = pltpu.make_async_copy(src_ref, sbuf, load_sem)
    loading.start()
    halo = [
        (thi_ref, tlo, ahead), (tlo_ref, thi, behind),
        (src_ref.at[:, 7], zlo, above), (src_ref.at[:, 0], zhi, below),
    ]
    copies = [
        pltpu.make_async_remote_copy(
            src_ref=s, dst_ref=t, send_sem=send_sems.at[n], recv_sem=recv_sems.at[n],
            device_id=to, device_id_type=pl.DeviceIdType.MESH,
        )
        for n, (s, t, to) in enumerate(halo)
    ]
    pl.semaphore_wait(barrier, 4)
    for copy in copies:
        copy.start()
    row = iota((32, 256), 0)
    lane = iota((32, 256), 1)
    for a in range(8):
        k = k_ref[a]
        near = [
            kzl_ref[...] if a == 0 else k_ref[a - 1],
            kzh_ref[...] if a == 7 else k_ref[a + 1],
            jnp.where(row == 0, ktl_ref[a : a + 1], pltpu.roll(k, 1, 0)),
            jnp.where(row == 31, kth_ref[a : a + 1], pltpu.roll(k, 31, 0)),
            jnp.where(lane == 0, 0.0, pltpu.roll(k, 1, 1)),
            jnp.where(lane == 255, 0.0, pltpu.roll(k, 255, 1)),
        ]
        scale = (0.2 * k) / vn_ref[a]
        total = None
        for n, kn in enumerate(near):
            w = scale * kn / (k + kn)
            w_ref[n, a] = w
            total = w if total is None else total + w
        w_ref[6, a] = 1.0 - total
    loading.wait()
    copies[0].wait()
    copies[1].wait()

    def plane(f, a, under, over):
        s = sbuf[f, a]
        near = [
            under, over,
            jnp.where(row == 0, tlo[f, a : a + 1], pltpu.roll(s, 1, 0)),
            jnp.where(row == 31, thi[f, a : a + 1], pltpu.roll(s, 31, 0)),
            pltpu.roll(s, 1, 1),
            pltpu.roll(s, 255, 1),
        ]
        out = w_ref[6, a] * s
        for n in range(6):
            out = out + w_ref[n, a] * near[n]
        obuf[f, a] = out

    def inner(f, unused):
        for a in range(1, 7):
            plane(f, a, sbuf[f, a - 1], sbuf[f, a + 1])
        return unused

    lax.fori_loop(0, 9, inner, 0)
    middle = pltpu.make_async_copy(obuf.at[:, 1:7], out_ref.at[:, 1:7], store_sems.at[0])
    middle.start()
    copies[2].wait()
    copies[3].wait()

    def ends(f, unused):
        plane(f, 0, zlo[f], sbuf[f, 1])
        plane(f, 7, sbuf[f, 6], zhi[f])
        return unused

    lax.fori_loop(0, 9, ends, 0)
    first = pltpu.make_async_copy(obuf.at[:, 0], out_ref.at[:, 0], store_sems.at[1])
    last = pltpu.make_async_copy(obuf.at[:, 7], out_ref.at[:, 7], store_sems.at[2])
    first.start()
    last.start()
    middle.wait()
    first.wait()
    last.wait()


def diffuse(src, tlo, thi, k, vn, kzl, kzh, ktl, kth):
    any_ = pl.BlockSpec(memory_space=pl.ANY)
    dma = pltpu.SemaphoreType.DMA
    cells = (9, 8, 32, 256)
    return pl.pallas_call(
        diffuse_kernel,
        out_shape=jax.ShapeDtypeStruct(cells, F32),
        in_specs=[any_] * 3 + [VM] * 6,
        out_specs=any_,
        scratch_shapes=[
            pltpu.VMEM(cells, F32), pltpu.VMEM(cells, F32),
            pltpu.VMEM((9, 32, 256), F32), pltpu.VMEM((9, 32, 256), F32),
            pltpu.VMEM((9, 8, 256), F32), pltpu.VMEM((9, 8, 256), F32),
            pltpu.VMEM((7, 8, 32, 256), F32), dma((4,)), dma((4,)), dma, dma((3,)),
        ],
        compiler_params=pltpu.CompilerParams(has_side_effects=True, collective_id=1),
        name="diffuse",
    )(src, tlo, thi, k, vn, kzl, kzh, ktl, kth)


def exchange_kernel(
    loads_ref, dest_ref, cell_ref, sz_ref, kz_ref, kz0_ref, st_ref, kt_ref, kt0_ref,
    fields_ref, areas_ref, vol_ref,
    chan_ref, saz_ref, stt_ref, kzl_ref, kzh_ref, ktl_ref, kth_ref, grads_ref,
    acc_ref, d_ref, rank_ref, out_buf, in_buf, azs, ts, cs, kbs, zr, tr, cr, kar, knr,
    fbuf, abuf, vbuf, gbuf, f_ref, w_ref, a0_ref, a1_ref,
    send_sems, recv_sems, psend_sem, precv_sem, own_sem, load_sems, store_sems,
):
    slab, sector = lax.axis_index("slab"), lax.axis_index("sector")
    me = slab * 4 + sector
    barrier = pltpu.get_barrier_semaphore()
    loading = [
        pltpu.make_async_copy(s, t, load_sems.at[n])
        for n, (s, t) in enumerate(((fields_ref, fbuf), (areas_ref, abuf), (vol_ref, vbuf)))
    ]
    for copy in loading:
        copy.start()

    def greet(k, unused):
        to = lax.rem(me + k, 128)
        pl.semaphore_signal(barrier, inc=1, device_id=(to // 4, lax.rem(to, 4)), device_id_type=pl.DeviceIdType.MESH)
        return unused

    lax.fori_loop(1, 128, greet, 0)

    blk, devices = 256, 128
    earlier = before(blk)
    carry = jnp.zeros((devices, 1), F32)
    count = 4096 // blk
    for b in range(count):
        d_ref[b * 128 : (b + 1) * 128, :] = one_hot(dest_ref[:, b * blk : (b + 1) * blk], devices)
    counts = jnp.dot(d_ref[...], earlier, preferred_element_type=F32)
    for b in range(count):
        df = d_ref[b * 128 : (b + 1) * 128, :].astype(F32)
        rank_ref[:, b * blk : (b + 1) * blk] = jnp.sum(
            df * (counts[b * 128 : (b + 1) * 128] + carry), axis=0, keepdims=True
        ).astype(I32)
        carry = carry + jnp.sum(df, axis=1, keepdims=True)

    for copy in loading:
        copy.wait()
    for n in range(12):
        x = abuf[n // 4, 4 + n % 4, 7].astype(F32)
        azs[n] = x
        cs[9 + n : 10 + n] = x[31:32]
        for a in range(8):
            ts[9 + n, a : a + 1, :] = abuf[n // 4, (2, 3, 6, 7)[n % 4], a].astype(F32)[31:32]
    for f in range(9):
        ts[f] = fbuf[f, :, 31, :]
        cs[f : f + 1] = fbuf[f, 7, 31:32]
    ts[21] = vbuf[:, 31, :]
    cs[21:22] = vbuf[7, 31:32]
    for n, (t_ref, z_ref) in enumerate(((st_ref, sz_ref), (kt_ref, kz_ref))):
        ts[22 + n] = t_ref[:, 7, :]
        cs[22 + n : 23 + n] = z_ref[0, 31:32]
    kbs[...] = kt0_ref[:, 0, :]

    above = (lax.rem(slab + 1, 32), sector)
    below = (lax.rem(slab + 31, 32), sector)
    ahead = (slab, lax.rem(sector + 1, 4))
    behind = (slab, lax.rem(sector + 3, 4))
    across = (lax.rem(slab + 1, 32), lax.rem(sector + 1, 4))
    halo = [
        (sz_ref.at[0], zr.at[22], above),
        (kz_ref.at[0], zr.at[23], above),
        (kz0_ref.at[0], kar, below),
        (kbs, knr, behind),
        (ts, tr, ahead),
        (cs, cr, across),
        (vbuf.at[7], zr.at[21], above),
        (fbuf.at[:, 7], zr.at[0:9], above),
        (azs, zr.at[9:21], above),
    ]
    copies = [
        pltpu.make_async_remote_copy(
            src_ref=s, dst_ref=t, send_sem=send_sems.at[n], recv_sem=recv_sems.at[n],
            device_id=to, device_id_type=pl.DeviceIdType.MESH,
        )
        for n, (s, t, to) in enumerate(halo)
    ]
    acc_ref[...] = jnp.zeros_like(acc_ref)
    part = 512
    for b in range(4096 // part):
        sl = pl.ds(b * part, part)
        o = one_hot(rank_ref[:, sl], 64)
        hi, lo = split(loads_ref[:, sl])
        cell = cell_ref[:, sl]
        row = (lax.shift_right_logical(cell, 8) * 256).astype(F32).astype(BF16)
        col = ((cell & 255) + 1).astype(F32).astype(BF16)
        his = jnp.concatenate([hi[c : c + 1] * o for c in range(9)] + [row * o], 0)
        los = jnp.concatenate([lo[c : c + 1] * o for c in range(9)] + [col * o], 0)
        d = jnp.concatenate([d_ref[(2 * b + i) * 128 : (2 * b + i + 1) * 128, :] for i in range(2)], 1)
        acc_ref[...] += nt(jnp.concatenate([his, los], 1), jnp.concatenate([d, d], 1))
    for s in range(5):
        out_buf[:, s, :] = acc_ref[s * 128 : (s + 1) * 128, :].T

    pl.semaphore_wait(barrier, 127)
    for copy in copies:
        copy.start()
    own = pltpu.make_async_copy(out_buf.at[me], in_buf.at[me], own_sem)
    own.start()

    def send(k, unused):
        to = lax.rem(me + k, 128)
        pltpu.make_async_remote_copy(
            src_ref=out_buf.at[to], dst_ref=in_buf.at[me], send_sem=psend_sem, recv_sem=precv_sem,
            device_id=(to // 4, lax.rem(to, 4)), device_id_type=pl.DeviceIdType.MESH,
        ).start()
        return unused

    lax.fori_loop(1, 128, send, 0)
    copies[4].wait()

    def beside(plane):
        return lambda c: tr[c, pl.ds(plane, 1), :]

    def prepare_own(slot, plane):
        prepare(f_ref, w_ref, slot, lambda f: fbuf[f, plane], vbuf[plane], beside(plane))

    def own_areas(ref, plane, dz):
        prepare_areas(
            ref, lambda i, q: abuf[i, 4 * dz + q, plane].astype(F32),
            lambda i, q: beside(plane)(9 + 4 * i + 2 * dz + q % 2),
        )

    def store(a):
        return pltpu.make_async_copy(gbuf.at[:, a], grads_ref.at[:, a], store_sems.at[a])

    prepare_own(1, 7)

    def plane(n, unused):
        a = 7 - n
        now = lax.rem(a, 2)
        prepare_own(1 - now, a - 1)
        own_areas(a0_ref, a, 0)
        own_areas(a1_ref, a - 1, 1)
        gradient_plane(f_ref, w_ref, a0_ref, a1_ref, now, 1 - now, gbuf, a)
        store(a).start()
        return unused

    lax.fori_loop(0, 7, plane, 0)
    own.wait()
    for n, copy in enumerate(copies):
        if n != 4:
            copy.wait()
    inside = slab > 0

    def under(x):
        return jnp.where(inside, x, 0.0)

    prepare(f_ref, w_ref, 1, lambda f: under(zr[f]), under(zr[21]), lambda c: under(cr[c : c + 1, :]))
    own_areas(a0_ref, 0, 0)
    prepare_areas(a1_ref, lambda i, q: zr[9 + 4 * i + q], lambda i, q: cr[9 + 4 * i + q : 10 + 4 * i + q, :])
    gradient_plane(f_ref, w_ref, a0_ref, a1_ref, 0, 1, gbuf, 0)
    store(0).start()
    saz_ref[...] = under(zr[22])
    kzl_ref[...] = under(zr[23])
    kzh_ref[...] = jnp.where(slab < 31, kar[...], 0.0)
    stt_ref[...] = tr[22]
    ktl_ref[...] = tr[23]
    kth_ref[...] = knr[...]
    most = pl.ds(0, 127)
    pltpu.make_async_copy(out_buf.at[most], in_buf.at[most], psend_sem).wait()
    pltpu.make_async_copy(out_buf.at[most], in_buf.at[most], precv_sem).wait()
    lane = iota((64, 128), 1) < 64
    for s in range(5):
        first, second = in_buf[0:64, s, :], in_buf[64:128, s, :]
        chan_ref[2 * s] = jnp.where(lane, first, pltpu.roll(second, 64, 1))
        chan_ref[2 * s + 1] = jnp.where(lane, pltpu.roll(first, 64, 1), second)
    for a in range(8):
        store(a).wait()


def exchange(loads, dest, cell, fields, areas, volume, sa, st, k):
    at = lambda shape, *index: pl.BlockSpec(shape, lambda i: index)
    whole = lambda *shape: at(shape, *(0,) * len(shape))
    any_ = pl.BlockSpec(memory_space=pl.ANY)
    shapes = [(10, 64, 128), (32, 256), (8, 256), (32, 256), (32, 256), (8, 256), (8, 256)]
    dma = pltpu.SemaphoreType.DMA
    vm = lambda *shape, t=F32: pltpu.VMEM(shape, t)
    plane, column = (1, 32, 256), (8, 8, 256)
    return pl.pallas_call(
        exchange_kernel,
        grid=(1,),
        out_shape=[jax.ShapeDtypeStruct(s, F32) for s in shapes + [(27, 8, 32, 256)]],
        in_specs=[
            whole(9, 4096), whole(1, 4096), whole(1, 4096),
            at(plane, 7, 0, 0), at(plane, 7, 0, 0), at(plane, 0, 0, 0),
            at(column, 0, 3, 0), at(column, 0, 3, 0), at(column, 0, 0, 0),
            any_, any_, any_,
        ],
        out_specs=[whole(*s) for s in shapes] + [any_],
        scratch_shapes=[
            vm(640, 128), vm(2048, 256, t=BF16), vm(1, 4096, t=I32), vm(128, 5, 128), vm(128, 5, 128),
            vm(12, 32, 256), vm(24, 8, 256), vm(24, 256), vm(8, 256),
            vm(24, 32, 256), vm(24, 8, 256), vm(24, 256), vm(32, 256), vm(8, 256),
            vm(9, 8, 32, 256), vm(3, 8, 8, 32, 256, t=BF16), vm(8, 32, 256), vm(27, 8, 32, 256),
            vm(2, 4, 9, 32, 256), vm(2, 32, 256), vm(3, 4, 32, 256), vm(3, 4, 32, 256),
            dma((9,)), dma((9,)), dma, dma, dma, dma((3,)), dma((8,)),
        ],
        compiler_params=pltpu.CompilerParams(has_side_effects=True, collective_id=0),
        name="exchange",
    )(loads, dest.reshape(1, 4096), cell.reshape(1, 4096), sa, k, k, st, k, k, fields, areas, volume)


def local(fields, volume, swept_axial, swept_angular, swept_radial, conductivity, corner_areas, parcel_loads, dest_device, dest_cell):
    chan, saz, stt, kzl, kzh, ktl, kth, grads = exchange(
        parcel_loads, dest_device, dest_cell, fields, corner_areas, volume, swept_axial, swept_angular, conductivity
    )
    vn, src, tlo, thi, grads = deposit(
        chan, fields, volume, swept_axial, swept_angular, swept_radial, saz, stt, grads
    )
    diffused = diffuse(src, tlo, thi, conductivity, vn, kzl, kzh, ktl, kth)
    return vn, diffused, grads


def solution(mesh):
    P = jax.sharding.PartitionSpec
    cells = P("slab", "sector", None)
    in_specs = (
        P(None, "slab", "sector", None), cells, cells, cells, cells, cells,
        P(None, None, "slab", "sector", None), P(None, ("slab", "sector")), P(("slab", "sector"), None), P(("slab", "sector")),
    )
    out_specs = (cells, P(None, "slab", "sector", None), P(None, "slab", "sector", None))
    return jax.shard_map(local, mesh=mesh, in_specs=in_specs, out_specs=out_specs, check_vma=False)
```

```python
import jax
import jax.numpy as jnp
from jax import lax
from jax.experimental import pallas as pl
from jax.experimental.pallas import tpu as pltpu

F32, BF16, I32 = jnp.float32, jnp.bfloat16, jnp.int32
VM = pl.BlockSpec(memory_space=pltpu.VMEM)


def nt(a, b):
    return lax.dot_general(a, b, (((1,), (1,)), ((), ())), preferred_element_type=F32)


def iota(shape, dim):
    return lax.broadcasted_iota(I32, shape, dim)


def one_hot(row, count):
    n = row.shape[1]
    return jnp.where(iota((count, n), 0) == row, 1.0, 0.0).astype(BF16)


def split(x):
    hi = x.astype(BF16)
    return hi, (x - hi.astype(F32)).astype(BF16)


def before(n):
    return jnp.where(iota((n, n), 0) < iota((n, n), 1), 1.0, 0.0).astype(BF16)


GROUPS, ROWS, SLOTS, CHUNK = 16, 16, 256, 2048


def deposit_kernel(
    chan_ref, fields_ref, vol_ref, sa_ref, st_ref, sr_ref, saz_ref, stt_ref, grads_ref,
    vn_ref, vn2_ref, src_ref, tlo_ref, thi_ref, grads_out_ref,
    sort_ref, acc_ref, rank_ref, sem,
):
    leaving = pltpu.make_async_copy(grads_ref, grads_out_ref, sem)
    leaving.start()
    for a in range(8):
        below = saz_ref[...] if a == 0 else sa_ref[a - 1]
        stp = st_ref[a]
        row = iota((32, 256), 0)
        side = jnp.where(row == 0, stt_ref[a : a + 1], pltpu.roll(stp, 1, 0))
        srp = sr_ref[a]
        lane = iota((32, 256), 1)
        inner = jnp.where(lane == 0, 0.0, pltpu.roll(srp, 1, 1))
        vn = vol_ref[a] + sa_ref[a] - below + stp - side + srp - inner
        vn_ref[a] = vn
        vn2_ref[a] = vn
    acc_ref[...] = jnp.zeros_like(acc_ref)
    earlier = before(256)

    def rows_of(c, start, count):
        part = chan_ref[c, start : start + count, :]
        return jnp.concatenate([part[i : i + 1] for i in range(count)], 1)

    for ch in range(8192 // CHUNK):
        nrow = CHUNK // 128
        carry = jnp.zeros((GROUPS, 1), F32)
        cell = rows_of(9, ch * nrow, nrow).astype(I32) - 1
        group = lax.shift_right_arithmetic(cell, 12)
        g = one_hot(group, GROUPS)
        gf = g.astype(F32)
        ranks = []
        for b in range(CHUNK // 256):
            gb = gf[:, b * 256 : (b + 1) * 256]
            count = jnp.dot(g[:, b * 256 : (b + 1) * 256], earlier, preferred_element_type=F32)
            ranks.append(jnp.sum(gb * (count + carry) , axis=0, keepdims=True))
            carry = carry + jnp.sum(gb, axis=1, keepdims=True)
        rank_ref[...] = jnp.concatenate(ranks, 1).astype(I32)
        most = jnp.max(carry).astype(I32)
        his, los = [], []
        for c in range(9):
            hi, lo = split(rows_of(c, ch * nrow, nrow))
            his.append(hi * g)
            los.append(lo * g)
        rowin = (lax.shift_right_logical(cell, 8) & 15).astype(F32).astype(BF16)
        colin = (cell & 255).astype(F32).astype(BF16)
        lhs = jnp.concatenate(his + los + [(rowin + 1.0) * g, colin * g], 0)

        def one_round(r, carry_unused):
            o = one_hot(rank_ref[...] - r * SLOTS, SLOTS)
            sort_ref[...] = nt(lhs, o)
            for gi in range(GROUPS):
                pick = lambda c: sort_ref[c * GROUPS + gi : c * GROUPS + gi + 1, :]
                rm = one_hot(pick(18).astype(I32) - 1, ROWS)
                j = one_hot(pick(19).astype(I32), 256)
                left = jnp.concatenate([pick(c).astype(BF16) * rm for c in range(18)], 0)
                out = nt(left, j)
                for f in range(9):
                    acc_ref[f, gi // 2, (gi % 2) * 16 : (gi % 2) * 16 + 16, :] += (
                        out[f * 16 : f * 16 + 16] + out[(9 + f) * 16 : (9 + f) * 16 + 16]
                    )
            return carry_unused

        lax.fori_loop(0, (most + SLOTS - 1) // SLOTS, one_round, 0)
    for a in range(8):
        inv = 1.0 / vn2_ref[a]
        for f in range(9):
            v = fields_ref[f, a] + acc_ref[f, a] * inv
            src_ref[f, a] = v
            tlo_ref[f, a : a + 1, :] = v[0:1]
            thi_ref[f, a : a + 1, :] = v[31:32]
    leaving.wait()


def deposit(chan, fields, volume, sa, st, sr, saz, stt, grads):
    sd = jax.ShapeDtypeStruct
    return pl.pallas_call(
        deposit_kernel,
        out_shape=(
            sd((8, 32, 256), F32), sd((8, 32, 256), F32), sd((9, 8, 32, 256), F32),
            sd((9, 8, 256), F32), sd((9, 8, 256), F32),
            sd((27, 8, 32, 256), F32),
        ),
        in_specs=[VM] * 8 + [pl.BlockSpec(memory_space=pl.ANY)],
        out_specs=[VM] * 5 + [pl.BlockSpec(memory_space=pl.ANY)],
        scratch_shapes=[
            pltpu.VMEM((320, 256), F32),
            pltpu.VMEM((9, 8, 32, 256), F32),
            pltpu.VMEM((1, CHUNK), I32),
            pltpu.SemaphoreType.DMA,
        ],
        compiler_params=pltpu.CompilerParams(vmem_limit_bytes=24 << 20),
        name="deposit",
    )(chan, fields, volume, sa, st, sr, saz, stt, grads)


def t_shift(x, edge):
    return jnp.where(iota(x.shape, 0) == 0, edge, pltpu.roll(x, 1, 0))


def r_shift(x):
    n = x.shape[1]
    return jnp.where(iota(x.shape, 1) == n - 1, 0.0, pltpu.roll(x, n - 1, 1))


def prepare(f_ref, w_ref, slot, field, vol, edge):
    for f in range(9):
        x = field(f)
        xt = t_shift(x, edge(f))
        f_ref[slot, 0, f] = r_shift(x)
        f_ref[slot, 1, f] = x
        f_ref[slot, 2, f] = r_shift(xt)
        f_ref[slot, 3, f] = xt
    v = vol * 0.125
    v = v + t_shift(v, edge(21) * 0.125)
    w_ref[slot] = v + r_shift(v)


def prepare_areas(a_ref, area, edge):
    for i in range(3):
        for q in range(4):
            x = area(i, q)
            if q // 2 == 1:
                x = t_shift(x, edge(i, q))
            a_ref[i, q] = x if q % 2 == 1 else pltpu.roll(x, 255, 1)


def gradient_plane(f_ref, w_ref, a0_ref, a1_ref, now, prev, out_ref, a):
    def part(n, unused):
        i = lax.rem(n, 3)
        rows = pl.ds(pl.multiple_of(n // 3 * 8, 8), 8)
        inv = 1.0 / (w_ref[now, rows] + w_ref[prev, rows])
        acc = [None] * 9
        for dz in range(2):
            for q in range(4):
                area = (a1_ref if dz else a0_ref)[i, q, rows]
                for f in range(9):
                    term = area * f_ref[prev if dz else now, q, f, rows]
                    acc[f] = term if dz + q == 0 else acc[f] + term
        for f in range(9):
            out_ref[9 * i + f, a, rows] = acc[f] * inv
        return unused

    lax.fori_loop(0, 12, part, 0)


def diffuse_kernel(
    src_ref, tlo_ref, thi_ref, k_ref, vn_ref, kzl_ref, kzh_ref, ktl_ref, kth_ref, out_ref,
    zlo, zhi, tlo, thi, w_ref, send_sems, recv_sems,
):
    slab, sector = lax.axis_index("slab"), lax.axis_index("sector")
    above = (lax.rem(slab + 1, 32), sector)
    below = (lax.rem(slab + 31, 32), sector)
    ahead = (slab, lax.rem(sector + 1, 4))
    behind = (slab, lax.rem(sector + 3, 4))
    barrier = pltpu.get_barrier_semaphore()
    for to in (above, below, ahead, behind):
        pl.semaphore_signal(barrier, inc=1, device_id=to, device_id_type=pl.DeviceIdType.MESH)
    halo = [
        (thi_ref, tlo, ahead), (tlo_ref, thi, behind),
        (src_ref.at[:, 7], zlo, above), (src_ref.at[:, 0], zhi, below),
    ]
    copies = [
        pltpu.make_async_remote_copy(
            src_ref=s, dst_ref=t, send_sem=send_sems.at[n], recv_sem=recv_sems.at[n],
            device_id=to, device_id_type=pl.DeviceIdType.MESH,
        )
        for n, (s, t, to) in enumerate(halo)
    ]
    pl.semaphore_wait(barrier, 4)
    for copy in copies:
        copy.start()
    row = iota((32, 256), 0)
    lane = iota((32, 256), 1)
    for a in range(8):
        k = k_ref[a]
        near = [
            kzl_ref[...] if a == 0 else k_ref[a - 1],
            kzh_ref[...] if a == 7 else k_ref[a + 1],
            jnp.where(row == 0, ktl_ref[a : a + 1], pltpu.roll(k, 1, 0)),
            jnp.where(row == 31, kth_ref[a : a + 1], pltpu.roll(k, 31, 0)),
            jnp.where(lane == 0, 0.0, pltpu.roll(k, 1, 1)),
            jnp.where(lane == 255, 0.0, pltpu.roll(k, 255, 1)),
        ]
        scale = (0.2 * k) / vn_ref[a]
        total = None
        for n, kn in enumerate(near):
            w = scale * kn / (k + kn)
            w_ref[n, a] = w
            total = w if total is None else total + w
        w_ref[6, a] = 1.0 - total
    copies[0].wait()
    copies[1].wait()

    def plane(f, a, under, over):
        s = src_ref[f, a]
        near = [
            under, over,
            jnp.where(row == 0, tlo[f, a : a + 1], pltpu.roll(s, 1, 0)),
            jnp.where(row == 31, thi[f, a : a + 1], pltpu.roll(s, 31, 0)),
            pltpu.roll(s, 1, 1),
            pltpu.roll(s, 255, 1),
        ]
        out = w_ref[6, a] * s
        for n in range(6):
            out = out + w_ref[n, a] * near[n]
        out_ref[f, a] = out

    def inner(f, unused):
        for a in range(1, 7):
            plane(f, a, src_ref[f, a - 1], src_ref[f, a + 1])
        return unused

    lax.fori_loop(0, 9, inner, 0)
    copies[2].wait()
    copies[3].wait()

    def ends(f, unused):
        plane(f, 0, zlo[f], src_ref[f, 1])
        plane(f, 7, src_ref[f, 6], zhi[f])
        return unused

    lax.fori_loop(0, 9, ends, 0)


def diffuse(src, tlo, thi, k, vn, kzl, kzh, ktl, kth):
    dma = pltpu.SemaphoreType.DMA
    cells = (9, 8, 32, 256)
    return pl.pallas_call(
        diffuse_kernel,
        out_shape=jax.ShapeDtypeStruct(cells, F32),
        in_specs=[VM] * 9,
        out_specs=VM,
        scratch_shapes=[
            pltpu.VMEM((9, 32, 256), F32), pltpu.VMEM((9, 32, 256), F32),
            pltpu.VMEM((9, 8, 256), F32), pltpu.VMEM((9, 8, 256), F32),
            pltpu.VMEM((7, 8, 32, 256), F32), dma((4,)), dma((4,)),
        ],
        compiler_params=pltpu.CompilerParams(has_side_effects=True, collective_id=1, vmem_limit_bytes=16 << 20),
        name="diffuse",
    )(src, tlo, thi, k, vn, kzl, kzh, ktl, kth)


def exchange_kernel(
    loads_in, dest_in, cell_in, fields_in, areas_in, vol_in, sa_in, st_in, k_in,
    chan_ref, saz_ref, stt_ref, kzl_ref, kzh_ref, ktl_ref, kth_ref, grads_ref,
    acc_ref, d_ref, rank_ref, out_buf, in_buf, azs, ts, cs, kbs, zr, tr, cr, kar, knr,
    loads_ref, dest_ref, cell_ref, sz_ref, kz_ref, kz0_ref, st_ref, kt_ref, kt0_ref,
    fbuf, abuf, vbuf, f_ref, w_ref, a0_ref, a1_ref,
    send_sems, recv_sems, psend_sem, precv_sem, own_sem, load_sems,
):
    slab, sector = lax.axis_index("slab"), lax.axis_index("sector")
    me = slab * 4 + sector
    barrier = pltpu.get_barrier_semaphore()
    loading = [
        pltpu.make_async_copy(s, t, load_sems.at[n])
        for n, (s, t) in enumerate((
            (dest_in, dest_ref), (loads_in, loads_ref), (cell_in, cell_ref),
            (fields_in, fbuf), (areas_in, abuf), (vol_in, vbuf),
            (sa_in.at[7], sz_ref), (k_in.at[7], kz_ref), (k_in.at[0], kz0_ref),
            (st_in.at[:, 24:32], st_ref), (k_in.at[:, 24:32], kt_ref), (k_in.at[:, 0:8], kt0_ref),
        ))
    ]
    for copy in loading:
        copy.start()

    def greet(k, unused):
        to = lax.rem(me + k, 128)
        pl.semaphore_signal(barrier, inc=1, device_id=(to // 4, lax.rem(to, 4)), device_id_type=pl.DeviceIdType.MESH)
        return unused

    lax.fori_loop(1, 128, greet, 0)

    loading[0].wait()
    blk, devices = 256, 128
    earlier = before(blk)
    carry = jnp.zeros((devices, 1), F32)
    count = 4096 // blk
    for b in range(count):
        d_ref[b * 128 : (b + 1) * 128, :] = one_hot(dest_ref[:, b * blk : (b + 1) * blk], devices)
    counts = jnp.dot(d_ref[...], earlier, preferred_element_type=F32)
    for b in range(count):
        df = d_ref[b * 128 : (b + 1) * 128, :].astype(F32)
        rank_ref[:, b * blk : (b + 1) * blk] = jnp.sum(
            df * (counts[b * 128 : (b + 1) * 128] + carry), axis=0, keepdims=True
        ).astype(I32)
        carry = carry + jnp.sum(df, axis=1, keepdims=True)

    for copy in loading[1:]:
        copy.wait()
    for n in range(12):
        x = abuf[n // 4, 4 + n % 4, 7].astype(F32)
        azs[n] = x
        cs[9 + n : 10 + n] = x[31:32]
        for a in range(8):
            ts[9 + n, a : a + 1, :] = abuf[n // 4, (2, 3, 6, 7)[n % 4], a].astype(F32)[31:32]
    for f in range(9):
        ts[f] = fbuf[f, :, 31, :]
        cs[f : f + 1] = fbuf[f, 7, 31:32]
    ts[21] = vbuf[:, 31, :]
    cs[21:22] = vbuf[7, 31:32]
    for n, (t_ref, z_ref) in enumerate(((st_ref, sz_ref), (kt_ref, kz_ref))):
        ts[22 + n] = t_ref[:, 7, :]
        cs[22 + n : 23 + n] = z_ref[31:32]
    kbs[...] = kt0_ref[:, 0, :]

    above = (lax.rem(slab + 1, 32), sector)
    below = (lax.rem(slab + 31, 32), sector)
    ahead = (slab, lax.rem(sector + 1, 4))
    behind = (slab, lax.rem(sector + 3, 4))
    across = (lax.rem(slab + 1, 32), lax.rem(sector + 1, 4))
    halo = [
        (sz_ref, zr.at[22], above),
        (kz_ref, zr.at[23], above),
        (kz0_ref, kar, below),
        (kbs, knr, behind),
        (ts, tr, ahead),
        (cs, cr, across),
        (vbuf.at[7], zr.at[21], above),
        (fbuf.at[:, 7], zr.at[0:9], above),
        (azs, zr.at[9:21], above),
    ]
    copies = [
        pltpu.make_async_remote_copy(
            src_ref=s, dst_ref=t, send_sem=send_sems.at[n], recv_sem=recv_sems.at[n],
            device_id=to, device_id_type=pl.DeviceIdType.MESH,
        )
        for n, (s, t, to) in enumerate(halo)
    ]
    acc_ref[...] = jnp.zeros_like(acc_ref)
    part = 512
    for b in range(4096 // part):
        sl = pl.ds(b * part, part)
        rank = rank_ref[:, sl]
        o = one_hot(rank & 31, 32)
        hi, lo = split(loads_ref[:, sl])
        cell = cell_ref[:, sl]
        row = (lax.shift_right_logical(cell, 8) * 256).astype(F32).astype(BF16)
        col = ((cell & 255) + 1).astype(F32).astype(BF16)
        his = jnp.concatenate([hi[c : c + 1] * o for c in range(9)] + [row * o], 0)
        los = jnp.concatenate([lo[c : c + 1] * o for c in range(9)] + [col * o], 0)
        d = one_hot(dest_ref[:, sl] + lax.shift_right_logical(rank, 5) * 128, 256)
        acc_ref[...] += nt(jnp.concatenate([his, los], 1), jnp.concatenate([d, d], 1))
    for s in range(5):
        block = jnp.concatenate(
            [acc_ref[c * 32 : (c + 1) * 32, h * 128 : (h + 1) * 128] for c in (2 * s, 2 * s + 1) for h in range(2)], 0
        )
        out_buf[:, s, :] = block.T
    pl.semaphore_wait(barrier, 127)
    for copy in copies:
        copy.start()
    own = pltpu.make_async_copy(out_buf.at[me], in_buf.at[me], own_sem)
    own.start()

    def send(k, unused):
        to = lax.rem(me + k, 128)
        pltpu.make_async_remote_copy(
            src_ref=out_buf.at[to], dst_ref=in_buf.at[me], send_sem=psend_sem, recv_sem=precv_sem,
            device_id=(to // 4, lax.rem(to, 4)), device_id_type=pl.DeviceIdType.MESH,
        ).start()
        return unused

    lax.fori_loop(1, 128, send, 0)
    copies[4].wait()

    def beside(plane):
        return lambda c: tr[c, pl.ds(plane, 1), :]

    def prepare_own(slot, plane):
        prepare(f_ref, w_ref, slot, lambda f: fbuf[f, plane], vbuf[plane], beside(plane))

    def own_areas(ref, plane, dz):
        prepare_areas(
            ref, lambda i, q: abuf[i, 4 * dz + q, plane].astype(F32),
            lambda i, q: beside(plane)(9 + 4 * i + 2 * dz + q % 2),
        )

    prepare_own(1, 7)

    def plane(n, unused):
        a = 7 - n
        now = lax.rem(a, 2)
        prepare_own(1 - now, a - 1)
        own_areas(a0_ref, a, 0)
        own_areas(a1_ref, a - 1, 1)
        gradient_plane(f_ref, w_ref, a0_ref, a1_ref, now, 1 - now, grads_ref, a)
        return unused

    lax.fori_loop(0, 7, plane, 0)
    own.wait()
    for n, copy in enumerate(copies):
        if n != 4:
            copy.wait()
    inside = slab > 0

    def under(x):
        return jnp.where(inside, x, 0.0)

    prepare(f_ref, w_ref, 1, lambda f: under(zr[f]), under(zr[21]), lambda c: under(cr[c : c + 1, :]))
    own_areas(a0_ref, 0, 0)
    prepare_areas(a1_ref, lambda i, q: zr[9 + 4 * i + q], lambda i, q: cr[9 + 4 * i + q : 10 + 4 * i + q, :])
    gradient_plane(f_ref, w_ref, a0_ref, a1_ref, 0, 1, grads_ref, 0)
    saz_ref[...] = under(zr[22])
    kzl_ref[...] = under(zr[23])
    kzh_ref[...] = jnp.where(slab < 31, kar[...], 0.0)
    stt_ref[...] = tr[22]
    ktl_ref[...] = tr[23]
    kth_ref[...] = knr[...]
    most = pl.ds(0, 127)
    pltpu.make_async_copy(out_buf.at[most], in_buf.at[most], psend_sem).wait()
    pltpu.make_async_copy(out_buf.at[most], in_buf.at[most], precv_sem).wait()
    lane = iota((64, 128), 1) < 64
    for s in range(5):
        first, second = in_buf[0:64, s, :], in_buf[64:128, s, :]
        chan_ref[2 * s] = jnp.where(lane, first, pltpu.roll(second, 64, 1))
        chan_ref[2 * s + 1] = jnp.where(lane, pltpu.roll(first, 64, 1), second)


def exchange(loads, dest, cell, fields, areas, volume, sa, st, k):
    hbm = pl.BlockSpec(memory_space=pltpu.HBM)
    shapes = [(10, 64, 128), (32, 256), (8, 256), (32, 256), (32, 256), (8, 256), (8, 256), (27, 8, 32, 256)]
    dma = pltpu.SemaphoreType.DMA
    vm = lambda *shape, t=F32: pltpu.VMEM(shape, t)
    return pl.pallas_call(
        exchange_kernel,
        out_shape=[jax.ShapeDtypeStruct(s, F32) for s in shapes],
        in_specs=[hbm] * 9,
        out_specs=[VM] * 8,
        scratch_shapes=[
            vm(320, 256), vm(2048, 256, t=BF16), vm(1, 4096, t=I32), vm(128, 5, 128), vm(128, 5, 128),
            vm(12, 32, 256), vm(24, 8, 256), vm(24, 256), vm(8, 256),
            vm(24, 32, 256), vm(24, 8, 256), vm(24, 256), vm(32, 256), vm(8, 256),
            vm(9, 4096), vm(1, 4096, t=I32), vm(1, 4096, t=I32), vm(32, 256), vm(32, 256), vm(32, 256),
            vm(8, 8, 256), vm(8, 8, 256), vm(8, 8, 256),
            vm(9, 8, 32, 256), vm(3, 8, 8, 32, 256, t=BF16), vm(8, 32, 256),
            vm(2, 4, 9, 32, 256), vm(2, 32, 256), vm(3, 4, 32, 256), vm(3, 4, 32, 256),
            dma((9,)), dma((9,)), dma, dma, dma, dma((12,)),
        ],
        compiler_params=pltpu.CompilerParams(has_side_effects=True, collective_id=0, vmem_limit_bytes=40 << 20),
        name="exchange",
    )(loads, dest.reshape(1, 4096), cell.reshape(1, 4096), fields, areas, volume, sa, st, k)


def local(fields, volume, swept_axial, swept_angular, swept_radial, conductivity, corner_areas, parcel_loads, dest_device, dest_cell):
    chan, saz, stt, kzl, kzh, ktl, kth, grads = exchange(
        parcel_loads, dest_device, dest_cell, fields, corner_areas, volume, swept_axial, swept_angular, conductivity
    )
    vn, vn2, src, tlo, thi, grads = deposit(
        chan, fields, volume, swept_axial, swept_angular, swept_radial, saz, stt, grads
    )
    diffused = diffuse(src, tlo, thi, conductivity, vn2, kzl, kzh, ktl, kth)
    return vn, diffused, grads


def solution(mesh):
    P = jax.sharding.PartitionSpec
    cells = P("slab", "sector", None)
    in_specs = (
        P(None, "slab", "sector", None), cells, cells, cells, cells, cells,
        P(None, None, "slab", "sector", None), P(None, ("slab", "sector")), P(("slab", "sector"), None), P(("slab", "sector")),
    )
    out_specs = (cells, P(None, "slab", "sector", None), P(None, "slab", "sector", None))
    return jax.shard_map(local, mesh=mesh, in_specs=in_specs, out_specs=out_specs, check_vma=False)
```

```python
import jax
import jax.numpy as jnp
from jax import lax
from jax.experimental import pallas as pl
from jax.experimental.pallas import tpu as pltpu

F32, BF16, I32 = jnp.float32, jnp.bfloat16, jnp.int32
VM = pl.BlockSpec(memory_space=pltpu.VMEM)


def nt(a, b):
    return lax.dot_general(a, b, (((1,), (1,)), ((), ())), preferred_element_type=F32)


def iota(shape, dim):
    return lax.broadcasted_iota(I32, shape, dim)


def one_hot(row, count):
    n = row.shape[1]
    return jnp.where(iota((count, n), 0) == row, 1.0, 0.0).astype(BF16)


def split(x):
    hi = x.astype(BF16)
    return hi, (x - hi.astype(F32)).astype(BF16)


def before(n):
    return jnp.where(iota((n, n), 0) < iota((n, n), 1), 1.0, 0.0).astype(BF16)


GROUPS, ROWS, SLOTS, CHUNK = 16, 16, 256, 2048


def deposit_kernel(
    chan_ref, fields_ref, vol_ref, sa_ref, st_ref, sr_ref, grads_ref,
    vn_ref, vn2_ref, src_ref, tlo_ref, thi_ref, grads_out_ref,
    sort_ref, acc_ref, rank_ref, gbuf, sems,
):
    arriving = pltpu.make_async_copy(grads_ref, gbuf, sems.at[0])
    leaving = pltpu.make_async_copy(gbuf, grads_out_ref, sems.at[1])
    arriving.start()
    beneath = jnp.concatenate([chan_ref[10, 0:32], chan_ref[10, 32:64]], 1)
    aside = jnp.concatenate([chan_ref[11, 0:8], chan_ref[11, 8:16]], 1)
    for a in range(8):
        below = beneath if a == 0 else sa_ref[a - 1]
        stp = st_ref[a]
        row = iota((32, 256), 0)
        side = jnp.where(row == 0, aside[a : a + 1], pltpu.roll(stp, 1, 0))
        srp = sr_ref[a]
        lane = iota((32, 256), 1)
        inner = jnp.where(lane == 0, 0.0, pltpu.roll(srp, 1, 1))
        vn = vol_ref[a] + sa_ref[a] - below + stp - side + srp - inner
        vn_ref[a] = vn
        vn2_ref[a] = vn
    acc_ref[...] = jnp.zeros_like(acc_ref)
    earlier = before(256)

    def rows_of(c, start, count):
        part = chan_ref[c, start : start + count, :]
        return jnp.concatenate([part[i : i + 1] for i in range(count)], 1)

    for ch in range(8192 // CHUNK):
        nrow = CHUNK // 128
        carry = jnp.zeros((GROUPS, 1), F32)
        cell = rows_of(9, ch * nrow, nrow).astype(I32) - 1
        group = lax.shift_right_arithmetic(cell, 12)
        g = one_hot(group, GROUPS)
        gf = g.astype(F32)
        ranks = []
        for b in range(CHUNK // 256):
            gb = gf[:, b * 256 : (b + 1) * 256]
            count = jnp.dot(g[:, b * 256 : (b + 1) * 256], earlier, preferred_element_type=F32)
            ranks.append(jnp.sum(gb * (count + carry) , axis=0, keepdims=True))
            carry = carry + jnp.sum(gb, axis=1, keepdims=True)
        if ch == 1:
            arriving.wait()
            leaving.start()
        rank_ref[...] = jnp.concatenate(ranks, 1).astype(I32)
        most = jnp.max(carry).astype(I32)
        his, los = [], []
        for c in range(9):
            hi, lo = split(rows_of(c, ch * nrow, nrow))
            his.append(hi * g)
            los.append(lo * g)
        rowin = (lax.shift_right_logical(cell, 8) & 15).astype(F32).astype(BF16)
        colin = (cell & 255).astype(F32).astype(BF16)
        lhs = jnp.concatenate(his + los + [(rowin + 1.0) * g, colin * g], 0)

        def one_round(r, carry_unused):
            o = one_hot(rank_ref[...] - r * SLOTS, SLOTS)
            sort_ref[...] = nt(lhs, o)
            for gi in range(GROUPS):
                pick = lambda c: sort_ref[c * GROUPS + gi : c * GROUPS + gi + 1, :]
                rm = one_hot(pick(18).astype(I32) - 1, ROWS)
                j = one_hot(pick(19).astype(I32), 256)
                left = jnp.concatenate([pick(c).astype(BF16) * rm for c in range(18)], 0)
                out = nt(left, j)
                for f in range(9):
                    acc_ref[f, gi // 2, (gi % 2) * 16 : (gi % 2) * 16 + 16, :] += (
                        out[f * 16 : f * 16 + 16] + out[(9 + f) * 16 : (9 + f) * 16 + 16]
                    )
            return carry_unused

        lax.fori_loop(0, (most + SLOTS - 1) // SLOTS, one_round, 0)
    for a in range(8):
        inv = 1.0 / vn2_ref[a]
        for f in range(9):
            v = fields_ref[f, a] + acc_ref[f, a] * inv
            src_ref[f, a] = v
            tlo_ref[f, a : a + 1, :] = v[0:1]
            thi_ref[f, a : a + 1, :] = v[31:32]
    leaving.wait()


def deposit(chan, fields, volume, sa, st, sr, grads):
    sd = jax.ShapeDtypeStruct
    return pl.pallas_call(
        deposit_kernel,
        out_shape=(
            sd((8, 32, 256), F32), sd((8, 32, 256), F32), sd((9, 8, 32, 256), F32),
            sd((9, 8, 256), F32), sd((9, 8, 256), F32),
            sd((27, 8, 32, 256), F32),
        ),
        in_specs=[VM] * 6 + [pl.BlockSpec(memory_space=pl.ANY)],
        out_specs=[VM] * 5 + [pl.BlockSpec(memory_space=pl.ANY)],
        scratch_shapes=[
            pltpu.VMEM((320, 256), F32),
            pltpu.VMEM((9, 8, 32, 256), F32),
            pltpu.VMEM((1, CHUNK), I32),
            pltpu.VMEM((27, 8, 32, 256), F32),
            pltpu.SemaphoreType.DMA((2,)),
        ],
        compiler_params=pltpu.CompilerParams(vmem_limit_bytes=44 << 20),
        name="deposit",
    )(chan, fields, volume, sa, st, sr, grads)


def t_shift(x, edge):
    return jnp.where(iota(x.shape, 0) == 0, edge, pltpu.roll(x, 1, 0))


def r_shift(x):
    n = x.shape[1]
    return jnp.where(iota(x.shape, 1) == n - 1, 0.0, pltpu.roll(x, n - 1, 1))


def prepare(f_ref, w_ref, slot, field, vol, edge):
    for f in range(9):
        x = field(f)
        xt = t_shift(x, edge(f))
        f_ref[slot, 0, f] = r_shift(x)
        f_ref[slot, 1, f] = x
        f_ref[slot, 2, f] = r_shift(xt)
        f_ref[slot, 3, f] = xt
    v = vol * 0.125
    v = v + t_shift(v, edge(21) * 0.125)
    w_ref[slot] = v + r_shift(v)


def prepare_areas(a_ref, area, edge):
    for i in range(3):
        for q in range(4):
            x = area(i, q)
            if q // 2 == 1:
                x = t_shift(x, edge(i, q))
            a_ref[i, q] = x if q % 2 == 1 else pltpu.roll(x, 255, 1)


def gradient_plane(f_ref, w_ref, a0_ref, a1_ref, now, prev, out_ref, a):
    def part(n, unused):
        i = lax.rem(n, 3)
        rows = pl.ds(pl.multiple_of(n // 3 * 8, 8), 8)
        inv = 1.0 / (w_ref[now, rows] + w_ref[prev, rows])
        acc = [None] * 9
        for dz in range(2):
            for q in range(4):
                area = (a1_ref if dz else a0_ref)[i, q, rows]
                for f in range(9):
                    term = area * f_ref[prev if dz else now, q, f, rows]
                    acc[f] = term if dz + q == 0 else acc[f] + term
        for f in range(9):
            out_ref[9 * i + f, a, rows] = acc[f] * inv
        return unused

    lax.fori_loop(0, 12, part, 0)


def diffuse_kernel(
    src_ref, tlo_ref, thi_ref, k_ref, vn_ref, kzl_ref, kzh_ref, ktl_ref, kth_ref, out_ref,
    zlo, zhi, tlo, thi, w_ref, send_sems, recv_sems,
):
    slab, sector = lax.axis_index("slab"), lax.axis_index("sector")
    above = (lax.rem(slab + 1, 32), sector)
    below = (lax.rem(slab + 31, 32), sector)
    ahead = (slab, lax.rem(sector + 1, 4))
    behind = (slab, lax.rem(sector + 3, 4))
    barrier = pltpu.get_barrier_semaphore()
    for to in (above, below, ahead, behind):
        pl.semaphore_signal(barrier, inc=1, device_id=to, device_id_type=pl.DeviceIdType.MESH)
    halo = [
        (thi_ref, tlo, ahead), (tlo_ref, thi, behind),
        (src_ref.at[:, 7], zlo, above), (src_ref.at[:, 0], zhi, below),
    ]
    copies = [
        pltpu.make_async_remote_copy(
            src_ref=s, dst_ref=t, send_sem=send_sems.at[n], recv_sem=recv_sems.at[n],
            device_id=to, device_id_type=pl.DeviceIdType.MESH,
        )
        for n, (s, t, to) in enumerate(halo)
    ]
    pl.semaphore_wait(barrier, 4)
    for copy in copies:
        copy.start()
    row = iota((32, 256), 0)
    lane = iota((32, 256), 1)
    for a in range(8):
        k = k_ref[a]
        near = [
            kzl_ref[...] if a == 0 else k_ref[a - 1],
            kzh_ref[...] if a == 7 else k_ref[a + 1],
            jnp.where(row == 0, ktl_ref[a : a + 1], pltpu.roll(k, 1, 0)),
            jnp.where(row == 31, kth_ref[a : a + 1], pltpu.roll(k, 31, 0)),
            jnp.where(lane == 0, 0.0, pltpu.roll(k, 1, 1)),
            jnp.where(lane == 255, 0.0, pltpu.roll(k, 255, 1)),
        ]
        scale = (0.2 * k) / vn_ref[a]
        total = None
        for n, kn in enumerate(near):
            w = scale * kn / (k + kn)
            w_ref[n, a] = w
            total = w if total is None else total + w
        w_ref[6, a] = 1.0 - total
    copies[0].wait()
    copies[1].wait()

    def plane(f, a, under, over):
        s = src_ref[f, a]
        near = [
            under, over,
            jnp.where(row == 0, tlo[f, a : a + 1], pltpu.roll(s, 1, 0)),
            jnp.where(row == 31, thi[f, a : a + 1], pltpu.roll(s, 31, 0)),
            pltpu.roll(s, 1, 1),
            pltpu.roll(s, 255, 1),
        ]
        out = w_ref[6, a] * s
        for n in range(6):
            out = out + w_ref[n, a] * near[n]
        out_ref[f, a] = out

    def inner(f, unused):
        for a in range(1, 7):
            plane(f, a, src_ref[f, a - 1], src_ref[f, a + 1])
        return unused

    lax.fori_loop(0, 9, inner, 0)
    copies[2].wait()
    copies[3].wait()

    def ends(f, unused):
        plane(f, 0, zlo[f], src_ref[f, 1])
        plane(f, 7, src_ref[f, 6], zhi[f])
        return unused

    lax.fori_loop(0, 9, ends, 0)


def diffuse(src, tlo, thi, k, vn, kzl, kzh, ktl, kth):
    dma = pltpu.SemaphoreType.DMA
    cells = (9, 8, 32, 256)
    return pl.pallas_call(
        diffuse_kernel,
        out_shape=jax.ShapeDtypeStruct(cells, F32),
        in_specs=[VM] * 9,
        out_specs=VM,
        scratch_shapes=[
            pltpu.VMEM((9, 32, 256), F32), pltpu.VMEM((9, 32, 256), F32),
            pltpu.VMEM((9, 8, 256), F32), pltpu.VMEM((9, 8, 256), F32),
            pltpu.VMEM((7, 8, 32, 256), F32), dma((4,)), dma((4,)),
        ],
        compiler_params=pltpu.CompilerParams(has_side_effects=True, collective_id=1, vmem_limit_bytes=16 << 20),
        name="diffuse",
    )(src, tlo, thi, k, vn, kzl, kzh, ktl, kth)


def exchange_kernel(
    loads_in, dest_in, cell_in, fields_in, areas_in, vol_in, sa_in, st_in, k_in,
    chan_ref, kzl_ref, kzh_ref, ktl_ref, kth_ref, grads_ref,
    acc_ref, d_ref, rank_ref, out_buf, in_buf, azs, ts, cs, kbs, zr, tr, cr, kar, knr,
    loads_ref, dest_ref, cell_ref, sz_ref, kz_ref, kz0_ref, st_ref, kt_ref, kt0_ref,
    fbuf, abuf, vbuf, gbuf, f_ref, w_ref, a0_ref, a1_ref,
    send_sems, recv_sems, psend_sem, precv_sem, own_sem, load_sems, store_sems,
):
    slab, sector = lax.axis_index("slab"), lax.axis_index("sector")
    me = slab * 4 + sector
    barrier = pltpu.get_barrier_semaphore()
    loading = [
        pltpu.make_async_copy(s, t, load_sems.at[n])
        for n, (s, t) in enumerate((
            (dest_in, dest_ref), (loads_in, loads_ref), (cell_in, cell_ref),
            (fields_in, fbuf), (areas_in, abuf), (vol_in, vbuf),
            (sa_in.at[7], sz_ref), (k_in.at[7], kz_ref), (k_in.at[0], kz0_ref),
            (st_in.at[:, 24:32], st_ref), (k_in.at[:, 24:32], kt_ref), (k_in.at[:, 0:8], kt0_ref),
        ))
    ]
    for copy in loading:
        copy.start()

    def greet(k, unused):
        to = lax.rem(me + k, 128)
        pl.semaphore_signal(barrier, inc=1, device_id=(to // 4, lax.rem(to, 4)), device_id_type=pl.DeviceIdType.MESH)
        return unused

    lax.fori_loop(1, 128, greet, 0)

    loading[0].wait()
    blk, devices = 256, 128
    earlier = before(blk)
    carry = jnp.zeros((devices, 1), F32)
    count = 4096 // blk
    for b in range(count):
        d_ref[b * 128 : (b + 1) * 128, :] = one_hot(dest_ref[:, b * blk : (b + 1) * blk], devices)
    counts = jnp.dot(d_ref[...], earlier, preferred_element_type=F32)
    for b in range(count):
        df = d_ref[b * 128 : (b + 1) * 128, :].astype(F32)
        rank_ref[:, b * blk : (b + 1) * blk] = jnp.sum(
            df * (counts[b * 128 : (b + 1) * 128] + carry), axis=0, keepdims=True
        ).astype(I32)
        carry = carry + jnp.sum(df, axis=1, keepdims=True)

    for copy in loading[1:]:
        copy.wait()
    for n in range(12):
        x = abuf[n // 4, 4 + n % 4, 7].astype(F32)
        azs[n] = x
        cs[9 + n : 10 + n] = x[31:32]
        for a in range(8):
            ts[9 + n, a : a + 1, :] = abuf[n // 4, (2, 3, 6, 7)[n % 4], a].astype(F32)[31:32]
    for f in range(9):
        ts[f] = fbuf[f, :, 31, :]
        cs[f : f + 1] = fbuf[f, 7, 31:32]
    ts[21] = vbuf[:, 31, :]
    cs[21:22] = vbuf[7, 31:32]
    for n, (t_ref, z_ref) in enumerate(((st_ref, sz_ref), (kt_ref, kz_ref))):
        ts[22 + n] = t_ref[:, 7, :]
        cs[22 + n : 23 + n] = z_ref[31:32]
    kbs[...] = kt0_ref[:, 0, :]

    above = (lax.rem(slab + 1, 32), sector)
    below = (lax.rem(slab + 31, 32), sector)
    ahead = (slab, lax.rem(sector + 1, 4))
    behind = (slab, lax.rem(sector + 3, 4))
    across = (lax.rem(slab + 1, 32), lax.rem(sector + 1, 4))
    halo = [
        (sz_ref, zr.at[22], above),
        (kz_ref, zr.at[23], above),
        (kz0_ref, kar, below),
        (kbs, knr, behind),
        (ts, tr, ahead),
        (cs, cr, across),
        (vbuf.at[7], zr.at[21], above),
        (fbuf.at[:, 7], zr.at[0:9], above),
        (azs, zr.at[9:21], above),
    ]
    copies = [
        pltpu.make_async_remote_copy(
            src_ref=s, dst_ref=t, send_sem=send_sems.at[n], recv_sem=recv_sems.at[n],
            device_id=to, device_id_type=pl.DeviceIdType.MESH,
        )
        for n, (s, t, to) in enumerate(halo)
    ]
    acc_ref[...] = jnp.zeros_like(acc_ref)
    part = 512
    for b in range(4096 // part):
        sl = pl.ds(b * part, part)
        rank = rank_ref[:, sl]
        o = one_hot(rank & 31, 32)
        hi, lo = split(loads_ref[:, sl])
        cell = cell_ref[:, sl]
        row = (lax.shift_right_logical(cell, 8) * 256).astype(F32).astype(BF16)
        col = ((cell & 255) + 1).astype(F32).astype(BF16)
        his = jnp.concatenate([hi[c : c + 1] * o for c in range(9)] + [row * o], 0)
        los = jnp.concatenate([lo[c : c + 1] * o for c in range(9)] + [col * o], 0)
        d = one_hot(dest_ref[:, sl] + lax.shift_right_logical(rank, 5) * 128, 256)
        acc_ref[...] += nt(jnp.concatenate([his, los], 1), jnp.concatenate([d, d], 1))
    for s in range(5):
        block = jnp.concatenate(
            [acc_ref[c * 32 : (c + 1) * 32, h * 128 : (h + 1) * 128] for c in (2 * s, 2 * s + 1) for h in range(2)], 0
        )
        out_buf[:, s, :] = block.T
    pl.semaphore_wait(barrier, 127)
    for copy in copies:
        copy.start()
    own = pltpu.make_async_copy(out_buf.at[me], in_buf.at[me], own_sem)
    own.start()

    def send(k, unused):
        to = lax.rem(me + k, 128)
        pltpu.make_async_remote_copy(
            src_ref=out_buf.at[to], dst_ref=in_buf.at[me], send_sem=psend_sem, recv_sem=precv_sem,
            device_id=(to // 4, lax.rem(to, 4)), device_id_type=pl.DeviceIdType.MESH,
        ).start()
        return unused

    lax.fori_loop(1, 128, send, 0)
    copies[4].wait()

    def beside(plane):
        return lambda c: tr[c, pl.ds(plane, 1), :]

    def prepare_own(slot, plane):
        prepare(f_ref, w_ref, slot, lambda f: fbuf[f, plane], vbuf[plane], beside(plane))

    def own_areas(ref, plane, dz):
        prepare_areas(
            ref, lambda i, q: abuf[i, 4 * dz + q, plane].astype(F32),
            lambda i, q: beside(plane)(9 + 4 * i + 2 * dz + q % 2),
        )

    def store(a):
        return pltpu.make_async_copy(gbuf.at[:, a], grads_ref.at[:, a], store_sems.at[a])

    prepare_own(1, 7)

    def plane(n, unused):
        a = 7 - n
        now = lax.rem(a, 2)
        prepare_own(1 - now, a - 1)
        own_areas(a0_ref, a, 0)
        own_areas(a1_ref, a - 1, 1)
        gradient_plane(f_ref, w_ref, a0_ref, a1_ref, now, 1 - now, gbuf, a)
        store(a).start()
        return unused

    lax.fori_loop(0, 7, plane, 0)
    own.wait()
    for n, copy in enumerate(copies):
        if n != 4:
            copy.wait()
    inside = slab > 0

    def under(x):
        return jnp.where(inside, x, 0.0)

    prepare(f_ref, w_ref, 1, lambda f: under(zr[f]), under(zr[21]), lambda c: under(cr[c : c + 1, :]))
    own_areas(a0_ref, 0, 0)
    prepare_areas(a1_ref, lambda i, q: zr[9 + 4 * i + q], lambda i, q: cr[9 + 4 * i + q : 10 + 4 * i + q, :])
    gradient_plane(f_ref, w_ref, a0_ref, a1_ref, 0, 1, gbuf, 0)
    store(0).start()
    for h in range(2):
        chan_ref[10, 32 * h : 32 * h + 32] = under(zr[22, :, 128 * h : 128 * h + 128])
        chan_ref[11, 8 * h : 8 * h + 8] = tr[22, :, 128 * h : 128 * h + 128]
    kzl_ref[...] = under(zr[23])
    kzh_ref[...] = jnp.where(slab < 31, kar[...], 0.0)
    ktl_ref[...] = tr[23]
    kth_ref[...] = knr[...]
    most = pl.ds(0, 127)
    pltpu.make_async_copy(out_buf.at[most], in_buf.at[most], psend_sem).wait()
    pltpu.make_async_copy(out_buf.at[most], in_buf.at[most], precv_sem).wait()
    lane = iota((64, 128), 1) < 64
    for s in range(5):
        first, second = in_buf[0:64, s, :], in_buf[64:128, s, :]
        chan_ref[2 * s] = jnp.where(lane, first, pltpu.roll(second, 64, 1))
        chan_ref[2 * s + 1] = jnp.where(lane, pltpu.roll(first, 64, 1), second)
    for a in range(8):
        store(a).wait()


def exchange(loads, dest, cell, fields, areas, volume, sa, st, k):
    hbm = pl.BlockSpec(memory_space=pltpu.HBM)
    shapes = [(12, 64, 128), (32, 256), (32, 256), (8, 256), (8, 256), (27, 8, 32, 256)]
    dma = pltpu.SemaphoreType.DMA
    vm = lambda *shape, t=F32: pltpu.VMEM(shape, t)
    return pl.pallas_call(
        exchange_kernel,
        out_shape=[jax.ShapeDtypeStruct(s, F32) for s in shapes],
        in_specs=[hbm] * 9,
        out_specs=[VM] * 5 + [hbm],
        scratch_shapes=[
            vm(320, 256), vm(2048, 256, t=BF16), vm(1, 4096, t=I32), vm(128, 5, 128), vm(128, 5, 128),
            vm(12, 32, 256), vm(24, 8, 256), vm(24, 256), vm(8, 256),
            vm(24, 32, 256), vm(24, 8, 256), vm(24, 256), vm(32, 256), vm(8, 256),
            vm(9, 4096), vm(1, 4096, t=I32), vm(1, 4096, t=I32), vm(32, 256), vm(32, 256), vm(32, 256),
            vm(8, 8, 256), vm(8, 8, 256), vm(8, 8, 256),
            vm(9, 8, 32, 256), vm(3, 8, 8, 32, 256, t=BF16), vm(8, 32, 256), vm(27, 8, 32, 256),
            vm(2, 4, 9, 32, 256), vm(2, 32, 256), vm(3, 4, 32, 256), vm(3, 4, 32, 256),
            dma((9,)), dma((9,)), dma, dma, dma, dma((12,)), dma((8,)),
        ],
        compiler_params=pltpu.CompilerParams(has_side_effects=True, collective_id=0, vmem_limit_bytes=56 << 20),
        name="exchange",
    )(loads, dest.reshape(1, 4096), cell.reshape(1, 4096), fields, areas, volume, sa, st, k)


def local(fields, volume, swept_axial, swept_angular, swept_radial, conductivity, corner_areas, parcel_loads, dest_device, dest_cell):
    chan, kzl, kzh, ktl, kth, grads = exchange(
        parcel_loads, dest_device, dest_cell, fields, corner_areas, volume, swept_axial, swept_angular, conductivity
    )
    vn, vn2, src, tlo, thi, grads = deposit(
        chan, fields, volume, swept_axial, swept_angular, swept_radial, grads
    )
    diffused = diffuse(src, tlo, thi, conductivity, vn2, kzl, kzh, ktl, kth)
    return vn, diffused, grads


def solution(mesh):
    P = jax.sharding.PartitionSpec
    cells = P("slab", "sector", None)
    in_specs = (
        P(None, "slab", "sector", None), cells, cells, cells, cells, cells,
        P(None, None, "slab", "sector", None), P(None, ("slab", "sector")), P(("slab", "sector"), None), P(("slab", "sector")),
    )
    out_specs = (cells, P(None, "slab", "sector", None), P(None, "slab", "sector", None))
    return jax.shard_map(local, mesh=mesh, in_specs=in_specs, out_specs=out_specs, check_vma=False)
```

```python
import jax
import jax.numpy as jnp
from jax import lax
from jax.experimental import pallas as pl
from jax.experimental.pallas import tpu as pltpu

F32, BF16, I32 = jnp.float32, jnp.bfloat16, jnp.int32
VM = pl.BlockSpec(memory_space=pltpu.VMEM)


def nt(a, b):
    return lax.dot_general(a, b, (((1,), (1,)), ((), ())), preferred_element_type=F32)


def iota(shape, dim):
    return lax.broadcasted_iota(I32, shape, dim)


def one_hot(row, count):
    n = row.shape[1]
    return jnp.where(iota((count, n), 0) == row, 1.0, 0.0).astype(BF16)


def split(x):
    hi = x.astype(BF16)
    return hi, (x - hi.astype(F32)).astype(BF16)


def before(n):
    return jnp.where(iota((n, n), 0) < iota((n, n), 1), 1.0, 0.0).astype(BF16)


GROUPS, ROWS, SLOTS, CHUNK = 16, 16, 384, 4096


def deposit_kernel(
    chan_ref, fields_ref, vol_ref, sa_ref, st_ref, sr_ref, grads_ref,
    vn_ref, vn2_ref, src_ref, tlo_ref, thi_ref, grads_out_ref,
    sort_ref, acc_ref, rank_ref, gbuf, sems,
):
    arriving = pltpu.make_async_copy(grads_ref, gbuf, sems.at[0])
    leaving = pltpu.make_async_copy(gbuf, grads_out_ref, sems.at[1])
    arriving.start()
    beneath = jnp.concatenate([chan_ref[10, 0:32], chan_ref[10, 32:64]], 1)
    aside = jnp.concatenate([chan_ref[11, 0:8], chan_ref[11, 8:16]], 1)
    for a in range(8):
        below = beneath if a == 0 else sa_ref[a - 1]
        stp = st_ref[a]
        row = iota((32, 256), 0)
        side = jnp.where(row == 0, aside[a : a + 1], pltpu.roll(stp, 1, 0))
        srp = sr_ref[a]
        lane = iota((32, 256), 1)
        inner = jnp.where(lane == 0, 0.0, pltpu.roll(srp, 1, 1))
        vn = vol_ref[a] + sa_ref[a] - below + stp - side + srp - inner
        vn_ref[a] = vn
        vn2_ref[a] = vn
    acc_ref[...] = jnp.zeros_like(acc_ref)
    earlier = before(256)

    def rows_of(c, start, count):
        part = chan_ref[c, start : start + count, :]
        return jnp.concatenate([part[i : i + 1] for i in range(count)], 1)

    for ch in range(8192 // CHUNK):
        nrow = CHUNK // 128
        carry = jnp.zeros((GROUPS, 1), F32)
        cell = rows_of(9, ch * nrow, nrow).astype(I32) - 1
        group = lax.shift_right_arithmetic(cell, 12)
        g = one_hot(group, GROUPS)
        gf = g.astype(F32)
        ranks = []
        for b in range(CHUNK // 256):
            gb = gf[:, b * 256 : (b + 1) * 256]
            count = jnp.dot(g[:, b * 256 : (b + 1) * 256], earlier, preferred_element_type=F32)
            ranks.append(jnp.sum(gb * (count + carry) , axis=0, keepdims=True))
            carry = carry + jnp.sum(gb, axis=1, keepdims=True)
        if ch == 1:
            arriving.wait()
            leaving.start()
        rank_ref[...] = jnp.concatenate(ranks, 1).astype(I32)
        most = jnp.max(carry).astype(I32)
        his, los = [], []
        for c in range(9):
            hi, lo = split(rows_of(c, ch * nrow, nrow))
            his.append(hi * g)
            los.append(lo * g)
        rowin = (lax.shift_right_logical(cell, 8) & 15).astype(F32).astype(BF16)
        colin = (cell & 255).astype(F32).astype(BF16)
        lhs = jnp.concatenate(his + los + [(rowin + 1.0) * g, colin * g], 0)

        def one_round(r, carry_unused):
            o = one_hot(rank_ref[...] - r * SLOTS, SLOTS)
            sort_ref[...] = nt(lhs, o)
            for gi in range(GROUPS):
                pick = lambda c: sort_ref[c * GROUPS + gi : c * GROUPS + gi + 1, :]
                rm = one_hot(pick(18).astype(I32) - 1, ROWS)
                j = one_hot(pick(19).astype(I32), 256)
                left = jnp.concatenate([pick(c).astype(BF16) * rm for c in range(18)], 0)
                out = nt(left, j)
                for f in range(9):
                    acc_ref[f, gi // 2, (gi % 2) * 16 : (gi % 2) * 16 + 16, :] += (
                        out[f * 16 : f * 16 + 16] + out[(9 + f) * 16 : (9 + f) * 16 + 16]
                    )
            return carry_unused

        lax.fori_loop(0, (most + SLOTS - 1) // SLOTS, one_round, 0)
    for a in range(8):
        inv = 1.0 / vn2_ref[a]
        for f in range(9):
            v = fields_ref[f, a] + acc_ref[f, a] * inv
            src_ref[f, a] = v
            tlo_ref[f, a : a + 1, :] = v[0:1]
            thi_ref[f, a : a + 1, :] = v[31:32]
    leaving.wait()


def deposit(chan, fields, volume, sa, st, sr, grads):
    sd = jax.ShapeDtypeStruct
    return pl.pallas_call(
        deposit_kernel,
        out_shape=(
            sd((8, 32, 256), F32), sd((8, 32, 256), F32), sd((9, 8, 32, 256), F32),
            sd((9, 8, 256), F32), sd((9, 8, 256), F32),
            sd((27, 8, 32, 256), F32),
        ),
        in_specs=[VM] * 6 + [pl.BlockSpec(memory_space=pl.ANY)],
        out_specs=[VM] * 5 + [pl.BlockSpec(memory_space=pl.ANY)],
        scratch_shapes=[
            pltpu.VMEM((20 * GROUPS, SLOTS), F32),
            pltpu.VMEM((9, 8, 32, 256), F32),
            pltpu.VMEM((1, CHUNK), I32),
            pltpu.VMEM((27, 8, 32, 256), F32),
            pltpu.SemaphoreType.DMA((2,)),
        ],
        compiler_params=pltpu.CompilerParams(vmem_limit_bytes=44 << 20),
        name="deposit",
    )(chan, fields, volume, sa, st, sr, grads)


def t_shift(x, edge):
    return jnp.where(iota(x.shape, 0) == 0, edge, pltpu.roll(x, 1, 0))


def r_shift(x):
    n = x.shape[1]
    return jnp.where(iota(x.shape, 1) == n - 1, 0.0, pltpu.roll(x, n - 1, 1))


def prepare(f_ref, w_ref, slot, field, vol, edge):
    for f in range(9):
        x = field(f)
        xt = t_shift(x, edge(f))
        f_ref[slot, 0, f] = r_shift(x)
        f_ref[slot, 1, f] = x
        f_ref[slot, 2, f] = r_shift(xt)
        f_ref[slot, 3, f] = xt
    v = vol * 0.125
    v = v + t_shift(v, edge(21) * 0.125)
    w_ref[slot] = v + r_shift(v)


def prepare_areas(a_ref, area, edge):
    for i in range(3):
        for q in range(4):
            x = area(i, q)
            if q // 2 == 1:
                x = t_shift(x, edge(i, q))
            a_ref[i, q] = x if q % 2 == 1 else pltpu.roll(x, 255, 1)


def gradient_plane(f_ref, w_ref, a0_ref, a1_ref, now, prev, out_ref, a):
    def part(n, unused):
        i = lax.rem(n, 3)
        rows = pl.ds(pl.multiple_of(n // 3 * 8, 8), 8)
        inv = 1.0 / (w_ref[now, rows] + w_ref[prev, rows])
        acc = [None] * 9
        for dz in range(2):
            for q in range(4):
                area = (a1_ref if dz else a0_ref)[i, q, rows]
                for f in range(9):
                    term = area * f_ref[prev if dz else now, q, f, rows]
                    acc[f] = term if dz + q == 0 else acc[f] + term
        for f in range(9):
            out_ref[9 * i + f, a, rows] = acc[f] * inv
        return unused

    lax.fori_loop(0, 12, part, 0)


def diffuse_kernel(
    src_ref, tlo_ref, thi_ref, k_ref, vn_ref, kzl_ref, kzh_ref, ktl_ref, kth_ref, out_ref,
    zlo, zhi, tlo, thi, w_ref, send_sems, recv_sems,
):
    slab, sector = lax.axis_index("slab"), lax.axis_index("sector")
    above = (lax.rem(slab + 1, 32), sector)
    below = (lax.rem(slab + 31, 32), sector)
    ahead = (slab, lax.rem(sector + 1, 4))
    behind = (slab, lax.rem(sector + 3, 4))
    barrier = pltpu.get_barrier_semaphore()
    for to in (above, below, ahead, behind):
        pl.semaphore_signal(barrier, inc=1, device_id=to, device_id_type=pl.DeviceIdType.MESH)
    halo = [
        (thi_ref, tlo, ahead), (tlo_ref, thi, behind),
        (src_ref.at[:, 7], zlo, above), (src_ref.at[:, 0], zhi, below),
    ]
    copies = [
        pltpu.make_async_remote_copy(
            src_ref=s, dst_ref=t, send_sem=send_sems.at[n], recv_sem=recv_sems.at[n],
            device_id=to, device_id_type=pl.DeviceIdType.MESH,
        )
        for n, (s, t, to) in enumerate(halo)
    ]
    pl.semaphore_wait(barrier, 4)
    for copy in copies:
        copy.start()
    row = iota((32, 256), 0)
    lane = iota((32, 256), 1)
    for a in range(8):
        k = k_ref[a]
        near = [
            kzl_ref[...] if a == 0 else k_ref[a - 1],
            kzh_ref[...] if a == 7 else k_ref[a + 1],
            jnp.where(row == 0, ktl_ref[a : a + 1], pltpu.roll(k, 1, 0)),
            jnp.where(row == 31, kth_ref[a : a + 1], pltpu.roll(k, 31, 0)),
            jnp.where(lane == 0, 0.0, pltpu.roll(k, 1, 1)),
            jnp.where(lane == 255, 0.0, pltpu.roll(k, 255, 1)),
        ]
        scale = (0.2 * k) / vn_ref[a]
        total = None
        for n, kn in enumerate(near):
            w = scale * kn / (k + kn)
            w_ref[n, a] = w
            total = w if total is None else total + w
        w_ref[6, a] = 1.0 - total
    copies[0].wait()
    copies[1].wait()

    def plane(f, a, under, over):
        s = src_ref[f, a]
        near = [
            under, over,
            jnp.where(row == 0, tlo[f, a : a + 1], pltpu.roll(s, 1, 0)),
            jnp.where(row == 31, thi[f, a : a + 1], pltpu.roll(s, 31, 0)),
            pltpu.roll(s, 1, 1),
            pltpu.roll(s, 255, 1),
        ]
        out = w_ref[6, a] * s
        for n in range(6):
            out = out + w_ref[n, a] * near[n]
        out_ref[f, a] = out

    def inner(f, unused):
        for a in range(1, 7):
            plane(f, a, src_ref[f, a - 1], src_ref[f, a + 1])
        return unused

    lax.fori_loop(0, 9, inner, 0)
    copies[2].wait()
    copies[3].wait()

    def ends(f, unused):
        plane(f, 0, zlo[f], src_ref[f, 1])
        plane(f, 7, src_ref[f, 6], zhi[f])
        return unused

    lax.fori_loop(0, 9, ends, 0)


def diffuse(src, tlo, thi, k, vn, kzl, kzh, ktl, kth):
    dma = pltpu.SemaphoreType.DMA
    cells = (9, 8, 32, 256)
    return pl.pallas_call(
        diffuse_kernel,
        out_shape=jax.ShapeDtypeStruct(cells, F32),
        in_specs=[VM] * 9,
        out_specs=VM,
        scratch_shapes=[
            pltpu.VMEM((9, 32, 256), F32), pltpu.VMEM((9, 32, 256), F32),
            pltpu.VMEM((9, 8, 256), F32), pltpu.VMEM((9, 8, 256), F32),
            pltpu.VMEM((7, 8, 32, 256), F32), dma((4,)), dma((4,)),
        ],
        compiler_params=pltpu.CompilerParams(has_side_effects=True, collective_id=1, vmem_limit_bytes=16 << 20),
        name="diffuse",
    )(src, tlo, thi, k, vn, kzl, kzh, ktl, kth)


def exchange_kernel(
    loads_in, dest_in, cell_in, fields_in, areas_in, vol_in, sa_in, st_in, k_in,
    chan_ref, kzl_ref, kzh_ref, ktl_ref, kth_ref, grads_ref,
    acc_ref, d_ref, rank_ref, out_buf, in_buf, azs, ts, cs, kbs, zr, tr, cr, kar, knr,
    loads_ref, dest_ref, cell_ref, sz_ref, kz_ref, kz0_ref, st_ref, kt_ref, kt0_ref,
    fbuf, abuf, vbuf, gbuf, f_ref, w_ref, a0_ref, a1_ref,
    send_sems, recv_sems, psend_sem, precv_sem, own_sem, load_sems, store_sems,
):
    slab, sector = lax.axis_index("slab"), lax.axis_index("sector")
    me = slab * 4 + sector
    barrier = pltpu.get_barrier_semaphore()
    loading = [
        pltpu.make_async_copy(s, t, load_sems.at[n])
        for n, (s, t) in enumerate((
            (dest_in, dest_ref), (loads_in, loads_ref), (cell_in, cell_ref),
            (fields_in, fbuf), (areas_in, abuf), (vol_in, vbuf),
            (sa_in.at[7], sz_ref), (k_in.at[7], kz_ref), (k_in.at[0], kz0_ref),
            (st_in.at[:, 24:32], st_ref), (k_in.at[:, 24:32], kt_ref), (k_in.at[:, 0:8], kt0_ref),
        ))
    ]
    for copy in loading:
        copy.start()

    def greet(k, unused):
        to = lax.rem(me + k, 128)
        pl.semaphore_signal(barrier, inc=1, device_id=(to // 4, lax.rem(to, 4)), device_id_type=pl.DeviceIdType.MESH)
        return unused

    lax.fori_loop(1, 128, greet, 0)

    loading[0].wait()
    blk, devices = 256, 128
    earlier = before(blk)
    carry = jnp.zeros((devices, 1), F32)
    count = 4096 // blk
    for b in range(count):
        d_ref[b * 128 : (b + 1) * 128, :] = one_hot(dest_ref[:, b * blk : (b + 1) * blk], devices)
    counts = jnp.dot(d_ref[...], earlier, preferred_element_type=F32)
    for b in range(count):
        df = d_ref[b * 128 : (b + 1) * 128, :].astype(F32)
        rank_ref[:, b * blk : (b + 1) * blk] = jnp.sum(
            df * (counts[b * 128 : (b + 1) * 128] + carry), axis=0, keepdims=True
        ).astype(I32)
        carry = carry + jnp.sum(df, axis=1, keepdims=True)

    for copy in loading[1:]:
        copy.wait()
    for n in range(12):
        x = abuf[n // 4, 4 + n % 4, 7].astype(F32)
        azs[n] = x
        cs[9 + n : 10 + n] = x[31:32]
        for a in range(8):
            ts[9 + n, a : a + 1, :] = abuf[n // 4, (2, 3, 6, 7)[n % 4], a].astype(F32)[31:32]
    for f in range(9):
        ts[f] = fbuf[f, :, 31, :]
        cs[f : f + 1] = fbuf[f, 7, 31:32]
    ts[21] = vbuf[:, 31, :]
    cs[21:22] = vbuf[7, 31:32]
    for n, (t_ref, z_ref) in enumerate(((st_ref, sz_ref), (kt_ref, kz_ref))):
        ts[22 + n] = t_ref[:, 7, :]
        cs[22 + n : 23 + n] = z_ref[31:32]
    kbs[...] = kt0_ref[:, 0, :]

    above = (lax.rem(slab + 1, 32), sector)
    below = (lax.rem(slab + 31, 32), sector)
    ahead = (slab, lax.rem(sector + 1, 4))
    behind = (slab, lax.rem(sector + 3, 4))
    across = (lax.rem(slab + 1, 32), lax.rem(sector + 1, 4))
    halo = [
        (sz_ref, zr.at[22], above),
        (kz_ref, zr.at[23], above),
        (kz0_ref, kar, below),
        (kbs, knr, behind),
        (ts, tr, ahead),
        (cs, cr, across),
        (vbuf.at[7], zr.at[21], above),
        (fbuf.at[:, 7], zr.at[0:9], above),
        (azs, zr.at[9:21], above),
    ]
    copies = [
        pltpu.make_async_remote_copy(
            src_ref=s, dst_ref=t, send_sem=send_sems.at[n], recv_sem=recv_sems.at[n],
            device_id=to, device_id_type=pl.DeviceIdType.MESH,
        )
        for n, (s, t, to) in enumerate(halo)
    ]
    acc_ref[...] = jnp.zeros_like(acc_ref)
    part = 512
    for b in range(4096 // part):
        sl = pl.ds(b * part, part)
        rank = rank_ref[:, sl]
        o = one_hot(rank & 31, 32)
        hi, lo = split(loads_ref[:, sl])
        cell = cell_ref[:, sl]
        row = (lax.shift_right_logical(cell, 8) * 256).astype(F32).astype(BF16)
        col = ((cell & 255) + 1).astype(F32).astype(BF16)
        his = jnp.concatenate([hi[c : c + 1] * o for c in range(9)] + [row * o], 0)
        los = jnp.concatenate([lo[c : c + 1] * o for c in range(9)] + [col * o], 0)
        d = one_hot(dest_ref[:, sl] + lax.shift_right_logical(rank, 5) * 128, 256)
        acc_ref[...] += nt(jnp.concatenate([his, los], 1), jnp.concatenate([d, d], 1))
    for s in range(5):
        block = jnp.concatenate(
            [acc_ref[c * 32 : (c + 1) * 32, h * 128 : (h + 1) * 128] for c in (2 * s, 2 * s + 1) for h in range(2)], 0
        )
        out_buf[:, s, :] = block.T
    pl.semaphore_wait(barrier, 127)
    for copy in copies:
        copy.start()
    own = pltpu.make_async_copy(out_buf.at[me], in_buf.at[me], own_sem)
    own.start()

    def send(k, unused):
        to = lax.rem(me + k, 128)
        pltpu.make_async_remote_copy(
            src_ref=out_buf.at[to], dst_ref=in_buf.at[me], send_sem=psend_sem, recv_sem=precv_sem,
            device_id=(to // 4, lax.rem(to, 4)), device_id_type=pl.DeviceIdType.MESH,
        ).start()
        return unused

    lax.fori_loop(1, 128, send, 0)
    copies[4].wait()

    def beside(plane):
        return lambda c: tr[c, pl.ds(plane, 1), :]

    def prepare_own(slot, plane):
        prepare(f_ref, w_ref, slot, lambda f: fbuf[f, plane], vbuf[plane], beside(plane))

    def own_areas(ref, plane, dz):
        prepare_areas(
            ref, lambda i, q: abuf[i, 4 * dz + q, plane].astype(F32),
            lambda i, q: beside(plane)(9 + 4 * i + 2 * dz + q % 2),
        )

    def store(a):
        return pltpu.make_async_copy(gbuf.at[:, a], grads_ref.at[:, a], store_sems.at[a])

    prepare_own(1, 7)

    def plane(n, unused):
        a = 7 - n
        now = lax.rem(a, 2)
        prepare_own(1 - now, a - 1)
        own_areas(a0_ref, a, 0)
        own_areas(a1_ref, a - 1, 1)
        gradient_plane(f_ref, w_ref, a0_ref, a1_ref, now, 1 - now, gbuf, a)
        store(a).start()
        return unused

    lax.fori_loop(0, 7, plane, 0)
    own_areas(a0_ref, 0, 0)
    inside = slab > 0

    def under(x):
        return jnp.where(inside, x, 0.0)

    own.wait()
    for n in (0, 1, 2, 3, 5):
        copies[n].wait()
    for h in range(2):
        chan_ref[10, 32 * h : 32 * h + 32] = under(zr[22, :, 128 * h : 128 * h + 128])
        chan_ref[11, 8 * h : 8 * h + 8] = tr[22, :, 128 * h : 128 * h + 128]
    kzl_ref[...] = under(zr[23])
    kzh_ref[...] = jnp.where(slab < 31, kar[...], 0.0)
    ktl_ref[...] = tr[23]
    kth_ref[...] = knr[...]
    most = pl.ds(0, 127)
    pltpu.make_async_copy(out_buf.at[most], in_buf.at[most], psend_sem).wait()
    pltpu.make_async_copy(out_buf.at[most], in_buf.at[most], precv_sem).wait()
    lane = iota((64, 128), 1) < 64
    for s in range(5):
        first, second = in_buf[0:64, s, :], in_buf[64:128, s, :]
        chan_ref[2 * s] = jnp.where(lane, first, pltpu.roll(second, 64, 1))
        chan_ref[2 * s + 1] = jnp.where(lane, pltpu.roll(first, 64, 1), second)
    for n in (6, 7, 8):
        copies[n].wait()
    prepare(f_ref, w_ref, 1, lambda f: under(zr[f]), under(zr[21]), lambda c: under(cr[c : c + 1, :]))
    prepare_areas(a1_ref, lambda i, q: zr[9 + 4 * i + q], lambda i, q: cr[9 + 4 * i + q : 10 + 4 * i + q, :])
    gradient_plane(f_ref, w_ref, a0_ref, a1_ref, 0, 1, gbuf, 0)
    store(0).start()
    for a in range(8):
        store(a).wait()


def exchange(loads, dest, cell, fields, areas, volume, sa, st, k):
    hbm = pl.BlockSpec(memory_space=pltpu.HBM)
    shapes = [(12, 64, 128), (32, 256), (32, 256), (8, 256), (8, 256), (27, 8, 32, 256)]
    dma = pltpu.SemaphoreType.DMA
    vm = lambda *shape, t=F32: pltpu.VMEM(shape, t)
    return pl.pallas_call(
        exchange_kernel,
        out_shape=[jax.ShapeDtypeStruct(s, F32) for s in shapes],
        in_specs=[hbm] * 9,
        out_specs=[VM] * 5 + [hbm],
        scratch_shapes=[
            vm(320, 256), vm(2048, 256, t=BF16), vm(1, 4096, t=I32), vm(128, 5, 128), vm(128, 5, 128),
            vm(12, 32, 256), vm(24, 8, 256), vm(24, 256), vm(8, 256),
            vm(24, 32, 256), vm(24, 8, 256), vm(24, 256), vm(32, 256), vm(8, 256),
            vm(9, 4096), vm(1, 4096, t=I32), vm(1, 4096, t=I32), vm(32, 256), vm(32, 256), vm(32, 256),
            vm(8, 8, 256), vm(8, 8, 256), vm(8, 8, 256),
            vm(9, 8, 32, 256), vm(3, 8, 8, 32, 256, t=BF16), vm(8, 32, 256), vm(27, 8, 32, 256),
            vm(2, 4, 9, 32, 256), vm(2, 32, 256), vm(3, 4, 32, 256), vm(3, 4, 32, 256),
            dma((9,)), dma((9,)), dma, dma, dma, dma((12,)), dma((8,)),
        ],
        compiler_params=pltpu.CompilerParams(has_side_effects=True, collective_id=0, vmem_limit_bytes=56 << 20),
        name="exchange",
    )(loads, dest.reshape(1, 4096), cell.reshape(1, 4096), fields, areas, volume, sa, st, k)


def local(fields, volume, swept_axial, swept_angular, swept_radial, conductivity, corner_areas, parcel_loads, dest_device, dest_cell):
    chan, kzl, kzh, ktl, kth, grads = exchange(
        parcel_loads, dest_device, dest_cell, fields, corner_areas, volume, swept_axial, swept_angular, conductivity
    )
    vn, vn2, src, tlo, thi, grads = deposit(
        chan, fields, volume, swept_axial, swept_angular, swept_radial, grads
    )
    diffused = diffuse(src, tlo, thi, conductivity, vn2, kzl, kzh, ktl, kth)
    return vn, diffused, grads


def solution(mesh):
    P = jax.sharding.PartitionSpec
    cells = P("slab", "sector", None)
    in_specs = (
        P(None, "slab", "sector", None), cells, cells, cells, cells, cells,
        P(None, None, "slab", "sector", None), P(None, ("slab", "sector")), P(("slab", "sector"), None), P(("slab", "sector")),
    )
    out_specs = (cells, P(None, "slab", "sector", None), P(None, "slab", "sector", None))
    return jax.shard_map(local, mesh=mesh, in_specs=in_specs, out_specs=out_specs, check_vma=False)
```

```python
import jax
import jax.numpy as jnp
from jax import lax
from jax.experimental import pallas as pl
from jax.experimental.pallas import tpu as pltpu

F32, BF16, I32 = jnp.float32, jnp.bfloat16, jnp.int32
VM = pl.BlockSpec(memory_space=pltpu.VMEM)


def nt(a, b):
    return lax.dot_general(a, b, (((1,), (1,)), ((), ())), preferred_element_type=F32)


def iota(shape, dim):
    return lax.broadcasted_iota(I32, shape, dim)


def one_hot(row, count):
    n = row.shape[1]
    return jnp.where(iota((count, n), 0) == row, 1.0, 0.0).astype(BF16)


def split(x):
    hi = x.astype(BF16)
    return hi, (x - hi.astype(F32)).astype(BF16)


def before(n):
    return jnp.where(iota((n, n), 0) < iota((n, n), 1), 1.0, 0.0).astype(BF16)


GROUPS, ROWS, SLOTS, CHUNK = 16, 16, 384, 4096


def deposit_kernel(
    chan_ref, fields_ref, vol_ref, sa_ref, st_ref, sr_ref, grads_ref,
    vn_ref, vn2_ref, src_ref, tlo_ref, thi_ref, grads_out_ref,
    sort_ref, acc_ref, rank_ref, gbuf, sems,
):
    arriving = pltpu.make_async_copy(grads_ref, gbuf, sems.at[0])
    leaving = pltpu.make_async_copy(gbuf, grads_out_ref, sems.at[1])
    arriving.start()
    beneath = jnp.concatenate([chan_ref[10, 0:32], chan_ref[10, 32:64]], 1)
    aside = jnp.concatenate([chan_ref[11, 0:8], chan_ref[11, 8:16]], 1)
    for a in range(8):
        below = beneath if a == 0 else sa_ref[a - 1]
        stp = st_ref[a]
        row = iota((32, 256), 0)
        side = jnp.where(row == 0, aside[a : a + 1], pltpu.roll(stp, 1, 0))
        srp = sr_ref[a]
        lane = iota((32, 256), 1)
        inner = jnp.where(lane == 0, 0.0, pltpu.roll(srp, 1, 1))
        vn = vol_ref[a] + sa_ref[a] - below + stp - side + srp - inner
        vn_ref[a] = vn
        vn2_ref[a] = vn
    acc_ref[...] = jnp.zeros_like(acc_ref)
    earlier = before(256)

    def rows_of(c, start, count):
        part = chan_ref[c, start : start + count, :]
        return jnp.concatenate([part[i : i + 1] for i in range(count)], 1)

    for ch in range(8192 // CHUNK):
        nrow = CHUNK // 128
        carry = jnp.zeros((GROUPS, 1), F32)
        cell = rows_of(9, ch * nrow, nrow).astype(I32) - 1
        group = lax.shift_right_arithmetic(cell, 12)
        g = one_hot(group, GROUPS)
        gf = g.astype(F32)
        ranks = []
        for b in range(CHUNK // 256):
            gb = gf[:, b * 256 : (b + 1) * 256]
            count = jnp.dot(g[:, b * 256 : (b + 1) * 256], earlier, preferred_element_type=F32)
            ranks.append(jnp.sum(gb * (count + carry) , axis=0, keepdims=True))
            carry = carry + jnp.sum(gb, axis=1, keepdims=True)
        if ch == 1:
            arriving.wait()
            leaving.start()
        rank_ref[...] = jnp.concatenate(ranks, 1).astype(I32)
        most = jnp.max(carry).astype(I32)
        his, los = [], []
        for c in range(9):
            hi, lo = split(rows_of(c, ch * nrow, nrow))
            his.append(hi * g)
            los.append(lo * g)
        rowin = (lax.shift_right_logical(cell, 8) & 15).astype(F32).astype(BF16)
        colin = (cell & 255).astype(F32).astype(BF16)
        lhs = jnp.concatenate(his + los + [(rowin + 1.0) * g, colin * g], 0)

        def one_round(r, carry_unused):
            o = one_hot(rank_ref[...] - r * SLOTS, SLOTS)
            sort_ref[...] = nt(lhs, o)
            for gi in range(GROUPS):
                pick = lambda c: sort_ref[c * GROUPS + gi : c * GROUPS + gi + 1, :]
                rm = one_hot(pick(18).astype(I32) - 1, ROWS)
                j = one_hot(pick(19).astype(I32), 256)
                left = jnp.concatenate([pick(c).astype(BF16) * rm for c in range(18)], 0)
                out = nt(left, j)
                for f in range(9):
                    acc_ref[f, gi // 2, (gi % 2) * 16 : (gi % 2) * 16 + 16, :] += (
                        out[f * 16 : f * 16 + 16] + out[(9 + f) * 16 : (9 + f) * 16 + 16]
                    )
            return carry_unused

        lax.fori_loop(0, (most + SLOTS - 1) // SLOTS, one_round, 0)
    for a in range(8):
        inv = 1.0 / vn2_ref[a]
        for f in range(9):
            v = fields_ref[f, a] + acc_ref[f, a] * inv
            src_ref[f, a] = v
            tlo_ref[f, a : a + 1, :] = v[0:1]
            thi_ref[f, a : a + 1, :] = v[31:32]
    leaving.wait()


def deposit(chan, fields, volume, sa, st, sr, grads):
    sd = jax.ShapeDtypeStruct
    return pl.pallas_call(
        deposit_kernel,
        out_shape=(
            sd((8, 32, 256), F32), sd((8, 32, 256), F32), sd((9, 8, 32, 256), F32),
            sd((9, 8, 256), F32), sd((9, 8, 256), F32),
            sd((27, 8, 32, 256), F32),
        ),
        in_specs=[VM] * 6 + [pl.BlockSpec(memory_space=pl.ANY)],
        out_specs=[VM] * 5 + [pl.BlockSpec(memory_space=pl.ANY)],
        scratch_shapes=[
            pltpu.VMEM((20 * GROUPS, SLOTS), F32),
            pltpu.VMEM((9, 8, 32, 256), F32),
            pltpu.VMEM((1, CHUNK), I32),
            pltpu.VMEM((27, 8, 32, 256), F32),
            pltpu.SemaphoreType.DMA((2,)),
        ],
        compiler_params=pltpu.CompilerParams(vmem_limit_bytes=44 << 20),
        name="deposit",
    )(chan, fields, volume, sa, st, sr, grads)


def t_shift(x, edge):
    return jnp.where(iota(x.shape, 0) == 0, edge, pltpu.roll(x, 1, 0))


def r_shift(x):
    n = x.shape[1]
    return jnp.where(iota(x.shape, 1) == n - 1, 0.0, pltpu.roll(x, n - 1, 1))


def prepare(f_ref, w_ref, slot, field, vol, edge):
    for f in range(9):
        x = field(f)
        xt = t_shift(x, edge(f))
        f_ref[slot, 0, f] = r_shift(x)
        f_ref[slot, 1, f] = x
        f_ref[slot, 2, f] = r_shift(xt)
        f_ref[slot, 3, f] = xt
    v = vol * 0.125
    v = v + t_shift(v, edge(21) * 0.125)
    w_ref[slot] = v + r_shift(v)


def prepare_areas(a_ref, area, edge):
    for i in range(3):
        for q in range(4):
            x = area(i, q)
            if q // 2 == 1:
                x = t_shift(x, edge(i, q))
            a_ref[i, q] = x if q % 2 == 1 else pltpu.roll(x, 255, 1)


def gradient_plane(f_ref, w_ref, a0_ref, a1_ref, now, prev, out_ref, a, first=0, last=12):
    def part(n, unused):
        i = lax.rem(n, 3)
        rows = pl.ds(pl.multiple_of(n // 3 * 8, 8), 8)
        inv = 1.0 / (w_ref[now, rows] + w_ref[prev, rows])
        acc = [None] * 9
        for dz in range(2):
            for q in range(4):
                area = (a1_ref if dz else a0_ref)[i, q, rows]
                for f in range(9):
                    term = area * f_ref[prev if dz else now, q, f, rows]
                    acc[f] = term if dz + q == 0 else acc[f] + term
        for f in range(9):
            out_ref[9 * i + f, a, rows] = acc[f] * inv
        return unused

    lax.fori_loop(first, last, part, 0)


def diffuse_kernel(
    src_ref, tlo_ref, thi_ref, k_ref, vn_ref, kzl_ref, kzh_ref, ktl_ref, kth_ref, out_ref,
    zlo, zhi, tlo, thi, w_ref, send_sems, recv_sems,
):
    slab, sector = lax.axis_index("slab"), lax.axis_index("sector")
    above = (lax.rem(slab + 1, 32), sector)
    below = (lax.rem(slab + 31, 32), sector)
    ahead = (slab, lax.rem(sector + 1, 4))
    behind = (slab, lax.rem(sector + 3, 4))
    barrier = pltpu.get_barrier_semaphore()
    for to in (above, below, ahead, behind):
        pl.semaphore_signal(barrier, inc=1, device_id=to, device_id_type=pl.DeviceIdType.MESH)
    halo = [
        (thi_ref, tlo, ahead), (tlo_ref, thi, behind),
        (src_ref.at[:, 7], zlo, above), (src_ref.at[:, 0], zhi, below),
    ]
    copies = [
        pltpu.make_async_remote_copy(
            src_ref=s, dst_ref=t, send_sem=send_sems.at[n], recv_sem=recv_sems.at[n],
            device_id=to, device_id_type=pl.DeviceIdType.MESH,
        )
        for n, (s, t, to) in enumerate(halo)
    ]
    pl.semaphore_wait(barrier, 4)
    for copy in copies:
        copy.start()
    row = iota((32, 256), 0)
    lane = iota((32, 256), 1)
    for a in range(8):
        k = k_ref[a]
        near = [
            kzl_ref[...] if a == 0 else k_ref[a - 1],
            kzh_ref[...] if a == 7 else k_ref[a + 1],
            jnp.where(row == 0, ktl_ref[a : a + 1], pltpu.roll(k, 1, 0)),
            jnp.where(row == 31, kth_ref[a : a + 1], pltpu.roll(k, 31, 0)),
            jnp.where(lane == 0, 0.0, pltpu.roll(k, 1, 1)),
            jnp.where(lane == 255, 0.0, pltpu.roll(k, 255, 1)),
        ]
        scale = (0.2 * k) / vn_ref[a]
        total = None
        for n, kn in enumerate(near):
            w = scale * kn / (k + kn)
            w_ref[n, a] = w
            total = w if total is None else total + w
        w_ref[6, a] = 1.0 - total
    copies[0].wait()
    copies[1].wait()

    def plane(f, a, under, over):
        s = src_ref[f, a]
        near = [
            under, over,
            jnp.where(row == 0, tlo[f, a : a + 1], pltpu.roll(s, 1, 0)),
            jnp.where(row == 31, thi[f, a : a + 1], pltpu.roll(s, 31, 0)),
            pltpu.roll(s, 1, 1),
            pltpu.roll(s, 255, 1),
        ]
        out = w_ref[6, a] * s
        for n in range(6):
            out = out + w_ref[n, a] * near[n]
        out_ref[f, a] = out

    def inner(f, unused):
        for a in range(1, 7):
            plane(f, a, src_ref[f, a - 1], src_ref[f, a + 1])
        return unused

    lax.fori_loop(0, 9, inner, 0)
    copies[2].wait()
    copies[3].wait()

    def ends(f, unused):
        plane(f, 0, zlo[f], src_ref[f, 1])
        plane(f, 7, src_ref[f, 6], zhi[f])
        return unused

    lax.fori_loop(0, 9, ends, 0)


def diffuse(src, tlo, thi, k, vn, kzl, kzh, ktl, kth):
    dma = pltpu.SemaphoreType.DMA
    cells = (9, 8, 32, 256)
    return pl.pallas_call(
        diffuse_kernel,
        out_shape=jax.ShapeDtypeStruct(cells, F32),
        in_specs=[VM] * 9,
        out_specs=VM,
        scratch_shapes=[
            pltpu.VMEM((9, 32, 256), F32), pltpu.VMEM((9, 32, 256), F32),
            pltpu.VMEM((9, 8, 256), F32), pltpu.VMEM((9, 8, 256), F32),
            pltpu.VMEM((7, 8, 32, 256), F32), dma((4,)), dma((4,)),
        ],
        compiler_params=pltpu.CompilerParams(has_side_effects=True, collective_id=1, vmem_limit_bytes=16 << 20),
        name="diffuse",
    )(src, tlo, thi, k, vn, kzl, kzh, ktl, kth)


def exchange_kernel(
    loads_in, dest_in, cell_in, fields_in, areas_in, vol_in, sa_in, st_in, k_in,
    chan_ref, kzl_ref, kzh_ref, ktl_ref, kth_ref, grads_ref,
    acc_ref, d_ref, rank_ref, out_buf, in_buf, azs, ts, cs, kbs, zr, tr, cr, kar, knr,
    loads_ref, dest_ref, cell_ref, sz_ref, kz_ref, kz0_ref, st_ref, kt_ref, kt0_ref,
    fbuf, abuf, vbuf, gbuf, f_ref, w_ref, a0_ref, a1_ref,
    send_sems, recv_sems, psend_sem, precv_sem, own_sem, load_sems, store_sems,
):
    slab, sector = lax.axis_index("slab"), lax.axis_index("sector")
    me = slab * 4 + sector
    barrier = pltpu.get_barrier_semaphore()
    loading = [
        pltpu.make_async_copy(s, t, load_sems.at[n])
        for n, (s, t) in enumerate((
            (dest_in, dest_ref), (loads_in, loads_ref), (cell_in, cell_ref),
            (fields_in, fbuf), (areas_in, abuf), (vol_in, vbuf),
            (sa_in.at[7], sz_ref), (k_in.at[7], kz_ref), (k_in.at[0], kz0_ref),
            (st_in.at[:, 24:32], st_ref), (k_in.at[:, 24:32], kt_ref), (k_in.at[:, 0:8], kt0_ref),
        ))
    ]
    for copy in loading:
        copy.start()

    def greet(k, unused):
        to = lax.rem(me + k, 128)
        pl.semaphore_signal(barrier, inc=1, device_id=(to // 4, lax.rem(to, 4)), device_id_type=pl.DeviceIdType.MESH)
        return unused

    lax.fori_loop(1, 128, greet, 0)

    loading[0].wait()
    blk, devices = 256, 128
    earlier = before(blk)
    carry = jnp.zeros((devices, 1), F32)
    count = 4096 // blk
    for b in range(count):
        d_ref[b * 128 : (b + 1) * 128, :] = one_hot(dest_ref[:, b * blk : (b + 1) * blk], devices)
    counts = jnp.dot(d_ref[...], earlier, preferred_element_type=F32)
    for b in range(count):
        df = d_ref[b * 128 : (b + 1) * 128, :].astype(F32)
        rank_ref[:, b * blk : (b + 1) * blk] = jnp.sum(
            df * (counts[b * 128 : (b + 1) * 128] + carry), axis=0, keepdims=True
        ).astype(I32)
        carry = carry + jnp.sum(df, axis=1, keepdims=True)

    for copy in loading[1:]:
        copy.wait()
    for n in range(12):
        x = abuf[n // 4, 4 + n % 4, 7].astype(F32)
        azs[n] = x
        cs[9 + n : 10 + n] = x[31:32]
        for a in range(8):
            ts[9 + n, a : a + 1, :] = abuf[n // 4, (2, 3, 6, 7)[n % 4], a].astype(F32)[31:32]
    for f in range(9):
        ts[f] = fbuf[f, :, 31, :]
        cs[f : f + 1] = fbuf[f, 7, 31:32]
    ts[21] = vbuf[:, 31, :]
    cs[21:22] = vbuf[7, 31:32]
    for n, (t_ref, z_ref) in enumerate(((st_ref, sz_ref), (kt_ref, kz_ref))):
        ts[22 + n] = t_ref[:, 7, :]
        cs[22 + n : 23 + n] = z_ref[31:32]
    kbs[...] = kt0_ref[:, 0, :]

    above = (lax.rem(slab + 1, 32), sector)
    below = (lax.rem(slab + 31, 32), sector)
    ahead = (slab, lax.rem(sector + 1, 4))
    behind = (slab, lax.rem(sector + 3, 4))
    across = (lax.rem(slab + 1, 32), lax.rem(sector + 1, 4))
    halo = [
        (sz_ref, zr.at[22], above),
        (kz_ref, zr.at[23], above),
        (kz0_ref, kar, below),
        (kbs, knr, behind),
        (ts, tr, ahead),
        (cs, cr, across),
        (vbuf.at[7], zr.at[21], above),
        (fbuf.at[:, 7], zr.at[0:9], above),
        (azs, zr.at[9:21], above),
    ]
    copies = [
        pltpu.make_async_remote_copy(
            src_ref=s, dst_ref=t, send_sem=send_sems.at[n], recv_sem=recv_sems.at[n],
            device_id=to, device_id_type=pl.DeviceIdType.MESH,
        )
        for n, (s, t, to) in enumerate(halo)
    ]
    acc_ref[...] = jnp.zeros_like(acc_ref)
    part = 512
    for b in range(4096 // part):
        sl = pl.ds(b * part, part)
        rank = rank_ref[:, sl]
        o = one_hot(rank & 31, 32)
        hi, lo = split(loads_ref[:, sl])
        cell = cell_ref[:, sl]
        row = (lax.shift_right_logical(cell, 8) * 256).astype(F32).astype(BF16)
        col = ((cell & 255) + 1).astype(F32).astype(BF16)
        his = jnp.concatenate([hi[c : c + 1] * o for c in range(9)] + [row * o], 0)
        los = jnp.concatenate([lo[c : c + 1] * o for c in range(9)] + [col * o], 0)
        d = one_hot(dest_ref[:, sl] + lax.shift_right_logical(rank, 5) * 128, 256)
        acc_ref[...] += nt(jnp.concatenate([his, los], 1), jnp.concatenate([d, d], 1))
    for s in range(5):
        block = jnp.concatenate(
            [acc_ref[c * 32 : (c + 1) * 32, h * 128 : (h + 1) * 128] for c in (2 * s, 2 * s + 1) for h in range(2)], 0
        )
        out_buf[:, s, :] = block.T
    nothing = jnp.zeros((1, 256), F32)
    for slot, a in ((1, 7), (0, 6)):
        prepare(f_ref, w_ref, slot, lambda f: fbuf[f, a], vbuf[a], lambda c: nothing)
    prepare_areas(a0_ref, lambda i, q: abuf[i, q, 7].astype(F32), lambda i, q: nothing)
    prepare_areas(a1_ref, lambda i, q: abuf[i, 4 + q, 6].astype(F32), lambda i, q: nothing)
    gradient_plane(f_ref, w_ref, a0_ref, a1_ref, 1, 0, gbuf, 7, 3, 12)
    pl.semaphore_wait(barrier, 127)
    for copy in copies:
        copy.start()
    own = pltpu.make_async_copy(out_buf.at[me], in_buf.at[me], own_sem)
    own.start()

    def send(k, unused):
        to = lax.rem(me + k, 128)
        pltpu.make_async_remote_copy(
            src_ref=out_buf.at[to], dst_ref=in_buf.at[me], send_sem=psend_sem, recv_sem=precv_sem,
            device_id=(to // 4, lax.rem(to, 4)), device_id_type=pl.DeviceIdType.MESH,
        ).start()
        return unused

    lax.fori_loop(1, 128, send, 0)
    copies[4].wait()

    def beside(plane):
        return lambda c: tr[c, pl.ds(plane, 1), :]

    def prepare_own(slot, plane):
        prepare(f_ref, w_ref, slot, lambda f: fbuf[f, plane], vbuf[plane], beside(plane))

    def own_areas(ref, plane, dz):
        prepare_areas(
            ref, lambda i, q: abuf[i, 4 * dz + q, plane].astype(F32),
            lambda i, q: beside(plane)(9 + 4 * i + 2 * dz + q % 2),
        )

    def store(a):
        return pltpu.make_async_copy(gbuf.at[:, a], grads_ref.at[:, a], store_sems.at[a])

    for slot, a in ((1, 7), (0, 6)):
        for f in range(9):
            x = tr[f, a : a + 1, :]
            f_ref[slot, 2, f, 0:1, :] = r_shift(x)
            f_ref[slot, 3, f, 0:1, :] = x
        v = vbuf[a, 0:1, :] * 0.125 + tr[21, a : a + 1, :] * 0.125
        w_ref[slot, 0:1, :] = v + r_shift(v)
    for ref, a, dz in ((a0_ref, 7, 0), (a1_ref, 6, 1)):
        for i in range(3):
            for q in (2, 3):
                x = tr[9 + 4 * i + 2 * dz + q % 2, a : a + 1, :]
                ref[i, q, 0:1, :] = x if q == 3 else pltpu.roll(x, 255, 1)
    gradient_plane(f_ref, w_ref, a0_ref, a1_ref, 1, 0, gbuf, 7, 0, 3)
    store(7).start()

    def plane(n, unused):
        a = 7 - n
        now = lax.rem(a, 2)
        prepare_own(1 - now, a - 1)
        own_areas(a0_ref, a, 0)
        own_areas(a1_ref, a - 1, 1)
        gradient_plane(f_ref, w_ref, a0_ref, a1_ref, now, 1 - now, gbuf, a)
        store(a).start()
        return unused

    lax.fori_loop(1, 7, plane, 0)
    own_areas(a0_ref, 0, 0)
    inside = slab > 0

    def under(x):
        return jnp.where(inside, x, 0.0)

    own.wait()
    for n in (0, 1, 2, 3, 5):
        copies[n].wait()
    for h in range(2):
        chan_ref[10, 32 * h : 32 * h + 32] = under(zr[22, :, 128 * h : 128 * h + 128])
        chan_ref[11, 8 * h : 8 * h + 8] = tr[22, :, 128 * h : 128 * h + 128]
    kzl_ref[...] = under(zr[23])
    kzh_ref[...] = jnp.where(slab < 31, kar[...], 0.0)
    ktl_ref[...] = tr[23]
    kth_ref[...] = knr[...]
    most = pl.ds(0, 127)
    pltpu.make_async_copy(out_buf.at[most], in_buf.at[most], psend_sem).wait()
    pltpu.make_async_copy(out_buf.at[most], in_buf.at[most], precv_sem).wait()
    lane = iota((64, 128), 1) < 64
    for s in range(5):
        first, second = in_buf[0:64, s, :], in_buf[64:128, s, :]
        chan_ref[2 * s] = jnp.where(lane, first, pltpu.roll(second, 64, 1))
        chan_ref[2 * s + 1] = jnp.where(lane, pltpu.roll(first, 64, 1), second)
    for n in (6, 7, 8):
        copies[n].wait()
    prepare(f_ref, w_ref, 1, lambda f: under(zr[f]), under(zr[21]), lambda c: under(cr[c : c + 1, :]))
    prepare_areas(a1_ref, lambda i, q: zr[9 + 4 * i + q], lambda i, q: cr[9 + 4 * i + q : 10 + 4 * i + q, :])
    gradient_plane(f_ref, w_ref, a0_ref, a1_ref, 0, 1, gbuf, 0)
    store(0).start()
    for a in range(8):
        store(a).wait()


def exchange(loads, dest, cell, fields, areas, volume, sa, st, k):
    hbm = pl.BlockSpec(memory_space=pltpu.HBM)
    shapes = [(12, 64, 128), (32, 256), (32, 256), (8, 256), (8, 256), (27, 8, 32, 256)]
    dma = pltpu.SemaphoreType.DMA
    vm = lambda *shape, t=F32: pltpu.VMEM(shape, t)
    return pl.pallas_call(
        exchange_kernel,
        out_shape=[jax.ShapeDtypeStruct(s, F32) for s in shapes],
        in_specs=[hbm] * 9,
        out_specs=[VM] * 5 + [hbm],
        scratch_shapes=[
            vm(320, 256), vm(2048, 256, t=BF16), vm(1, 4096, t=I32), vm(128, 5, 128), vm(128, 5, 128),
            vm(12, 32, 256), vm(24, 8, 256), vm(24, 256), vm(8, 256),
            vm(24, 32, 256), vm(24, 8, 256), vm(24, 256), vm(32, 256), vm(8, 256),
            vm(9, 4096), vm(1, 4096, t=I32), vm(1, 4096, t=I32), vm(32, 256), vm(32, 256), vm(32, 256),
            vm(8, 8, 256), vm(8, 8, 256), vm(8, 8, 256),
            vm(9, 8, 32, 256), vm(3, 8, 8, 32, 256, t=BF16), vm(8, 32, 256), vm(27, 8, 32, 256),
            vm(2, 4, 9, 32, 256), vm(2, 32, 256), vm(3, 4, 32, 256), vm(3, 4, 32, 256),
            dma((9,)), dma((9,)), dma, dma, dma, dma((12,)), dma((8,)),
        ],
        compiler_params=pltpu.CompilerParams(has_side_effects=True, collective_id=0, vmem_limit_bytes=56 << 20),
        name="exchange",
    )(loads, dest.reshape(1, 4096), cell.reshape(1, 4096), fields, areas, volume, sa, st, k)


def local(fields, volume, swept_axial, swept_angular, swept_radial, conductivity, corner_areas, parcel_loads, dest_device, dest_cell):
    chan, kzl, kzh, ktl, kth, grads = exchange(
        parcel_loads, dest_device, dest_cell, fields, corner_areas, volume, swept_axial, swept_angular, conductivity
    )
    vn, vn2, src, tlo, thi, grads = deposit(
        chan, fields, volume, swept_axial, swept_angular, swept_radial, grads
    )
    diffused = diffuse(src, tlo, thi, conductivity, vn2, kzl, kzh, ktl, kth)
    return vn, diffused, grads


def solution(mesh):
    P = jax.sharding.PartitionSpec
    cells = P("slab", "sector", None)
    in_specs = (
        P(None, "slab", "sector", None), cells, cells, cells, cells, cells,
        P(None, None, "slab", "sector", None), P(None, ("slab", "sector")), P(("slab", "sector"), None), P(("slab", "sector")),
    )
    out_specs = (cells, P(None, "slab", "sector", None), P(None, "slab", "sector", None))
    return jax.shard_map(local, mesh=mesh, in_specs=in_specs, out_specs=out_specs, check_vma=False)
```

```python
import jax
import jax.numpy as jnp
from jax import lax
from jax.experimental import pallas as pl
from jax.experimental.pallas import tpu as pltpu

F32, BF16, I32 = jnp.float32, jnp.bfloat16, jnp.int32
VM = pl.BlockSpec(memory_space=pltpu.VMEM)


def nt(a, b):
    return lax.dot_general(a, b, (((1,), (1,)), ((), ())), preferred_element_type=F32)


def iota(shape, dim):
    return lax.broadcasted_iota(I32, shape, dim)


def one_hot(row, count):
    n = row.shape[1]
    return jnp.where(iota((count, n), 0) == row, 1.0, 0.0).astype(BF16)


def split(x):
    hi = x.astype(BF16)
    return hi, (x - hi.astype(F32)).astype(BF16)


def before(n):
    return jnp.where(iota((n, n), 0) < iota((n, n), 1), 1.0, 0.0).astype(BF16)


GROUPS, ROWS, SLOTS, CHUNK = 16, 16, 384, 4096


def deposit_kernel(
    chan_ref, fields_ref, vol_ref, sa_ref, st_ref, sr_ref, grads_ref,
    vn_ref, vn2_ref, src_ref, tlo_ref, thi_ref, grads_out_ref,
    sort_ref, acc_ref, rank_ref, gbuf, sems,
):
    arriving = pltpu.make_async_copy(grads_ref, gbuf, sems.at[0])
    leaving = pltpu.make_async_copy(gbuf, grads_out_ref, sems.at[1])
    arriving.start()
    beneath = jnp.concatenate([chan_ref[10, 0:32], chan_ref[10, 32:64]], 1)
    aside = jnp.concatenate([chan_ref[11, 0:8], chan_ref[11, 8:16]], 1)
    for a in range(8):
        below = beneath if a == 0 else sa_ref[a - 1]
        stp = st_ref[a]
        row = iota((32, 256), 0)
        side = jnp.where(row == 0, aside[a : a + 1], pltpu.roll(stp, 1, 0))
        srp = sr_ref[a]
        lane = iota((32, 256), 1)
        inner = jnp.where(lane == 0, 0.0, pltpu.roll(srp, 1, 1))
        vn = vol_ref[a] + sa_ref[a] - below + stp - side + srp - inner
        vn_ref[a] = vn
        vn2_ref[a] = vn
    acc_ref[...] = jnp.zeros_like(acc_ref)
    earlier = before(256)

    def rows_of(c, start, count):
        part = chan_ref[c, start : start + count, :]
        return jnp.concatenate([part[i : i + 1] for i in range(count)], 1)

    for ch in range(8192 // CHUNK):
        nrow = CHUNK // 128
        carry = jnp.zeros((GROUPS, 1), F32)
        cell = rows_of(9, ch * nrow, nrow).astype(I32) - 1
        group = lax.shift_right_arithmetic(cell, 12)
        g = one_hot(group, GROUPS)
        gf = g.astype(F32)
        ranks = []
        for b in range(CHUNK // 256):
            gb = gf[:, b * 256 : (b + 1) * 256]
            count = jnp.dot(g[:, b * 256 : (b + 1) * 256], earlier, preferred_element_type=F32)
            ranks.append(jnp.sum(gb * (count + carry) , axis=0, keepdims=True))
            carry = carry + jnp.sum(gb, axis=1, keepdims=True)
        if ch == 1:
            arriving.wait()
            leaving.start()
        rank_ref[...] = jnp.concatenate(ranks, 1).astype(I32)
        most = jnp.max(carry).astype(I32)
        his, los = [], []
        for c in range(9):
            hi, lo = split(rows_of(c, ch * nrow, nrow))
            his.append(hi * g)
            los.append(lo * g)
        rowin = (lax.shift_right_logical(cell, 8) & 15).astype(F32).astype(BF16)
        colin = (cell & 255).astype(F32).astype(BF16)
        lhs = jnp.concatenate(his + los + [(rowin + 1.0) * g, colin * g], 0)

        def one_round(r, carry_unused):
            o = one_hot(rank_ref[...] - r * SLOTS, SLOTS)
            sort_ref[...] = nt(lhs, o)
            for gi in range(GROUPS):
                pick = lambda c: sort_ref[c * GROUPS + gi : c * GROUPS + gi + 1, :]
                rm = one_hot(pick(18).astype(I32) - 1, ROWS)
                j = one_hot(pick(19).astype(I32), 256)
                left = jnp.concatenate([pick(c).astype(BF16) * rm for c in range(18)], 0)
                out = nt(left, j)
                for f in range(9):
                    acc_ref[f, gi // 2, (gi % 2) * 16 : (gi % 2) * 16 + 16, :] += (
                        out[f * 16 : f * 16 + 16] + out[(9 + f) * 16 : (9 + f) * 16 + 16]
                    )
            return carry_unused

        lax.fori_loop(0, (most + SLOTS - 1) // SLOTS, one_round, 0)
    for a in range(8):
        inv = 1.0 / vn2_ref[a]
        for f in range(9):
            v = fields_ref[f, a] + acc_ref[f, a] * inv
            src_ref[f, a] = v
            tlo_ref[f, a : a + 1, :] = v[0:1]
            thi_ref[f, a : a + 1, :] = v[31:32]
    leaving.wait()


def deposit(chan, fields, volume, sa, st, sr, grads):
    sd = jax.ShapeDtypeStruct
    return pl.pallas_call(
        deposit_kernel,
        out_shape=(
            sd((8, 32, 256), F32), sd((8, 32, 256), F32), sd((9, 8, 32, 256), F32),
            sd((9, 8, 256), F32), sd((9, 8, 256), F32),
            sd((27, 8, 32, 256), F32),
        ),
        in_specs=[VM] * 6 + [pl.BlockSpec(memory_space=pl.ANY)],
        out_specs=[VM] * 5 + [pl.BlockSpec(memory_space=pl.ANY)],
        scratch_shapes=[
            pltpu.VMEM((20 * GROUPS, SLOTS), F32),
            pltpu.VMEM((9, 8, 32, 256), F32),
            pltpu.VMEM((1, CHUNK), I32),
            pltpu.VMEM((27, 8, 32, 256), F32),
            pltpu.SemaphoreType.DMA((2,)),
        ],
        compiler_params=pltpu.CompilerParams(vmem_limit_bytes=44 << 20),
        name="deposit",
    )(chan, fields, volume, sa, st, sr, grads)


def t_shift(x, edge):
    return jnp.where(iota(x.shape, 0) == 0, edge, pltpu.roll(x, 1, 0))


def r_shift(x):
    n = x.shape[1]
    return jnp.where(iota(x.shape, 1) == n - 1, 0.0, pltpu.roll(x, n - 1, 1))


def prepare(f_ref, w_ref, slot, field, vol, edge):
    for f in range(9):
        x = field(f)
        xt = t_shift(x, edge(f))
        f_ref[slot, 0, f] = r_shift(x)
        f_ref[slot, 1, f] = x
        f_ref[slot, 2, f] = r_shift(xt)
        f_ref[slot, 3, f] = xt
    v = vol * 0.125
    v = v + t_shift(v, edge(21) * 0.125)
    w_ref[slot] = v + r_shift(v)


def prepare_areas(a_ref, area, edge):
    for i in range(3):
        for q in range(4):
            x = area(i, q)
            if q // 2 == 1:
                x = t_shift(x, edge(i, q))
            a_ref[i, q] = x if q % 2 == 1 else pltpu.roll(x, 255, 1)


def gradient_plane(f_ref, w_ref, a0_ref, a1_ref, now, prev, out_ref, a):
    def part(n, unused):
        i = lax.rem(n, 3)
        rows = pl.ds(pl.multiple_of(n // 3 * 8, 8), 8)
        inv = 1.0 / (w_ref[now, rows] + w_ref[prev, rows])
        acc = [None] * 9
        for dz in range(2):
            for q in range(4):
                area = (a1_ref if dz else a0_ref)[i, q, rows]
                for f in range(9):
                    term = area * f_ref[prev if dz else now, q, f, rows]
                    acc[f] = term if dz + q == 0 else acc[f] + term
        for f in range(9):
            out_ref[9 * i + f, a, rows] = acc[f] * inv
        return unused

    lax.fori_loop(0, 12, part, 0)


def diffuse_kernel(
    src_ref, tlo_ref, thi_ref, k_ref, vn_ref, kzl_ref, kzh_ref, ktl_ref, kth_ref, out_ref,
    zlo, zhi, tlo, thi, w_ref, send_sems, recv_sems,
):
    slab, sector = lax.axis_index("slab"), lax.axis_index("sector")
    above = (lax.rem(slab + 1, 32), sector)
    below = (lax.rem(slab + 31, 32), sector)
    ahead = (slab, lax.rem(sector + 1, 4))
    behind = (slab, lax.rem(sector + 3, 4))
    barrier = pltpu.get_barrier_semaphore()
    for to in (above, below, ahead, behind):
        pl.semaphore_signal(barrier, inc=1, device_id=to, device_id_type=pl.DeviceIdType.MESH)
    halo = [
        (thi_ref, tlo, ahead), (tlo_ref, thi, behind),
        (src_ref.at[:, 7], zlo, above), (src_ref.at[:, 0], zhi, below),
    ]
    copies = [
        pltpu.make_async_remote_copy(
            src_ref=s, dst_ref=t, send_sem=send_sems.at[n], recv_sem=recv_sems.at[n],
            device_id=to, device_id_type=pl.DeviceIdType.MESH,
        )
        for n, (s, t, to) in enumerate(halo)
    ]
    pl.semaphore_wait(barrier, 4)
    for copy in copies:
        copy.start()
    row = iota((32, 256), 0)
    lane = iota((32, 256), 1)
    for a in range(8):
        k = k_ref[a]
        near = [
            kzl_ref[...] if a == 0 else k_ref[a - 1],
            kzh_ref[...] if a == 7 else k_ref[a + 1],
            jnp.where(row == 0, ktl_ref[a : a + 1], pltpu.roll(k, 1, 0)),
            jnp.where(row == 31, kth_ref[a : a + 1], pltpu.roll(k, 31, 0)),
            jnp.where(lane == 0, 0.0, pltpu.roll(k, 1, 1)),
            jnp.where(lane == 255, 0.0, pltpu.roll(k, 255, 1)),
        ]
        scale = (0.2 * k) / vn_ref[a]
        total = None
        for n, kn in enumerate(near):
            w = scale * kn / (k + kn)
            w_ref[n, a] = w
            total = w if total is None else total + w
        w_ref[6, a] = 1.0 - total
    copies[0].wait()
    copies[1].wait()

    def plane(f, a, under, over):
        s = src_ref[f, a]
        near = [
            under, over,
            jnp.where(row == 0, tlo[f, a : a + 1], pltpu.roll(s, 1, 0)),
            jnp.where(row == 31, thi[f, a : a + 1], pltpu.roll(s, 31, 0)),
            pltpu.roll(s, 1, 1),
            pltpu.roll(s, 255, 1),
        ]
        out = w_ref[6, a] * s
        for n in range(6):
            out = out + w_ref[n, a] * near[n]
        out_ref[f, a] = out

    def inner(f, unused):
        for a in range(1, 7):
            plane(f, a, src_ref[f, a - 1], src_ref[f, a + 1])
        return unused

    lax.fori_loop(0, 9, inner, 0)
    copies[2].wait()
    copies[3].wait()

    def ends(f, unused):
        plane(f, 0, zlo[f], src_ref[f, 1])
        plane(f, 7, src_ref[f, 6], zhi[f])
        return unused

    lax.fori_loop(0, 9, ends, 0)


def diffuse(src, tlo, thi, k, vn, kzl, kzh, ktl, kth):
    dma = pltpu.SemaphoreType.DMA
    cells = (9, 8, 32, 256)
    return pl.pallas_call(
        diffuse_kernel,
        out_shape=jax.ShapeDtypeStruct(cells, F32),
        in_specs=[VM] * 9,
        out_specs=VM,
        scratch_shapes=[
            pltpu.VMEM((9, 32, 256), F32), pltpu.VMEM((9, 32, 256), F32),
            pltpu.VMEM((9, 8, 256), F32), pltpu.VMEM((9, 8, 256), F32),
            pltpu.VMEM((7, 8, 32, 256), F32), dma((4,)), dma((4,)),
        ],
        compiler_params=pltpu.CompilerParams(has_side_effects=True, collective_id=1, vmem_limit_bytes=16 << 20),
        name="diffuse",
    )(src, tlo, thi, k, vn, kzl, kzh, ktl, kth)


def exchange_kernel(
    loads_in, dest_in, cell_in, fields_in, areas_in, vol_in, sa_in, st_in, k_in,
    chan_ref, kzl_ref, kzh_ref, ktl_ref, kth_ref, grads_ref,
    acc_ref, d_ref, rank_ref, out_buf, in_buf, azs, ts, cs, kbs, zr, tr, cr, kar, knr,
    loads_ref, dest_ref, cell_ref, sz_ref, kz_ref, kz0_ref, st_ref, kt_ref, kt0_ref,
    fbuf, abuf, vbuf, gbuf, f_ref, w_ref, a0_ref, a1_ref,
    send_sems, recv_sems, psend_sem, precv_sem, own_sem, load_sems, store_sems,
):
    slab, sector = lax.axis_index("slab"), lax.axis_index("sector")
    me = slab * 4 + sector
    barrier = pltpu.get_barrier_semaphore()
    loading = [
        pltpu.make_async_copy(s, t, load_sems.at[n])
        for n, (s, t) in enumerate((
            (dest_in, dest_ref), (loads_in, loads_ref), (cell_in, cell_ref),
            (fields_in, fbuf), (areas_in, abuf), (vol_in, vbuf),
            (sa_in.at[7], sz_ref), (k_in.at[7], kz_ref), (k_in.at[0], kz0_ref),
            (st_in.at[:, 24:32], st_ref), (k_in.at[:, 24:32], kt_ref), (k_in.at[:, 0:8], kt0_ref),
        ))
    ]
    for copy in loading:
        copy.start()

    def greet(k, unused):
        to = lax.rem(me + k, 128)
        pl.semaphore_signal(barrier, inc=1, device_id=(to // 4, lax.rem(to, 4)), device_id_type=pl.DeviceIdType.MESH)
        return unused

    lax.fori_loop(1, 128, greet, 0)

    loading[0].wait()
    blk, devices = 256, 128
    earlier = before(blk)
    carry = jnp.zeros((devices, 1), F32)
    count = 4096 // blk
    for b in range(count):
        d_ref[b * 128 : (b + 1) * 128, :] = one_hot(dest_ref[:, b * blk : (b + 1) * blk], devices)
    counts = jnp.dot(d_ref[...], earlier, preferred_element_type=F32)
    for b in range(count):
        df = d_ref[b * 128 : (b + 1) * 128, :].astype(F32)
        rank_ref[:, b * blk : (b + 1) * blk] = jnp.sum(
            df * (counts[b * 128 : (b + 1) * 128] + carry), axis=0, keepdims=True
        ).astype(I32)
        carry = carry + jnp.sum(df, axis=1, keepdims=True)

    for copy in loading[1:]:
        copy.wait()
    for n in range(12):
        x = abuf[n // 4, 4 + n % 4, 7].astype(F32)
        azs[n] = x
        cs[9 + n : 10 + n] = x[31:32]
        for a in range(8):
            ts[9 + n, a : a + 1, :] = abuf[n // 4, (2, 3, 6, 7)[n % 4], a].astype(F32)[31:32]
    for f in range(9):
        ts[f] = fbuf[f, :, 31, :]
        cs[f : f + 1] = fbuf[f, 7, 31:32]
    ts[21] = vbuf[:, 31, :]
    cs[21:22] = vbuf[7, 31:32]
    for n, (t_ref, z_ref) in enumerate(((st_ref, sz_ref), (kt_ref, kz_ref))):
        ts[22 + n] = t_ref[:, 7, :]
        cs[22 + n : 23 + n] = z_ref[31:32]
    kbs[...] = kt0_ref[:, 0, :]

    above = (lax.rem(slab + 1, 32), sector)
    below = (lax.rem(slab + 31, 32), sector)
    ahead = (slab, lax.rem(sector + 1, 4))
    behind = (slab, lax.rem(sector + 3, 4))
    across = (lax.rem(slab + 1, 32), lax.rem(sector + 1, 4))
    halo = [
        (sz_ref, zr.at[22], above),
        (kz_ref, zr.at[23], above),
        (kz0_ref, kar, below),
        (kbs, knr, behind),
        (ts, tr, ahead),
        (cs, cr, across),
        (vbuf.at[7], zr.at[21], above),
        (fbuf.at[:, 7], zr.at[0:9], above),
        (azs, zr.at[9:21], above),
    ]
    copies = [
        pltpu.make_async_remote_copy(
            src_ref=s, dst_ref=t, send_sem=send_sems.at[n], recv_sem=recv_sems.at[n],
            device_id=to, device_id_type=pl.DeviceIdType.MESH,
        )
        for n, (s, t, to) in enumerate(halo)
    ]
    pl.semaphore_wait(barrier, 127)
    for copy in copies:
        copy.start()
    acc_ref[...] = jnp.zeros_like(acc_ref)
    part = 512
    for b in range(4096 // part):
        sl = pl.ds(b * part, part)
        rank = rank_ref[:, sl]
        o = one_hot(rank & 31, 32)
        hi, lo = split(loads_ref[:, sl])
        cell = cell_ref[:, sl]
        row = (lax.shift_right_logical(cell, 8) * 256).astype(F32).astype(BF16)
        col = ((cell & 255) + 1).astype(F32).astype(BF16)
        his = jnp.concatenate([hi[c : c + 1] * o for c in range(9)] + [row * o], 0)
        los = jnp.concatenate([lo[c : c + 1] * o for c in range(9)] + [col * o], 0)
        d = one_hot(dest_ref[:, sl] + lax.shift_right_logical(rank, 5) * 128, 256)
        acc_ref[...] += nt(jnp.concatenate([his, los], 1), jnp.concatenate([d, d], 1))
    for s in range(5):
        block = jnp.concatenate(
            [acc_ref[c * 32 : (c + 1) * 32, h * 128 : (h + 1) * 128] for c in (2 * s, 2 * s + 1) for h in range(2)], 0
        )
        out_buf[:, s, :] = block.T
    own = pltpu.make_async_copy(out_buf.at[me], in_buf.at[me], own_sem)
    own.start()

    def send(k, unused):
        to = lax.rem(me + k, 128)
        pltpu.make_async_remote_copy(
            src_ref=out_buf.at[to], dst_ref=in_buf.at[me], send_sem=psend_sem, recv_sem=precv_sem,
            device_id=(to // 4, lax.rem(to, 4)), device_id_type=pl.DeviceIdType.MESH,
        ).start()
        return unused

    lax.fori_loop(1, 128, send, 0)
    copies[4].wait()

    def beside(plane):
        return lambda c: tr[c, pl.ds(plane, 1), :]

    def prepare_own(slot, plane):
        prepare(f_ref, w_ref, slot, lambda f: fbuf[f, plane], vbuf[plane], beside(plane))

    def own_areas(ref, plane, dz):
        prepare_areas(
            ref, lambda i, q: abuf[i, 4 * dz + q, plane].astype(F32),
            lambda i, q: beside(plane)(9 + 4 * i + 2 * dz + q % 2),
        )

    def store(a):
        return pltpu.make_async_copy(gbuf.at[:, a], grads_ref.at[:, a], store_sems.at[a])

    prepare_own(1, 7)

    def plane(n, unused):
        a = 7 - n
        now = lax.rem(a, 2)
        prepare_own(1 - now, a - 1)
        own_areas(a0_ref, a, 0)
        own_areas(a1_ref, a - 1, 1)
        gradient_plane(f_ref, w_ref, a0_ref, a1_ref, now, 1 - now, gbuf, a)
        store(a).start()
        return unused

    lax.fori_loop(0, 7, plane, 0)
    own_areas(a0_ref, 0, 0)
    inside = slab > 0

    def under(x):
        return jnp.where(inside, x, 0.0)

    own.wait()
    for n in (0, 1, 2, 3, 5):
        copies[n].wait()
    for h in range(2):
        chan_ref[10, 32 * h : 32 * h + 32] = under(zr[22, :, 128 * h : 128 * h + 128])
        chan_ref[11, 8 * h : 8 * h + 8] = tr[22, :, 128 * h : 128 * h + 128]
    kzl_ref[...] = under(zr[23])
    kzh_ref[...] = jnp.where(slab < 31, kar[...], 0.0)
    ktl_ref[...] = tr[23]
    kth_ref[...] = knr[...]
    most = pl.ds(0, 127)
    pltpu.make_async_copy(out_buf.at[most], in_buf.at[most], psend_sem).wait()
    pltpu.make_async_copy(out_buf.at[most], in_buf.at[most], precv_sem).wait()
    lane = iota((64, 128), 1) < 64
    for s in range(5):
        first, second = in_buf[0:64, s, :], in_buf[64:128, s, :]
        chan_ref[2 * s] = jnp.where(lane, first, pltpu.roll(second, 64, 1))
        chan_ref[2 * s + 1] = jnp.where(lane, pltpu.roll(first, 64, 1), second)
    for n in (6, 7, 8):
        copies[n].wait()
    prepare(f_ref, w_ref, 1, lambda f: under(zr[f]), under(zr[21]), lambda c: under(cr[c : c + 1, :]))
    prepare_areas(a1_ref, lambda i, q: zr[9 + 4 * i + q], lambda i, q: cr[9 + 4 * i + q : 10 + 4 * i + q, :])
    gradient_plane(f_ref, w_ref, a0_ref, a1_ref, 0, 1, gbuf, 0)
    store(0).start()
    for a in range(8):
        store(a).wait()


def exchange(loads, dest, cell, fields, areas, volume, sa, st, k):
    hbm = pl.BlockSpec(memory_space=pltpu.HBM)
    shapes = [(12, 64, 128), (32, 256), (32, 256), (8, 256), (8, 256), (27, 8, 32, 256)]
    dma = pltpu.SemaphoreType.DMA
    vm = lambda *shape, t=F32: pltpu.VMEM(shape, t)
    return pl.pallas_call(
        exchange_kernel,
        out_shape=[jax.ShapeDtypeStruct(s, F32) for s in shapes],
        in_specs=[hbm] * 9,
        out_specs=[VM] * 5 + [hbm],
        scratch_shapes=[
            vm(320, 256), vm(2048, 256, t=BF16), vm(1, 4096, t=I32), vm(128, 5, 128), vm(128, 5, 128),
            vm(12, 32, 256), vm(24, 8, 256), vm(24, 256), vm(8, 256),
            vm(24, 32, 256), vm(24, 8, 256), vm(24, 256), vm(32, 256), vm(8, 256),
            vm(9, 4096), vm(1, 4096, t=I32), vm(1, 4096, t=I32), vm(32, 256), vm(32, 256), vm(32, 256),
            vm(8, 8, 256), vm(8, 8, 256), vm(8, 8, 256),
            vm(9, 8, 32, 256), vm(3, 8, 8, 32, 256, t=BF16), vm(8, 32, 256), vm(27, 8, 32, 256),
            vm(2, 4, 9, 32, 256), vm(2, 32, 256), vm(3, 4, 32, 256), vm(3, 4, 32, 256),
            dma((9,)), dma((9,)), dma, dma, dma, dma((12,)), dma((8,)),
        ],
        compiler_params=pltpu.CompilerParams(has_side_effects=True, collective_id=0, vmem_limit_bytes=56 << 20),
        name="exchange",
    )(loads, dest.reshape(1, 4096), cell.reshape(1, 4096), fields, areas, volume, sa, st, k)


def local(fields, volume, swept_axial, swept_angular, swept_radial, conductivity, corner_areas, parcel_loads, dest_device, dest_cell):
    chan, kzl, kzh, ktl, kth, grads = exchange(
        parcel_loads, dest_device, dest_cell, fields, corner_areas, volume, swept_axial, swept_angular, conductivity
    )
    vn, vn2, src, tlo, thi, grads = deposit(
        chan, fields, volume, swept_axial, swept_angular, swept_radial, grads
    )
    diffused = diffuse(src, tlo, thi, conductivity, vn2, kzl, kzh, ktl, kth)
    return vn, diffused, grads


def solution(mesh):
    P = jax.sharding.PartitionSpec
    cells = P("slab", "sector", None)
    in_specs = (
        P(None, "slab", "sector", None), cells, cells, cells, cells, cells,
        P(None, None, "slab", "sector", None), P(None, ("slab", "sector")), P(("slab", "sector"), None), P(("slab", "sector")),
    )
    out_specs = (cells, P(None, "slab", "sector", None), P(None, "slab", "sector", None))
    return jax.shard_map(local, mesh=mesh, in_specs=in_specs, out_specs=out_specs, check_vma=False)
```
